512 devices in a mesh: gx: 16 (over x_hi, y, core), gy: 32 (over x_lo, z).
Axes of the slice: x: 4 (x_hi: 2, x_lo: 2; x = x_hi * 2 + x_lo), y: 4, z: 16, core: 2. Of those that a mesh axis runs over, the one named last changes fastest.
Arguments:
- entity_table: float32 [131072, 256], P(('gx', 'gy')), may hold values from -2.5 to 2.5
- relations: float32 [4, 256, 256], replicated, may hold values from -0.375 to 0.375
- rel_ids: int32 [3, 2048], P(None, ('gx', 'gy')), may hold values from 0 to 3
- edge_src: int32 [3, 3145728], P(None, ('gx', 'gy')), may hold values from 0 to 255
- edge_dst: int32 [3, 3145728], P(None, ('gx', 'gy')), may hold values from 0 to 255
Outputs:
- new_table: float32 [131072, 256], P(('gx', 'gy'))
- rel_grad: float32 [4, 256, 256], replicated
The draws below stay inside these ranges and needn't reach their ends.
All inputs are finite; a program needn't handle non-finite values.
Results may differ from the reference program's by a relative error of at most 0.0089.
Values may be sent and summed in bfloat16 or wider, within the bound.
No kernel may reach another device: no remote copies, remote signals or barrier semaphores. Data moves between devices by JAX's collectives and lax.ppermute only.
A program may use at most 64 MiB of HBM per device.

```python
import math
import jax
import jax.numpy as jnp
from jax import lax

D = 256
REL = 4
GROUPS = 4
ROUNDS = 3
ROWS = 256
EDGES_DEV = 6144
ENTITIES = 131072
GROUP_ALL = 2048
EDGE_ALL = 3145728
N_GX = 16
N_GY = 32


def with_ends(values, rng, least, high):
    spot = [jax.random.randint(jax.random.fold_in(rng, axis), (), 0, length) for axis, length in enumerate(values.shape)]
    main_axis = values.shape.index(max(values.shape))
    neighbour = spot[:main_axis] + [(spot[main_axis] + 1) % values.shape[main_axis]] + spot[main_axis + 1:]
    return values.at[tuple(spot)].set(least).at[tuple(neighbour)].set(high)


def level_of(rng, extent, shards, smallest, top_value):
    def one(dim, shards_of):
        draws = jax.random.uniform(jax.random.fold_in(jax.random.fold_in(rng, 6), dim), (shards_of,), jnp.float32, smallest / len(shards), top_value / len(shards))
        return jnp.repeat(jnp.exp(draws), extent[dim] // shards_of).reshape((-1,) + (1,) * (len(extent) - dim - 1))

    gain = one(*shards[0])
    for cut in shards[1:]:
        gain = gain * one(*cut)
    return gain


def scatter_about(rng, dims, deviation, limit, shards=(), kind=jnp.bfloat16):
    level = level_of(rng, dims, shards, -0.22, 0.18) if shards else 1.0
    drawn = jax.random.normal(rng, dims, jnp.float32) * deviation * level
    return jnp.minimum(jnp.maximum(drawn, -limit), limit).astype(kind)


def setup_inputs(seed: int = 0) -> dict:
    arg_keys = jax.random.split(jax.random.key(seed), 6)
    entity_table = scatter_about(arg_keys[0], (ENTITIES, D), 0.35, 2.5, ((0, 512),), jnp.float32)
    relations = scatter_about(arg_keys[1], (REL, D, D), D ** -0.5, 0.375, (), jnp.float32)
    rel_ids = with_ends(jax.random.randint(arg_keys[2], (ROUNDS, GROUP_ALL), 0, REL), jax.random.fold_in(arg_keys[2], 1), 0, REL - 1).astype(jnp.int32)
    edge_src = with_ends(jax.random.randint(arg_keys[3], (ROUNDS, EDGE_ALL), 0, ROWS), jax.random.fold_in(arg_keys[3], 1), 0, ROWS - 1).astype(jnp.int32)
    edge_dst = with_ends(jax.random.randint(arg_keys[4], (ROUNDS, EDGE_ALL), 0, ROWS), jax.random.fold_in(arg_keys[4], 1), 0, ROWS - 1).astype(jnp.int32)
    return {"entity_table": entity_table, "relations": relations, "rel_ids": rel_ids, "edge_src": edge_src, "edge_dst": edge_dst}


learn_rate = 0.5
highest = lax.Precision.HIGHEST

def bucket_terms(src_rows, dst_rows, relations, group_ids, sources, targets):
    row_count, feature = src_rows.shape
    group_count = group_ids.shape[0]
    kinds = relations.shape[0]
    selector = (group_ids[:, None] == jnp.arange(kinds, dtype=jnp.int32)[None, :]).astype(jnp.float32)
    chosen = jnp.einsum('gk,kde->gde', selector, relations, precision=highest).astype(jnp.bfloat16)
    src_b = src_rows.astype(jnp.bfloat16).reshape(group_count, row_count // group_count, feature)
    dst_b = dst_rows.astype(jnp.bfloat16)
    mapped = jnp.einsum('gsd,gde->gse', src_b.astype(jnp.float32), chosen.astype(jnp.float32), precision=highest).astype(jnp.bfloat16)
    mapped_flat = mapped.reshape(row_count, feature)
    scores = jnp.dot(mapped_flat, dst_b.T, preferred_element_type=jnp.float32)
    scaling = 1.0 / math.sqrt(row_count)
    slopes = jax.nn.sigmoid(scores) * scaling
    slopes = slopes.at[sources, targets].add(-scaling)
    slopes_b = slopes.astype(jnp.bfloat16)
    pulled = jnp.dot(slopes_b, dst_b, preferred_element_type=jnp.float32).astype(jnp.bfloat16)
    pulled = pulled.reshape(group_count, row_count // group_count, feature)
    src_grad = jnp.einsum('gse,gde->gsd', pulled.astype(jnp.float32), chosen.astype(jnp.float32), precision=highest).reshape(row_count, feature)
    dst_grad = jnp.dot(slopes_b.T, mapped_flat, preferred_element_type=jnp.float32).astype(jnp.bfloat16)
    dst_grad = lax.optimization_barrier(dst_grad).astype(jnp.float32)
    rel_group = jnp.einsum('gsd,gse->gde', src_b.astype(jnp.float32), pulled.astype(jnp.float32), precision=highest)
    rel_part = jnp.einsum('gk,gde->kde', selector, rel_group, precision=highest)
    return (src_grad, dst_grad, rel_part)

def reference(entity_table, relations, rel_ids, edge_src, edge_dst):
    part_count = N_GX * N_GY
    entity = entity_table.reshape(N_GX, N_GY, ROWS, D)
    buckets = ((1, 1), (0, 1), (1, -1))
    rel_total = jnp.zeros((REL, D, D), jnp.float32)
    for turn_index in range(ROUNDS):
        axis_number, offset = buckets[turn_index % 3]
        partner = jnp.roll(entity, offset, axis=axis_number)
        group_ids = rel_ids[turn_index].reshape(part_count, GROUPS)
        sources = edge_src[turn_index].reshape(part_count, EDGES_DEV)
        targets = edge_dst[turn_index].reshape(part_count, EDGES_DEV)

        def visit(carry, item):
            src_rows, dst_rows, ids_row, src_row, dst_row = item
            src_grad, dst_grad, rel_part = bucket_terms(src_rows, dst_rows, relations, ids_row, src_row, dst_row)
            return (carry + rel_part, (src_grad, dst_grad))
        rel_total, grads = lax.scan(visit, rel_total, (entity.reshape(part_count, ROWS, D), partner.reshape(part_count, ROWS, D), group_ids, sources, targets))
        src_grad, dst_grad = grads
        returned = jnp.roll(dst_grad.reshape(N_GX, N_GY, ROWS, D), -offset, axis=axis_number)
        entity = entity - learn_rate * (src_grad.reshape(N_GX, N_GY, ROWS, D) + returned)
    new_table = entity.reshape(ROWS * part_count, D)
    rel_grad = rel_total / math.sqrt(ROUNDS * part_count)
    return (new_table, rel_grad)
```

```python
import functools
import math

import jax
import jax.numpy as jnp
from jax import lax
from jax.experimental import pallas as pl
from jax.experimental.pallas import tpu as pltpu
from jax.sharding import Mesh
from jax.sharding import PartitionSpec as P


AXES = ("xh", "y", "c", "xl", "z")
GX = ("xh", "y", "c")
GY = ("xl", "z")
PLANE = ("xh", "y", "c", "xl")
LEARN_RATE = 0.5
VMEM = pl.BlockSpec(memory_space=pltpu.VMEM)
SMEM = pl.BlockSpec(memory_space=pltpu.SMEM)
F32 = jnp.float32
BF16 = jnp.bfloat16


def shifted(value, axes, steps):
    count = lax.axis_size(axes)
    pairs = [(source, (source + steps) % count) for source in range(count)]
    return lax.ppermute(value, axes, pairs)


def dot_nn(left, right):
    return lax.dot_general(left, right, (((1,), (0,)), ((), ())), preferred_element_type=F32)


def dot_nt(left, right):
    return lax.dot_general(left, right, (((1,), (1,)), ((), ())), preferred_element_type=F32)


def dot_tn(left, right):
    return lax.dot_general(left, right, (((0,), (0,)), ((), ())), preferred_element_type=F32)


def call(kernel, outs, in_specs, flops, name, scratch=(), aliases=None):
    moved = sum(math.prod(o.shape) * o.dtype.itemsize for o in outs)
    return pl.pallas_call(
        kernel,
        out_shape=tuple(outs),
        in_specs=list(in_specs),
        out_specs=tuple(VMEM for _ in outs),
        scratch_shapes=list(scratch),
        input_output_aliases=aliases or {},
        cost_estimate=pl.CostEstimate(
            flops=flops, bytes_accessed=4 * moved, transcendentals=0
        ),
        name=name,
    )


def map_rows(rows_b, rel_ref, ids_ref, turn, out_ref):
    groups = ids_ref.shape[1]
    size = rows_b.shape[0] // groups
    for g in range(groups):
        chosen = rel_ref[ids_ref[turn, g]].astype(BF16)
        part = slice(g * size, (g + 1) * size)
        out_ref[part, :] = dot_nn(rows_b[part, :], chosen).astype(BF16)


def prepare_kernel(ids_ref, x_ref, rel_ref, xb_ref, a_ref):
    rows_b = x_ref[...].astype(BF16)
    xb_ref[...] = rows_b
    map_rows(rows_b, rel_ref, ids_ref, 0, a_ref)


def count_kernel(turn, row_ref, col_ref, out_ref):
    size = out_ref.shape[0]
    total = row_ref.shape[1]
    chunk = 512
    lanes = lax.broadcasted_iota(jnp.int32, (size, chunk), 0)
    acc = jnp.zeros(out_ref.shape, F32)
    for k in range(0, total, chunk):
        rows = row_ref[turn : turn + 1, k : k + chunk].astype(jnp.int32)
        cols = col_ref[turn : turn + 1, k : k + chunk].astype(jnp.int32)
        row_hot = jnp.where(lanes == rows, 1.0, 0.0).astype(BF16)
        col_hot = jnp.where(lanes == cols, 1.0, 0.0).astype(BF16)
        acc = acc + dot_nt(row_hot, col_hot)
    out_ref[...] = acc


def slopes(scores, counts):
    scaling = 1.0 / math.sqrt(scores.shape[0])
    return ((jax.nn.sigmoid(scores) - counts) * scaling).astype(BF16)


def source_grad(pulled_b, rel_ref, ids_ref, turn):
    groups = ids_ref.shape[1]
    size = pulled_b.shape[0] // groups
    parts = []
    for g in range(groups):
        chosen = rel_ref[ids_ref[turn, g]].astype(BF16)
        parts.append(dot_nt(pulled_b[g * size : (g + 1) * size, :], chosen))
    return jnp.concatenate(parts, axis=0)


def target_grad(xb_ref, ap_ref, ctp_ref):
    slopes_t = slopes(dot_nt(xb_ref[...], ap_ref[...]), ctp_ref[...])
    return dot_nn(slopes_t, ap_ref[...]).astype(BF16).astype(F32)


def add_relation(acc_ref, xb_ref, pulled_b, ids_ref, turn):
    groups = ids_ref.shape[1]
    size = pulled_b.shape[0] // groups
    for g in range(groups):
        part = slice(g * size, (g + 1) * size)
        kind = ids_ref[turn, g]
        acc_ref[kind] = acc_ref[kind] + dot_tn(xb_ref[part, :], pulled_b[part, :])


def round_kernel(
    turn, ids_ref, xb_ref, xq_ref, a_ref, ap_ref, c_ref, ctp_ref, x_ref, rel_ref,
    xn_ref, xbn_ref, an_ref, h_ref,
):
    slopes_b = slopes(dot_nt(a_ref[...], xq_ref[...]), c_ref[...])
    pulled = dot_nn(slopes_b, xq_ref[...]).astype(BF16)
    h_ref[...] = pulled
    grad = source_grad(pulled, rel_ref, ids_ref, turn) + target_grad(xb_ref, ap_ref, ctp_ref)
    moved = x_ref[...] - LEARN_RATE * grad
    xn_ref[...] = moved
    moved_b = moved.astype(BF16)
    xbn_ref[...] = moved_b
    map_rows(moved_b, rel_ref, ids_ref, turn + 1, an_ref)


def relation_kernel(turn, fresh, ids_ref, xb_ref, h_ref, *refs):
    acc_ref = refs[-1]
    if fresh:
        acc_ref[...] = jnp.zeros_like(acc_ref)
    else:
        acc_ref[...] = refs[0][...]
    add_relation(acc_ref, xb_ref, h_ref[...], ids_ref, turn)


def last_kernel(turn, ids_ref, xb_ref, xq_ref, a_ref, c_ref, acc_ref, h_ref, pay_ref, sum_ref):
    slopes_b = slopes(dot_nt(a_ref[...], xq_ref[...]), c_ref[...])
    pulled = dot_nn(slopes_b, xq_ref[...]).astype(BF16)
    h_ref[...] = pulled
    sum_ref[...] = acc_ref[...]
    add_relation(sum_ref, xb_ref, pulled, ids_ref, turn)
    kinds, width = sum_ref.shape[:2]
    for k in range(kinds):
        pay_ref[k * width : (k + 1) * width, :] = sum_ref[k].astype(BF16)


def finish_kernel(turn, ids_ref, xb_ref, ap_ref, ctp_ref, h_ref, x_ref, rel_ref, xn_ref):
    grad = source_grad(h_ref[...], rel_ref, ids_ref, turn) + target_grad(xb_ref, ap_ref, ctp_ref)
    xn_ref[...] = x_ref[...] - LEARN_RATE * grad


def reduce_everywhere(payload):
    rows, width = payload.shape
    plane = lax.axis_size(PLANE)
    depth = lax.axis_size("z")
    share = rows // plane
    part = lax.all_to_all(payload.reshape(plane, share, width), PLANE, 0, 0)
    part = part.astype(F32).sum(0).astype(BF16)
    part = lax.all_to_all(jnp.broadcast_to(part[None], (depth, share, width)), "z", 0, 0)
    part = part.astype(F32).sum(0).astype(BF16)
    part = lax.all_to_all(jnp.broadcast_to(part[None], (plane, share, width)), PLANE, 0, 0)
    return part.reshape(rows, width).astype(F32)


def shards(entity, relations, rel_ids, edge_src, edge_dst):
    rows, width = entity.shape
    kinds = relations.shape[0]
    edges = edge_src.shape[1]
    square = 2 * rows * rows * width
    f_rows = jax.ShapeDtypeStruct((rows, width), F32)
    b_rows = jax.ShapeDtypeStruct((rows, width), BF16)
    f_count = jax.ShapeDtypeStruct((rows, rows), F32)
    f_rel = jax.ShapeDtypeStruct(relations.shape, F32)
    buckets = ((GY, 1), (GX, 1), (GY, -1))

    both = jnp.stack([edge_src, edge_dst], axis=1)

    def incoming_edges(turn):
        axes, offset = buckets[turn]
        return shifted(both[turn], axes, -offset)

    def counted(turn, row, col, name):
        return call(
            functools.partial(count_kernel, turn), [f_count], [VMEM, VMEM],
            2 * rows * rows * edges, name,
        )(row, col)[0]

    xb, a = call(prepare_kernel, [b_rows, b_rows], [SMEM, VMEM, VMEM], square, "prepare")(
        rel_ids, entity, relations
    )
    x = entity
    total = None
    far = [None] * 3
    for turn in range(3):
        axes, offset = buckets[turn]
        if turn == 0:
            far[0] = incoming_edges(0)
        xq = shifted(xb, axes, offset)
        ap = shifted(a, axes, -offset)
        if turn == 0:
            far[1] = incoming_edges(1)
            far[2] = incoming_edges(2)
        c = counted(turn, edge_src, edge_dst, f"count_{turn}")
        ctp = counted(0, far[turn][1:2], far[turn][0:1], f"count_far_{turn}")
        if turn < 2:
            xn, xbn, an, h = call(
                functools.partial(round_kernel, turn), [f_rows, b_rows, b_rows, b_rows],
                [SMEM] + [VMEM] * 8, 7 * square, f"round_{turn}",
            )(rel_ids, xb, xq, a, ap, c, ctp, x, relations)
            extra = () if total is None else (total,)
            total = call(
                functools.partial(relation_kernel, turn, total is None), [f_rel],
                [SMEM] + [VMEM] * (2 + len(extra)), square, f"relation_{turn}",
            )(rel_ids, xb, h, *extra)[0]
            x, xb, a = xn, xbn, an
        else:
            h, payload = call(
                functools.partial(last_kernel, turn),
                [b_rows, jax.ShapeDtypeStruct((kinds * width, width), BF16)],
                [SMEM] + [VMEM] * 5, 3 * square, "last",
                scratch=[pltpu.VMEM(relations.shape, F32)],
            )(rel_ids, xb, xq, a, c, total)
            x = call(
                functools.partial(finish_kernel, turn), [f_rows],
                [SMEM] + [VMEM] * 6, 3 * square, "finish",
            )(rel_ids, xb, ap, ctp, h, x, relations)[0]
    summed = reduce_everywhere(payload)
    divisor = math.sqrt(3 * lax.axis_size(AXES))
    return x, (summed / divisor).reshape(relations.shape)


def solution(mesh):
    inner = Mesh(mesh.devices.reshape(2, 4, 2, 2, 16), AXES)
    return jax.shard_map(
        shards,
        mesh=inner,
        in_specs=(P(AXES, None), P(), P(None, AXES), P(None, AXES), P(None, AXES)),
        out_specs=(P(AXES, None), P()),
        check_vma=False,
    )
```

```python
import functools
import math

import jax
import jax.numpy as jnp
from jax import lax
from jax.experimental import pallas as pl
from jax.experimental.pallas import tpu as pltpu
from jax.sharding import Mesh
from jax.sharding import PartitionSpec as P


AXES = ("xh", "y", "c", "xl", "z")
GX = ("xh", "y", "c")
GY = ("xl", "z")
PLANE = ("xh", "y", "c", "xl")
LEARN_RATE = 0.5
VMEM = pl.BlockSpec(memory_space=pltpu.VMEM)
SMEM = pl.BlockSpec(memory_space=pltpu.SMEM)
F32 = jnp.float32
BF16 = jnp.bfloat16


def shifted(value, axes, steps):
    count = lax.axis_size(axes)
    pairs = [(source, (source + steps) % count) for source in range(count)]
    return lax.ppermute(value, axes, pairs)


def dot_nn(left, right):
    return lax.dot_general(left, right, (((1,), (0,)), ((), ())), preferred_element_type=F32)


def dot_nt(left, right):
    return lax.dot_general(left, right, (((1,), (1,)), ((), ())), preferred_element_type=F32)


def dot_tn(left, right):
    return lax.dot_general(left, right, (((0,), (0,)), ((), ())), preferred_element_type=F32)


def call(kernel, outs, in_specs, flops, name, aliases=None):
    moved = sum(math.prod(o.shape) * o.dtype.itemsize for o in outs)
    return pl.pallas_call(
        kernel,
        out_shape=tuple(outs),
        in_specs=list(in_specs),
        out_specs=tuple(VMEM for _ in outs),
        input_output_aliases=aliases or {},
        compiler_params=pltpu.CompilerParams(vmem_limit_bytes=16 * 2**20),
        cost_estimate=pl.CostEstimate(
            flops=flops, bytes_accessed=4 * moved, transcendentals=0
        ),
        name=name,
    )


def map_rows(rows_b, rel_ref, ids_ref, turn, out_ref):
    groups = ids_ref.shape[1]
    size = rows_b.shape[0] // groups
    for g in range(groups):
        chosen = rel_ref[ids_ref[turn, g]].astype(BF16)
        part = slice(g * size, (g + 1) * size)
        out_ref[part, :] = dot_nn(rows_b[part, :], chosen).astype(BF16)


def folded(edge_ref, turn, width):
    pieces = edge_ref.shape[1] // width
    rows = [edge_ref[turn : turn + 1, i * width : (i + 1) * width] for i in range(pieces)]
    return jnp.concatenate(rows, axis=0).astype(F32).astype(BF16)


def one_hot(row, size):
    count = row.shape[1]
    wide = jnp.broadcast_to(row.astype(F32), (16, count)).astype(BF16)
    index = lax.broadcasted_iota(jnp.int32, (16, count), 0).astype(F32).astype(BF16)
    one = jnp.ones((16, count), BF16)
    zero = jnp.zeros((16, count), BF16)
    parts = [jnp.where(wide == index + BF16(16 * i), one, zero) for i in range(size // 16)]
    return jnp.concatenate(parts, axis=0)


def counted(row_of, col_of, pieces, size):
    acc = jnp.zeros((size, size), F32)
    for i in range(pieces):
        acc = acc + dot_nt(one_hot(row_of(i), size), one_hot(col_of(i), size))
    return acc


def own_count(src_ref, dst_ref, turn, size):
    def piece(ref):
        return lambda i: ref[turn : turn + 1, i * size : (i + 1) * size]

    return counted(piece(src_ref), piece(dst_ref), src_ref.shape[1] // size, size)


def far_count(ap_ref, size):
    pieces = (ap_ref.shape[0] - size) // 2

    def piece(first):
        return lambda i: ap_ref[first + i : first + i + 1, :]

    return counted(piece(size + pieces), piece(size), pieces, size)


def slopes(scores, counts):
    scaling = 1.0 / math.sqrt(scores.shape[0])
    return ((jax.nn.sigmoid(scores) - counts) * scaling).astype(BF16)


def source_grad(pulled_b, rel_ref, ids_ref, turn):
    groups = ids_ref.shape[1]
    size = pulled_b.shape[0] // groups
    parts = []
    for g in range(groups):
        chosen = rel_ref[ids_ref[turn, g]].astype(BF16)
        parts.append(dot_nt(pulled_b[g * size : (g + 1) * size, :], chosen))
    return jnp.concatenate(parts, axis=0)


def target_grad(xb_ref, ap_ref):
    size = xb_ref.shape[0]
    mapped = ap_ref[:size, :]
    slopes_t = slopes(dot_nt(xb_ref[...], mapped), far_count(ap_ref, size))
    return dot_nn(slopes_t, mapped).astype(BF16).astype(F32)


def add_relation(acc_ref, xb_ref, pulled_b, ids_ref, turn):
    groups = ids_ref.shape[1]
    size = pulled_b.shape[0] // groups
    for g in range(groups):
        part = slice(g * size, (g + 1) * size)
        kind = ids_ref[turn, g]
        acc_ref[kind] = acc_ref[kind] + dot_tn(xb_ref[part, :], pulled_b[part, :])


def prepare_kernel(ids_ref, x_ref, rel_ref, src_ref, dst_ref, xb_ref, pay_ref):
    size, width = x_ref.shape
    rows_b = x_ref[...].astype(BF16)
    xb_ref[...] = rows_b
    map_rows(rows_b, rel_ref, ids_ref, 0, pay_ref)
    pieces = (pay_ref.shape[0] - size) // 2
    pay_ref[size : size + pieces, :] = folded(src_ref, 0, width)
    pay_ref[size + pieces :, :] = folded(dst_ref, 0, width)


def first_window_kernel(src_ref, dst_ref, c_ref, ends_ref):
    size = c_ref.shape[0]
    c_ref[...] = own_count(src_ref, dst_ref, 0, size)
    pieces = ends_ref.shape[1] // 2
    for turn in range(1, src_ref.shape[0]):
        ends_ref[turn - 1, :pieces, :] = folded(src_ref, turn, size)
        ends_ref[turn - 1, pieces:, :] = folded(dst_ref, turn, size)


def window_kernel(turn, ids_ref, src_ref, dst_ref, xb_ref, h_ref, *refs):
    c_ref, acc_ref = refs[-2:]
    if len(refs) == 2:
        acc_ref[...] = jnp.zeros_like(acc_ref)
    else:
        acc_ref[...] = refs[0][...]
    add_relation(acc_ref, xb_ref, h_ref[...], ids_ref, turn - 1)
    c_ref[...] = own_count(src_ref, dst_ref, turn, c_ref.shape[0])


def round_kernel(
    turn, ids_ref, xb_ref, xq_ref, pay_ref, far_ref, c_ref, ends_ref, x_ref, rel_ref,
    xn_ref, xbn_ref, payn_ref, h_ref,
):
    size = xb_ref.shape[0]
    slopes_b = slopes(dot_nt(pay_ref[:size, :], xq_ref[...]), c_ref[...])
    pulled = dot_nn(slopes_b, xq_ref[...]).astype(BF16)
    h_ref[...] = pulled
    grad = source_grad(pulled, rel_ref, ids_ref, turn) + target_grad(xb_ref, far_ref)
    moved = x_ref[...] - LEARN_RATE * grad
    xn_ref[...] = moved
    moved_b = moved.astype(BF16)
    xbn_ref[...] = moved_b
    map_rows(moved_b, rel_ref, ids_ref, turn + 1, payn_ref)
    payn_ref[size:, :] = ends_ref[turn]


def last_kernel(turn, ids_ref, xb_ref, xq_ref, pay_ref, c_ref, acc_in_ref, h_ref, out_ref, acc_ref):
    size = xb_ref.shape[0]
    slopes_b = slopes(dot_nt(pay_ref[:size, :], xq_ref[...]), c_ref[...])
    pulled = dot_nn(slopes_b, xq_ref[...]).astype(BF16)
    h_ref[...] = pulled
    acc_ref[...] = acc_in_ref[...]
    add_relation(acc_ref, xb_ref, pulled, ids_ref, turn)
    kinds, width = acc_ref.shape[:2]
    for k in range(kinds):
        out_ref[k * width : (k + 1) * width, :] = acc_ref[k].astype(BF16)


def finish_kernel(turn, ids_ref, xb_ref, far_ref, h_ref, x_ref, rel_ref, xn_ref):
    grad = source_grad(h_ref[...], rel_ref, ids_ref, turn) + target_grad(xb_ref, far_ref)
    xn_ref[...] = x_ref[...] - LEARN_RATE * grad


def sum_kernel(in_ref, out_ref):
    acc = in_ref[0].astype(F32)
    for i in range(1, in_ref.shape[0]):
        acc = acc + in_ref[i].astype(F32)
    total = acc.astype(BF16)
    for i in range(out_ref.shape[0]):
        out_ref[i] = total


def summed_for(parts, copies, name):
    count, share, width = parts.shape
    out = jax.ShapeDtypeStruct((copies, share, width), BF16)
    return call(sum_kernel, [out], [VMEM], count * share * width, name)(parts)[0]


def reduce_everywhere(payload):
    rows, width = payload.shape
    plane = lax.axis_size(PLANE)
    depth = lax.axis_size("z")
    part = lax.all_to_all(payload.reshape(plane, rows // plane, width), PLANE, 0, 0)
    part = lax.all_to_all(summed_for(part, depth, "sum_plane"), "z", 0, 0)
    part = lax.all_to_all(summed_for(part, plane, "sum_z"), PLANE, 0, 0)
    return part.reshape(rows, width).astype(F32)


def shards(entity, relations, rel_ids, edge_src, edge_dst):
    rows, width = entity.shape
    kinds = relations.shape[0]
    turns, edges = edge_src.shape
    square = 2 * rows * rows * width
    counting = 2 * rows * rows * edges
    ends_rows = 2 * edges // width
    f_rows = jax.ShapeDtypeStruct((rows, width), F32)
    b_rows = jax.ShapeDtypeStruct((rows, width), BF16)
    b_pay = jax.ShapeDtypeStruct((rows + ends_rows, width), BF16)
    b_ends = jax.ShapeDtypeStruct((turns - 1, ends_rows, width), BF16)
    f_count = jax.ShapeDtypeStruct((rows, rows), F32)
    f_rel = jax.ShapeDtypeStruct(relations.shape, F32)
    buckets = ((GY, 1), (GX, 1), (GY, -1))

    xb, pay = call(prepare_kernel, [b_rows, b_pay], [SMEM] + [VMEM] * 4, square, "prepare")(
        rel_ids, entity, relations, edge_src, edge_dst
    )
    x = entity
    acc = None
    for turn in range(turns):
        axes, offset = buckets[turn % 3]
        xq = shifted(xb, axes, offset)
        far = shifted(pay, axes, -offset)
        if turn == 0:
            c, ends = call(
                first_window_kernel, [f_count, b_ends], [VMEM] * 2, counting, "window_0"
            )(edge_src, edge_dst)
        else:
            extra = () if acc is None else (acc,)
            c, acc = call(
                functools.partial(window_kernel, turn), [f_count, f_rel],
                [SMEM] + [VMEM] * (4 + len(extra)), counting + square, f"window_{turn}",
                aliases={5: 1} if extra else None,
            )(rel_ids, edge_src, edge_dst, xb_old, h, *extra)
        if turn < turns - 1:
            xb_old = xb
            x, xb, pay, h = call(
                functools.partial(round_kernel, turn), [f_rows, b_rows, b_pay, b_rows],
                [SMEM] + [VMEM] * 8, 7 * square + counting, f"round_{turn}",
            )(rel_ids, xb, xq, pay, far, c, ends, x, relations)
        else:
            h, payload, _ = call(
                functools.partial(last_kernel, turn),
                [b_rows, jax.ShapeDtypeStruct((kinds * width, width), BF16), f_rel],
                [SMEM] + [VMEM] * 5, 3 * square, "last", aliases={5: 2},
            )(rel_ids, xb, xq, pay, c, acc)
            x = call(
                functools.partial(finish_kernel, turn), [f_rows],
                [SMEM] + [VMEM] * 5, 3 * square + counting, "finish",
            )(rel_ids, xb, far, h, x, relations)[0]
    summed = reduce_everywhere(payload)
    divisor = math.sqrt(turns * lax.axis_size(AXES))
    return x, (summed / divisor).reshape(relations.shape)


def solution(mesh):
    inner = Mesh(mesh.devices.reshape(2, 4, 2, 2, 16), AXES)
    return jax.shard_map(
        shards,
        mesh=inner,
        in_specs=(P(AXES, None), P(), P(None, AXES), P(None, AXES), P(None, AXES)),
        out_specs=(P(AXES, None), P()),
        check_vma=False,
    )
```

```python
import functools
import math

import jax
import jax.numpy as jnp
from jax import lax
from jax.experimental import pallas as pl
from jax.experimental.pallas import tpu as pltpu
from jax.sharding import Mesh
from jax.sharding import PartitionSpec as P


AXES = ("xh", "y", "c", "xl", "zh", "zl")
GX = ("xh", "y", "c")
GY = ("xl", "zh", "zl")
NEAR = ("xh", "y", "c", "xl", "zl")
FAR = "zh"
LEARN_RATE = 0.5
FIRST_GRANT = 60 * 1024 * 1024 - 320 * 1024
VMEM = pl.BlockSpec(memory_space=pltpu.VMEM)
SMEM = pl.BlockSpec(memory_space=pltpu.SMEM)
HBM = pl.BlockSpec(memory_space=pltpu.HBM)
F32 = jnp.float32
BF16 = jnp.bfloat16


def shifted(value, axes, steps):
    count = lax.axis_size(axes)
    pairs = [(source, (source + steps) % count) for source in range(count)]
    return lax.ppermute(value, axes, pairs)


def dot_nn(left, right):
    return lax.dot_general(left, right, (((1,), (0,)), ((), ())), preferred_element_type=F32)


def dot_nt(left, right):
    return lax.dot_general(left, right, (((1,), (1,)), ((), ())), preferred_element_type=F32)


def dot_tn(left, right):
    return lax.dot_general(left, right, (((0,), (0,)), ((), ())), preferred_element_type=F32)


def call(kernel, outs, in_specs, flops, aliases=None, scratch=(), grant=16 * 2**20):
    moved = sum(math.prod(o.shape) * o.dtype.itemsize for o in outs)
    return pl.pallas_call(
        kernel,
        out_shape=tuple(outs),
        in_specs=list(in_specs),
        out_specs=tuple(VMEM for _ in outs),
        scratch_shapes=list(scratch),
        input_output_aliases=aliases or {},
        compiler_params=pltpu.CompilerParams(vmem_limit_bytes=grant),
        cost_estimate=pl.CostEstimate(
            flops=flops, bytes_accessed=4 * moved, transcendentals=0
        ),
    )


def map_rows(rows_b, rel_ref, ids_ref, turn, out_ref):
    groups = ids_ref.shape[1]
    size = rows_b.shape[0] // groups
    for g in range(groups):
        chosen = rel_ref[ids_ref[turn, g]].astype(BF16)
        part = slice(g * size, (g + 1) * size)
        out_ref[part, :] = dot_nn(rows_b[part, :], chosen).astype(BF16)


def folded(edge_ref, turn, width):
    pieces = edge_ref.shape[1] // width
    rows = [edge_ref[turn : turn + 1, i * width : (i + 1) * width] for i in range(pieces)]
    return jnp.concatenate(rows, axis=0).astype(F32).astype(BF16)


def one_hot(row, size):
    count = row.shape[1]
    wide = jnp.broadcast_to(row.astype(F32), (16, count)).astype(BF16)
    index = lax.broadcasted_iota(jnp.int32, (16, count), 0).astype(F32).astype(BF16)
    one = jnp.ones((16, count), BF16)
    zero = jnp.zeros((16, count), BF16)
    parts = [jnp.where(wide == index + BF16(16 * i), one, zero) for i in range(size // 16)]
    return jnp.concatenate(parts, axis=0)


def counted(row_of, col_of, pieces, size):
    acc = jnp.zeros((size, size), F32)
    for i in range(pieces):
        acc = acc + dot_nt(one_hot(row_of(i), size), one_hot(col_of(i), size))
    return acc


def pieces_of(ref, first):
    return lambda i: ref[first + i : first + i + 1, :]


def own_count(ends_ref, size, first=0):
    pieces = (ends_ref.shape[0] - first) // 2
    return counted(pieces_of(ends_ref, first), pieces_of(ends_ref, first + pieces), pieces, size)


def far_count(ends_ref, size, first=0):
    pieces = (ends_ref.shape[0] - first) // 2
    return counted(pieces_of(ends_ref, first + pieces), pieces_of(ends_ref, first), pieces, size)


def slopes(scores, counts):
    scaling = 1.0 / math.sqrt(scores.shape[0])
    return ((jax.nn.sigmoid(scores) - counts) * scaling).astype(BF16)


def source_grad(pulled_b, rel_ref, ids_ref, turn):
    groups = ids_ref.shape[1]
    size = pulled_b.shape[0] // groups
    parts = []
    for g in range(groups):
        chosen = rel_ref[ids_ref[turn, g]].astype(BF16)
        parts.append(dot_nt(pulled_b[g * size : (g + 1) * size, :], chosen))
    return jnp.concatenate(parts, axis=0)


def target_grad(xb_ref, ap_ref, counts_t):
    mapped = ap_ref[: xb_ref.shape[0], :]
    slopes_t = slopes(dot_nt(xb_ref[...], mapped), counts_t)
    return dot_nn(slopes_t, mapped).astype(BF16).astype(F32)


def add_relation(acc_ref, xb_ref, pulled_b, ids_ref, turn):
    groups = ids_ref.shape[1]
    size = pulled_b.shape[0] // groups
    for g in range(groups):
        part = slice(g * size, (g + 1) * size)
        kind = ids_ref[turn, g]
        acc_ref[kind] = acc_ref[kind] + dot_tn(xb_ref[part, :], pulled_b[part, :])


def fetched(pairs, sems):
    copies = [
        pltpu.make_async_copy(source, target, sems.at[i])
        for i, (source, target) in enumerate(pairs)
    ]
    for copy in copies:
        copy.start()
    return copies


def prepare_kernel(
    ids_ref, x_hbm, rel_hbm, src_hbm, dst_hbm, xb_ref, pay_ref, x_ref, rel_ref, src_ref, dst_ref, sems
):
    size, width = x_ref.shape
    pairs = [(x_hbm, x_ref), (rel_hbm, rel_ref), (src_hbm, src_ref), (dst_hbm, dst_ref)]
    copies = fetched(pairs, sems)
    copies[0].wait()
    rows_b = x_ref[...].astype(BF16)
    xb_ref[...] = rows_b
    copies[2].wait()
    copies[3].wait()
    pieces = (pay_ref.shape[0] - size) // 2
    pay_ref[size : size + pieces, :] = folded(src_ref, 0, width)
    pay_ref[size + pieces :, :] = folded(dst_ref, 0, width)
    copies[1].wait()
    map_rows(rows_b, rel_ref, ids_ref, 0, pay_ref)


def first_window_kernel(src_hbm, dst_hbm, c_ref, near_ref, last_ref, src_ref, dst_ref, ends_ref, sems):
    for copy in fetched([(src_hbm, src_ref), (dst_hbm, dst_ref)], sems):
        copy.wait()
    size = c_ref.shape[0]
    pieces = ends_ref.shape[0] // 2
    for turn, out in ((1, near_ref), (2, last_ref), (0, ends_ref)):
        out[:pieces, :] = folded(src_ref, turn, size)
        out[pieces:, :] = folded(dst_ref, turn, size)
    c_ref[...] = own_count(ends_ref, size)


def window_kernel(turn, fresh, ids_ref, ends_ref, xb_ref, h_ref, *refs):
    size = xb_ref.shape[0]
    refs = list(refs)
    if fresh:
        far_ref, c_ref, acc_ref, ct_ref = refs
        acc_ref[...] = jnp.zeros_like(acc_ref)
        ct_ref[...] = far_count(far_ref, size)
    else:
        acc_in_ref, c_ref, acc_ref = refs
        acc_ref[...] = acc_in_ref[...]
    add_relation(acc_ref, xb_ref, h_ref[...], ids_ref, turn - 1)
    c_ref[...] = own_count(ends_ref, size)


def round_kernel(
    turn, ids_ref, xb_ref, xq_ref, pay_ref, far_ref, c_ref, extra_ref, x_ref, rel_ref,
    xn_ref, xbn_ref, payn_ref, h_ref,
):
    size = xb_ref.shape[0]
    slopes_b = slopes(dot_nt(pay_ref[:size, :], xq_ref[...]), c_ref[...])
    pulled = dot_nn(slopes_b, xq_ref[...]).astype(BF16)
    h_ref[...] = pulled
    counts_t = far_count(far_ref, size, size) if turn == 0 else extra_ref[0][...]
    grad = source_grad(pulled, rel_ref, ids_ref, turn) + target_grad(xb_ref, far_ref, counts_t)
    moved = x_ref[...] - LEARN_RATE * grad
    xn_ref[...] = moved
    moved_b = moved.astype(BF16)
    xbn_ref[...] = moved_b
    map_rows(moved_b, rel_ref, ids_ref, turn + 1, payn_ref)
    if turn == 1:
        payn_ref[size:, :] = extra_ref[1][...]


def first_round_kernel(*refs):
    round_kernel(0, *refs[:6], None, *refs[6:])


def second_round_kernel(*refs):
    round_kernel(1, *refs[:6], refs[6:8], *refs[8:])


def last_kernel(turn, ids_ref, xb_ref, xq_ref, pay_ref, c_ref, acc_in_ref, h_ref, out_ref, acc_ref):
    size = xb_ref.shape[0]
    slopes_b = slopes(dot_nt(pay_ref[:size, :], xq_ref[...]), c_ref[...])
    pulled = dot_nn(slopes_b, xq_ref[...]).astype(BF16)
    h_ref[...] = pulled
    acc_ref[...] = acc_in_ref[...]
    add_relation(acc_ref, xb_ref, pulled, ids_ref, turn)
    kinds, width = acc_ref.shape[:2]
    for k in range(kinds):
        out_ref[k * width : (k + 1) * width, :] = acc_ref[k].astype(BF16)


def finish_kernel(turn, ids_ref, xb_ref, far_ref, h_ref, x_ref, rel_ref, xn_ref):
    counts_t = far_count(far_ref, xb_ref.shape[0], xb_ref.shape[0])
    grad = source_grad(h_ref[...], rel_ref, ids_ref, turn) + target_grad(xb_ref, far_ref, counts_t)
    xn_ref[...] = x_ref[...] - LEARN_RATE * grad


def sum_kernel(in_ref, out_ref):
    acc = in_ref[0].astype(F32)
    for i in range(1, in_ref.shape[0]):
        acc = acc + in_ref[i].astype(F32)
    total = acc.astype(BF16)
    for i in range(out_ref.shape[0]):
        out_ref[i] = total


def summed_for(parts, copies):
    count, share, width = parts.shape
    out = jax.ShapeDtypeStruct((copies, share, width), BF16)
    return call(sum_kernel, [out], [VMEM], count * share * width)(parts)[0]


def reduce_everywhere(payload):
    rows, width = payload.shape
    near = lax.axis_size(NEAR)
    far = lax.axis_size(FAR)
    part = lax.all_to_all(payload.reshape(near, rows // near, width), NEAR, 0, 0)
    part = lax.all_to_all(summed_for(part, far), FAR, 0, 0)
    part = lax.all_to_all(summed_for(part, near), NEAR, 0, 0)
    return part.reshape(rows, width).astype(F32)


def training(entity, relations, rel_ids, edge_src, edge_dst):
    rows, width = entity.shape
    kinds = relations.shape[0]
    turns, edges = edge_src.shape
    square = 2 * rows * rows * width
    counting = 2 * rows * rows * edges
    ends_rows = 2 * edges // width
    f_rows = jax.ShapeDtypeStruct((rows, width), F32)
    b_rows = jax.ShapeDtypeStruct((rows, width), BF16)
    b_pay = jax.ShapeDtypeStruct((rows + ends_rows, width), BF16)
    b_ends = jax.ShapeDtypeStruct((ends_rows, width), BF16)
    f_count = jax.ShapeDtypeStruct((rows, rows), F32)
    f_rel = jax.ShapeDtypeStruct(relations.shape, F32)
    b_rel = jax.ShapeDtypeStruct((kinds * width, width), BF16)
    edge_scratch = [pltpu.VMEM(edge_src.shape, jnp.int32)] * 2
    buckets = ((GY, 1), (GX, 1), (GY, -1))

    def exchanged(turn, rows_b, payload):
        axes, offset = buckets[turn]
        got = shifted(rows_b, axes, offset)
        far = shifted(payload, axes, -offset)
        return got, far

    xb0, pay0 = call(
        prepare_kernel, [b_rows, b_pay], [SMEM] + [HBM] * 4, square,
        scratch=[pltpu.VMEM(entity.shape, F32), pltpu.VMEM(relations.shape, F32)]
        + edge_scratch + [pltpu.SemaphoreType.DMA((4,))],
        grant=FIRST_GRANT,
    )(rel_ids, entity, relations, edge_src, edge_dst)

    xq, far = exchanged(0, xb0, pay0)
    c, ends1, ends2 = call(
        first_window_kernel, [f_count, b_ends, b_ends], [HBM] * 2, counting,
        scratch=edge_scratch + [pltpu.VMEM(b_ends.shape, BF16), pltpu.SemaphoreType.DMA((2,))],
    )(edge_src, edge_dst)
    far_ends = shifted(ends1, buckets[1][0], -buckets[1][1])
    x1, xb1, pay1, h0 = call(
        first_round_kernel, [f_rows, b_rows, b_rows, b_rows],
        [SMEM] + [VMEM] * 7, 7 * square + counting,
    )(rel_ids, xb0, xq, pay0, far, c, entity, relations)

    xq, far = exchanged(1, xb1, pay1)
    c, acc, ct = call(
        functools.partial(window_kernel, 1, True), [f_count, f_rel, f_count],
        [SMEM] + [VMEM] * 4, 2 * counting + square,
    )(rel_ids, ends1, xb0, h0, far_ends)
    x2, xb2, pay2, h1 = call(
        second_round_kernel, [f_rows, b_rows, b_pay, b_rows],
        [SMEM] + [VMEM] * 9, 7 * square,
    )(rel_ids, xb1, xq, pay1, far, c, ct, ends2, x1, relations)

    xq, far = exchanged(2, xb2, pay2)
    c, acc = call(
        functools.partial(window_kernel, 2, False), [f_count, f_rel],
        [SMEM] + [VMEM] * 4, counting + square, aliases={4: 1},
    )(rel_ids, ends2, xb1, h1, acc)
    h2, payload, _ = call(
        functools.partial(last_kernel, 2), [b_rows, b_rel, f_rel],
        [SMEM] + [VMEM] * 5, 3 * square, aliases={5: 2},
    )(rel_ids, xb2, xq, pay2, c, acc)
    x3 = call(
        functools.partial(finish_kernel, 2), [f_rows],
        [SMEM] + [VMEM] * 5, 3 * square + counting,
    )(rel_ids, xb2, far, h2, x2, relations)[0]

    summed = reduce_everywhere(payload)
    divisor = math.sqrt(turns * lax.axis_size(AXES))
    return x3, (summed / divisor).reshape(relations.shape)


def solution(mesh):
    inner = Mesh(mesh.devices.reshape(2, 4, 2, 2, 8, 2), AXES)
    return jax.shard_map(
        training,
        mesh=inner,
        in_specs=(P(AXES, None), P(), P(None, AXES), P(None, AXES), P(None, AXES)),
        out_specs=(P(AXES, None), P()),
        check_vma=False,
    )
```

```python
import math

import jax
import jax.numpy as jnp
from jax import lax
from jax.experimental import pallas as pl
from jax.experimental.pallas import tpu as pltpu
from jax.sharding import Mesh
from jax.sharding import PartitionSpec as P


AXES = ("xh", "y", "c", "xl", "zh", "zl")
GX = ("xh", "y", "c")
GY = ("xl", "zh", "zl")
NEAR = ("xh", "y", "c", "xl", "zl")
FAR = "zh"
LEARN_RATE = 0.5
FIRST_GRANT = 60 * 1024 * 1024 - 320 * 1024
VMEM = pl.BlockSpec(memory_space=pltpu.VMEM)
SMEM = pl.BlockSpec(memory_space=pltpu.SMEM)
HBM = pl.BlockSpec(memory_space=pltpu.HBM)
F32 = jnp.float32
BF16 = jnp.bfloat16


def shifted(value, axes, steps):
    count = lax.axis_size(axes)
    pairs = [(source, (source + steps) % count) for source in range(count)]
    return lax.ppermute(value, axes, pairs)


def swapped_inner(value, axes):
    return lax.ppermute(value, axes, [(i, i ^ 1) for i in range(lax.axis_size(axes))])


def swapped_outer(value, axes):
    count = lax.axis_size(axes)
    pairs = [(i, (i + (1 if i % 2 else -1)) % count) for i in range(count)]
    return lax.ppermute(value, axes, pairs)


def dot_nn(left, right):
    return lax.dot_general(left, right, (((1,), (0,)), ((), ())), preferred_element_type=F32)


def dot_nt(left, right):
    return lax.dot_general(left, right, (((1,), (1,)), ((), ())), preferred_element_type=F32)


def dot_tn(left, right):
    return lax.dot_general(left, right, (((0,), (0,)), ((), ())), preferred_element_type=F32)


def call(kernel, outs, in_specs, flops, aliases=None, scratch=(), grant=16 * 2**20):
    moved = sum(math.prod(o.shape) * o.dtype.itemsize for o in outs)
    return pl.pallas_call(
        kernel,
        out_shape=tuple(outs),
        in_specs=list(in_specs),
        out_specs=tuple(VMEM for _ in outs),
        scratch_shapes=list(scratch),
        input_output_aliases=aliases or {},
        compiler_params=pltpu.CompilerParams(vmem_limit_bytes=grant),
        cost_estimate=pl.CostEstimate(
            flops=flops, bytes_accessed=4 * moved, transcendentals=0
        ),
    )


def map_rows(rows_b, rel_ref, ids_ref, turn):
    groups = ids_ref.shape[1]
    size = rows_b.shape[0] // groups
    parts = []
    for g in range(groups):
        chosen = rel_ref[ids_ref[turn, g]].astype(BF16)
        part = slice(g * size, (g + 1) * size)
        parts.append(dot_nn(rows_b[part, :], chosen).astype(BF16))
    return jnp.concatenate(parts, axis=0)


def folded(edge_ref, turn, width):
    pieces = edge_ref.shape[1] // width
    rows = [edge_ref[turn : turn + 1, i * width : (i + 1) * width] for i in range(pieces)]
    return jnp.concatenate(rows, axis=0).astype(F32).astype(BF16)


def one_hot(row, size):
    count = row.shape[1]
    wide = jnp.broadcast_to(row.astype(F32), (16, count)).astype(BF16)
    index = lax.broadcasted_iota(jnp.int32, (16, count), 0).astype(F32).astype(BF16)
    one = jnp.ones((16, count), BF16)
    zero = jnp.zeros((16, count), BF16)
    parts = [jnp.where(wide == index + BF16(16 * i), one, zero) for i in range(size // 16)]
    return jnp.concatenate(parts, axis=0)


def counted(row_of, col_of, pieces, size):
    acc = jnp.zeros((size, size), F32)
    for i in range(pieces):
        acc = acc + dot_nt(one_hot(row_of(i), size), one_hot(col_of(i), size))
    return acc


def own_count(ends, size):
    pieces = ends.shape[0] // 2
    return counted(
        lambda i: ends[i : i + 1, :], lambda i: ends[pieces + i : pieces + i + 1, :], pieces, size
    )


def far_count(ends, size):
    pieces = ends.shape[0] // 2
    return counted(
        lambda i: ends[pieces + i : pieces + i + 1, :], lambda i: ends[i : i + 1, :], pieces, size
    )


def slopes(scores, counts):
    scaling = 1.0 / math.sqrt(scores.shape[0])
    return ((jax.nn.sigmoid(scores) - counts) * scaling).astype(BF16)


def source_grad(pulled_b, rel_ref, ids_ref, turn):
    groups = ids_ref.shape[1]
    size = pulled_b.shape[0] // groups
    parts = []
    for g in range(groups):
        chosen = rel_ref[ids_ref[turn, g]].astype(BF16)
        parts.append(dot_nt(pulled_b[g * size : (g + 1) * size, :], chosen))
    return jnp.concatenate(parts, axis=0)


def target_grad(rows_b, mapped, counts_t):
    slopes_t = slopes(dot_nt(rows_b, mapped), counts_t)
    return dot_nn(slopes_t, mapped).astype(BF16).astype(F32)


def add_relation(acc_ref, rows_b, pulled_b, ids_ref, turn):
    groups = ids_ref.shape[1]
    size = pulled_b.shape[0] // groups
    for g in range(groups):
        part = slice(g * size, (g + 1) * size)
        kind = ids_ref[turn, g]
        acc_ref[kind] = acc_ref[kind] + dot_tn(rows_b[part, :], pulled_b[part, :])


def fetched(pairs, sems):
    copies = [
        pltpu.make_async_copy(source, target, sems.at[i])
        for i, (source, target) in enumerate(pairs)
    ]
    for copy in copies:
        copy.start()
    return copies


def is_even(axis):
    return lax.axis_index(axis) == 0


def put(even, rows, mapped, inner_ref, outer_ref, part):
    inner_ref[part, :] = jnp.where(even, rows, mapped)
    outer_ref[part, :] = jnp.where(even, mapped, rows)


def sent(even, inner_ref, outer_ref, part):
    inner, outer = inner_ref[part, :], outer_ref[part, :]
    return jnp.where(even, inner, outer), jnp.where(even, outer, inner)


def got(even, inner_ref, outer_ref, part):
    inner, outer = inner_ref[part, :], outer_ref[part, :]
    return jnp.where(even, outer, inner), jnp.where(even, inner, outer)


def folded_both(src_ref, dst_ref, turn, width):
    return jnp.concatenate(
        [folded(src_ref, turn, width), folded(dst_ref, turn, width)], axis=0
    )


def prepare_kernel(
    ids_ref, x_hbm, rel_hbm, src_hbm, dst_hbm, inner_ref, outer_ref, x_ref, rel_ref, src_ref, dst_ref, sems
):
    size, width = x_ref.shape
    even = is_even(GY[-1])
    copies = fetched(
        [(src_hbm, src_ref), (dst_hbm, dst_ref), (x_hbm, x_ref), (rel_hbm, rel_ref)], sems
    )
    copies[0].wait()
    copies[1].wait()
    ends = [folded_both(src_ref, dst_ref, turn, width) for turn in (2, 0)]
    put(even, ends[0], ends[1], inner_ref, outer_ref, slice(size, inner_ref.shape[0]))
    copies[2].wait()
    rows_b = x_ref[...].astype(BF16)
    copies[3].wait()
    mapped = map_rows(rows_b, rel_ref, ids_ref, 0)
    put(even, rows_b, mapped, inner_ref, outer_ref, slice(0, size))


def first_window_kernel(src_hbm, dst_hbm, inner_ref, outer_ref, c_ref, near_ref, src_ref, dst_ref, sems):
    copies = fetched([(src_hbm, src_ref), (dst_hbm, dst_ref)], sems)
    size = c_ref.shape[0]
    _, ends = sent(is_even(GY[-1]), inner_ref, outer_ref, slice(size, inner_ref.shape[0]))
    c_ref[...] = own_count(ends.astype(F32), size)
    for copy in copies:
        copy.wait()
    near_ref[...] = folded_both(src_ref, dst_ref, 1, near_ref.shape[1])


def second_window_kernel(
    ids_ref, inner_ref, outer_ref, h_ref, ends_ref, c_ref, acc_ref
):
    size = h_ref.shape[0]
    acc_ref[...] = jnp.zeros_like(acc_ref)
    rows_b, _ = sent(is_even(GY[-1]), inner_ref, outer_ref, slice(0, size))
    add_relation(acc_ref, rows_b, h_ref[...], ids_ref, 0)
    c_ref[...] = own_count(ends_ref[...].astype(F32), size)


def third_window_kernel(
    ids_ref, inner_ref, outer_ref, h_ref, inner0_ref, outer0_ref, acc_in_ref, c_ref, acc_ref
):
    size = h_ref.shape[0]
    acc_ref[...] = acc_in_ref[...]
    rows_b, _ = sent(is_even(GX[-1]), inner_ref, outer_ref, slice(0, size))
    add_relation(acc_ref, rows_b, h_ref[...], ids_ref, 1)
    ends, _ = sent(is_even(GY[-1]), inner0_ref, outer0_ref, slice(size, inner0_ref.shape[0]))
    c_ref[...] = own_count(ends.astype(F32), size)


def stepped(turn, axis, ids_ref, sent_refs, got_refs, c_ref, x_ref, rel_ref, xn_ref, h_ref):
    size = x_ref.shape[0]
    even = is_even(axis)
    top, tail = slice(0, size), slice(size, sent_refs[0].shape[0])
    rows_b, mapped = sent(even, *sent_refs, top)
    target, far = got(even, *got_refs, top)
    slopes_b = slopes(dot_nt(mapped, target), c_ref[...])
    pulled = dot_nn(slopes_b, target).astype(BF16)
    h_ref[...] = pulled
    _, far_ends = got(even, *got_refs, tail)
    counts_t = far_count(far_ends.astype(F32), size)
    grad = source_grad(pulled, rel_ref, ids_ref, turn) + target_grad(rows_b, far, counts_t)
    moved = x_ref[...] - LEARN_RATE * grad
    xn_ref[...] = moved
    moved_b = moved.astype(BF16)
    return moved_b, map_rows(moved_b, rel_ref, ids_ref, turn + 1)


def first_round_kernel(
    ids_ref, si_ref, so_ref, gi_ref, go_ref, c_ref, near_ref, x_ref, rel_ref,
    xn_ref, h_ref, inner_ref, outer_ref,
):
    size = x_ref.shape[0]
    rows_b, mapped = stepped(
        0, GY[-1], ids_ref, (si_ref, so_ref), (gi_ref, go_ref), c_ref, x_ref, rel_ref, xn_ref, h_ref
    )
    put(is_even(GX[-1]), rows_b, mapped, inner_ref, outer_ref, slice(0, size))
    inner_ref[size:, :] = near_ref[...]
    outer_ref[size:, :] = near_ref[...]


def second_round_kernel(
    ids_ref, si_ref, so_ref, gi_ref, go_ref, c_ref, x_ref, rel_ref,
    xn_ref, h_ref, rows_ref, mapped_ref,
):
    rows_b, mapped = stepped(
        1, GX[-1], ids_ref, (si_ref, so_ref), (gi_ref, go_ref), c_ref, x_ref, rel_ref, xn_ref, h_ref
    )
    rows_ref[...] = rows_b
    mapped_ref[...] = mapped


def last_kernel(ids_ref, rows_ref, xq_ref, mapped_ref, c_ref, acc_in_ref, h_ref, out_ref, acc_ref):
    slopes_b = slopes(dot_nt(mapped_ref[...], xq_ref[...]), c_ref[...])
    pulled = dot_nn(slopes_b, xq_ref[...]).astype(BF16)
    h_ref[...] = pulled
    acc_ref[...] = acc_in_ref[...]
    add_relation(acc_ref, rows_ref, pulled, ids_ref, 2)
    kinds, width = acc_ref.shape[:2]
    for k in range(kinds):
        out_ref[k * width : (k + 1) * width, :] = acc_ref[k].astype(BF16)


def finish_kernel(ids_ref, rows_ref, far_ref, gi_ref, go_ref, h_ref, x_ref, rel_ref, xn_ref):
    size = x_ref.shape[0]
    ends, _ = got(is_even(GY[-1]), gi_ref, go_ref, slice(size, gi_ref.shape[0]))
    counts_t = far_count(ends.astype(F32), size)
    grad = source_grad(h_ref[...], rel_ref, ids_ref, 2)
    grad = grad + target_grad(rows_ref[...], far_ref[...], counts_t)
    xn_ref[...] = x_ref[...] - LEARN_RATE * grad


def sum_kernel(in_ref, out_ref):
    acc = in_ref[0].astype(F32)
    for i in range(1, in_ref.shape[0]):
        acc = acc + in_ref[i].astype(F32)
    total = acc.astype(BF16)
    for i in range(out_ref.shape[0]):
        out_ref[i] = total


def summed_for(parts, copies):
    count, share, width = parts.shape
    out = jax.ShapeDtypeStruct((copies, share, width), BF16)
    return call(sum_kernel, [out], [VMEM], count * share * width)(parts)[0]


def reduce_everywhere(payload):
    rows, width = payload.shape
    near = lax.axis_size(NEAR)
    far = lax.axis_size(FAR)
    part = lax.all_to_all(payload.reshape(near, rows // near, width), NEAR, 0, 0)
    part = lax.all_to_all(summed_for(part, far), FAR, 0, 0)
    part = lax.all_to_all(summed_for(part, near), NEAR, 0, 0)
    return part.reshape(rows, width).astype(F32)


def training(entity, relations, rel_ids, edge_src, edge_dst):
    rows, width = entity.shape
    kinds = relations.shape[0]
    turns, edges = edge_src.shape
    square = 2 * rows * rows * width
    counting = 2 * rows * rows * edges
    ends_rows = 2 * edges // width
    f_rows = jax.ShapeDtypeStruct((rows, width), F32)
    b_rows = jax.ShapeDtypeStruct((rows, width), BF16)
    b_pay = jax.ShapeDtypeStruct((rows + ends_rows, width), BF16)
    b_ends = jax.ShapeDtypeStruct((ends_rows, width), BF16)
    f_count = jax.ShapeDtypeStruct((rows, rows), F32)
    f_rel = jax.ShapeDtypeStruct(relations.shape, F32)
    b_rel = jax.ShapeDtypeStruct((kinds * width, width), BF16)
    edge_scratch = [pltpu.VMEM(edge_src.shape, jnp.int32)] * 2
    buckets = ((GY, 1), (GX, 1), (GY, -1))

    def exchanged(turn, inner, outer):
        axes = buckets[turn][0]
        outer_got = swapped_outer(outer, axes)
        inner_got = swapped_inner(inner, axes)
        return inner_got, outer_got

    sent0 = call(
        prepare_kernel, [b_pay, b_pay], [SMEM] + [HBM] * 4, square,
        scratch=[pltpu.VMEM(entity.shape, F32), pltpu.VMEM(relations.shape, F32)]
        + edge_scratch + [pltpu.SemaphoreType.DMA((4,))],
        grant=FIRST_GRANT,
    )(rel_ids, entity, relations, edge_src, edge_dst)

    got0 = exchanged(0, *sent0)
    c, ends1 = call(
        first_window_kernel, [f_count, b_ends], [HBM] * 2 + [VMEM] * 2, counting,
        scratch=edge_scratch + [pltpu.SemaphoreType.DMA((2,))],
    )(edge_src, edge_dst, *sent0)
    x1, h0, *sent1 = call(
        first_round_kernel, [f_rows, b_rows, b_pay, b_pay],
        [SMEM] + [VMEM] * 8, 7 * square + counting,
    )(rel_ids, *sent0, *got0, c, ends1, entity, relations)

    got1 = exchanged(1, *sent1)
    c, acc = call(
        second_window_kernel, [f_count, f_rel], [SMEM] + [VMEM] * 4, counting + square,
    )(rel_ids, *sent0, h0, ends1)
    x2, h1, rows2, mapped2 = call(
        second_round_kernel, [f_rows, b_rows, b_rows, b_rows],
        [SMEM] + [VMEM] * 7, 7 * square + counting,
    )(rel_ids, *sent1, *got1, c, x1, relations)

    axes, offset = buckets[2]
    xq = shifted(rows2, axes, offset)
    far = shifted(mapped2, axes, -offset)
    c, acc = call(
        third_window_kernel, [f_count, f_rel],
        [SMEM] + [VMEM] * 6, counting + square, aliases={6: 1},
    )(rel_ids, *sent1, h1, *sent0, acc)
    h2, payload, _ = call(
        last_kernel, [b_rows, b_rel, f_rel],
        [SMEM] + [VMEM] * 5, 3 * square, aliases={5: 2},
    )(rel_ids, rows2, xq, mapped2, c, acc)
    x3 = call(
        finish_kernel, [f_rows], [SMEM] + [VMEM] * 7, 3 * square + counting,
    )(rel_ids, rows2, far, *got0, h2, x2, relations)[0]

    summed = reduce_everywhere(payload)
    divisor = math.sqrt(turns * lax.axis_size(AXES))
    return x3, (summed / divisor).reshape(relations.shape)


def solution(mesh):
    inner = Mesh(mesh.devices.reshape(2, 4, 2, 2, 8, 2), AXES)
    return jax.shard_map(
        training,
        mesh=inner,
        in_specs=(P(AXES, None), P(), P(None, AXES), P(None, AXES), P(None, AXES)),
        out_specs=(P(AXES, None), P()),
        check_vma=False,
    )
```

```python
import math

import jax
import jax.numpy as jnp
from jax import lax
from jax.experimental import pallas as pl
from jax.experimental.pallas import tpu as pltpu
from jax.sharding import Mesh
from jax.sharding import PartitionSpec as P


AXES = ("xh", "y", "c", "xl", "zh", "zl")
GX = ("xh", "y", "c")
GY = ("xl", "zh", "zl")
NEAR = ("xh", "y", "c", "xl")
FAR = ("zh", "zl")
LEARN_RATE = 0.5
FIRST_GRANT = 60 * 1024 * 1024 - 320 * 1024
VMEM = pl.BlockSpec(memory_space=pltpu.VMEM)
SMEM = pl.BlockSpec(memory_space=pltpu.SMEM)
HBM = pl.BlockSpec(memory_space=pltpu.HBM)
F32 = jnp.float32
BF16 = jnp.bfloat16


def shifted(value, axes, steps):
    count = lax.axis_size(axes)
    pairs = [(source, (source + steps) % count) for source in range(count)]
    return lax.ppermute(value, axes, pairs)


def swapped_inner(value, axes):
    return lax.ppermute(value, axes, [(i, i ^ 1) for i in range(lax.axis_size(axes))])


def swapped_outer(value, axes):
    count = lax.axis_size(axes)
    pairs = [(i, (i + (1 if i % 2 else -1)) % count) for i in range(count)]
    return lax.ppermute(value, axes, pairs)


def dot_nn(left, right):
    return lax.dot_general(left, right, (((1,), (0,)), ((), ())), preferred_element_type=F32)


def dot_nt(left, right):
    return lax.dot_general(left, right, (((1,), (1,)), ((), ())), preferred_element_type=F32)


def dot_tn(left, right):
    return lax.dot_general(left, right, (((0,), (0,)), ((), ())), preferred_element_type=F32)


def call(kernel, outs, in_specs, flops, aliases=None, scratch=(), grant=16 * 2**20):
    moved = sum(math.prod(o.shape) * o.dtype.itemsize for o in outs)
    return pl.pallas_call(
        kernel,
        out_shape=tuple(outs),
        in_specs=list(in_specs),
        out_specs=tuple(VMEM for _ in outs),
        scratch_shapes=list(scratch),
        input_output_aliases=aliases or {},
        compiler_params=pltpu.CompilerParams(vmem_limit_bytes=grant),
        cost_estimate=pl.CostEstimate(
            flops=flops, bytes_accessed=4 * moved, transcendentals=0
        ),
    )


def map_rows(rows_b, rel_ref, ids_ref, turn):
    groups = ids_ref.shape[1]
    size = rows_b.shape[0] // groups
    parts = []
    for g in range(groups):
        chosen = rel_ref[ids_ref[turn, g]].astype(BF16)
        part = slice(g * size, (g + 1) * size)
        parts.append(dot_nn(rows_b[part, :], chosen).astype(BF16))
    return jnp.concatenate(parts, axis=0)


def folded(edge_ref, turn, width):
    pieces = edge_ref.shape[1] // width
    rows = [edge_ref[turn : turn + 1, i * width : (i + 1) * width] for i in range(pieces)]
    return jnp.concatenate(rows, axis=0).astype(F32).astype(BF16)


def one_hot(row, size):
    count = row.shape[1]
    wide = jnp.broadcast_to(row.astype(F32), (16, count)).astype(BF16)
    index = lax.broadcasted_iota(jnp.int32, (16, count), 0).astype(F32).astype(BF16)
    one = jnp.ones((16, count), BF16)
    zero = jnp.zeros((16, count), BF16)
    parts = [jnp.where(wide == index + BF16(16 * i), one, zero) for i in range(size // 16)]
    return jnp.concatenate(parts, axis=0)


def counted(row_of, col_of, pieces, size):
    acc = jnp.zeros((size, size), F32)
    for i in range(pieces):
        acc = acc + dot_nt(one_hot(row_of(i), size), one_hot(col_of(i), size))
    return acc


def own_count(ends, size):
    pieces = ends.shape[0] // 2
    return counted(
        lambda i: ends[i : i + 1, :], lambda i: ends[pieces + i : pieces + i + 1, :], pieces, size
    )


def far_count(ends, size):
    pieces = ends.shape[0] // 2
    return counted(
        lambda i: ends[pieces + i : pieces + i + 1, :], lambda i: ends[i : i + 1, :], pieces, size
    )


def slopes(scores, counts):
    scaling = 1.0 / math.sqrt(scores.shape[0])
    return ((jax.nn.sigmoid(scores) - counts) * scaling).astype(BF16)


def source_grad(pulled_b, rel_ref, ids_ref, turn):
    groups = ids_ref.shape[1]
    size = pulled_b.shape[0] // groups
    parts = []
    for g in range(groups):
        chosen = rel_ref[ids_ref[turn, g]].astype(BF16)
        parts.append(dot_nt(pulled_b[g * size : (g + 1) * size, :], chosen))
    return jnp.concatenate(parts, axis=0)


def target_grad(rows_b, mapped, counts_t):
    slopes_t = slopes(dot_nt(rows_b, mapped), counts_t)
    return dot_nn(slopes_t, mapped).astype(BF16).astype(F32)


def add_relation(acc_ref, rows_b, pulled_b, ids_ref, turn):
    groups = ids_ref.shape[1]
    size = pulled_b.shape[0] // groups
    for g in range(groups):
        part = slice(g * size, (g + 1) * size)
        kind = ids_ref[turn, g]
        acc_ref[kind] = acc_ref[kind] + dot_tn(rows_b[part, :], pulled_b[part, :])


def fetched(pairs, sems):
    copies = [
        pltpu.make_async_copy(source, target, sems.at[i])
        for i, (source, target) in enumerate(pairs)
    ]
    for copy in copies:
        copy.start()
    return copies


def is_even(axis):
    return lax.axis_index(axis) == 0


def put(even, rows, mapped, inner_ref, outer_ref, part):
    inner_ref[part, :] = jnp.where(even, rows, mapped)
    outer_ref[part, :] = jnp.where(even, mapped, rows)


def sent(even, inner_ref, outer_ref, part):
    inner, outer = inner_ref[part, :], outer_ref[part, :]
    return jnp.where(even, inner, outer), jnp.where(even, outer, inner)


def got(even, inner_ref, outer_ref, part):
    inner, outer = inner_ref[part, :], outer_ref[part, :]
    return jnp.where(even, outer, inner), jnp.where(even, inner, outer)


def folded_both(src_ref, dst_ref, turn, width):
    return jnp.concatenate(
        [folded(src_ref, turn, width), folded(dst_ref, turn, width)], axis=0
    )


def prepare_kernel(
    ids_ref, x_hbm, rel_hbm, src_hbm, dst_hbm, inner_ref, outer_ref, x_ref, rel_ref, src_ref, dst_ref, sems
):
    size, width = x_ref.shape
    even = is_even(GY[-1])
    copies = fetched(
        [(src_hbm, src_ref), (dst_hbm, dst_ref), (x_hbm, x_ref), (rel_hbm, rel_ref)], sems
    )
    copies[0].wait()
    copies[1].wait()
    ends = [folded_both(src_ref, dst_ref, turn, width) for turn in (2, 0)]
    put(even, ends[0], ends[1], inner_ref, outer_ref, slice(size, inner_ref.shape[0]))
    copies[2].wait()
    rows_b = x_ref[...].astype(BF16)
    copies[3].wait()
    mapped = map_rows(rows_b, rel_ref, ids_ref, 0)
    put(even, rows_b, mapped, inner_ref, outer_ref, slice(0, size))


def first_window_kernel(src_hbm, dst_hbm, *refs):
    *out_refs, src_ref, dst_ref, sems = refs
    near_ref = out_refs.pop()
    for copy in fetched([(src_hbm, src_ref), (dst_hbm, dst_ref)], sems):
        copy.wait()
    size = out_refs[0].shape[0]
    for turn, out_ref in enumerate(out_refs):
        ends = folded_both(src_ref, dst_ref, turn, size)
        if turn == 1:
            near_ref[...] = ends
        out_ref[...] = own_count(ends.astype(F32), size)


def relation_kernel(ids_ref, si0_ref, so0_ref, h0_ref, si1_ref, so1_ref, h1_ref, acc_ref):
    top = slice(0, h0_ref.shape[0])
    acc_ref[...] = jnp.zeros_like(acc_ref)
    rows_b, _ = sent(is_even(GY[-1]), si0_ref, so0_ref, top)
    add_relation(acc_ref, rows_b, h0_ref[...], ids_ref, 0)
    rows_b, _ = sent(is_even(GX[-1]), si1_ref, so1_ref, top)
    add_relation(acc_ref, rows_b, h1_ref[...], ids_ref, 1)


def stepped(turn, axis, ids_ref, sent_refs, got_refs, c_ref, x_ref, rel_ref, xn_ref, h_ref):
    size = x_ref.shape[0]
    even = is_even(axis)
    top, tail = slice(0, size), slice(size, sent_refs[0].shape[0])
    rows_b, mapped = sent(even, *sent_refs, top)
    target, far = got(even, *got_refs, top)
    slopes_b = slopes(dot_nt(mapped, target), c_ref[...])
    pulled = dot_nn(slopes_b, target).astype(BF16)
    h_ref[...] = pulled
    _, far_ends = got(even, *got_refs, tail)
    counts_t = far_count(far_ends.astype(F32), size)
    grad = source_grad(pulled, rel_ref, ids_ref, turn) + target_grad(rows_b, far, counts_t)
    moved = x_ref[...] - LEARN_RATE * grad
    xn_ref[...] = moved
    moved_b = moved.astype(BF16)
    return moved_b, map_rows(moved_b, rel_ref, ids_ref, turn + 1)


def first_round_kernel(
    ids_ref, si_ref, so_ref, gi_ref, go_ref, c_ref, near_ref, x_ref, rel_ref,
    xn_ref, h_ref, inner_ref, outer_ref,
):
    size = x_ref.shape[0]
    rows_b, mapped = stepped(
        0, GY[-1], ids_ref, (si_ref, so_ref), (gi_ref, go_ref), c_ref, x_ref, rel_ref, xn_ref, h_ref
    )
    put(is_even(GX[-1]), rows_b, mapped, inner_ref, outer_ref, slice(0, size))
    inner_ref[size:, :] = near_ref[...]
    outer_ref[size:, :] = near_ref[...]


def second_round_kernel(
    ids_ref, si_ref, so_ref, gi_ref, go_ref, c_ref, x_ref, rel_ref,
    xn_ref, h_ref, rows_ref, mapped_ref,
):
    rows_b, mapped = stepped(
        1, GX[-1], ids_ref, (si_ref, so_ref), (gi_ref, go_ref), c_ref, x_ref, rel_ref, xn_ref, h_ref
    )
    rows_ref[...] = rows_b
    mapped_ref[...] = mapped


def last_kernel(ids_ref, rows_ref, xq_ref, mapped_ref, c_ref, acc_in_ref, h_ref, out_ref, acc_ref):
    slopes_b = slopes(dot_nt(mapped_ref[...], xq_ref[...]), c_ref[...])
    pulled = dot_nn(slopes_b, xq_ref[...]).astype(BF16)
    h_ref[...] = pulled
    acc_ref[...] = acc_in_ref[...]
    add_relation(acc_ref, rows_ref, pulled, ids_ref, 2)
    kinds, width = acc_ref.shape[:2]
    for k in range(kinds):
        out_ref[k * width : (k + 1) * width, :] = acc_ref[k].astype(BF16)


def finish_kernel(ids_ref, rows_ref, far_ref, gi_ref, go_ref, h_ref, x_ref, rel_ref, xn_ref):
    size = x_ref.shape[0]
    ends, _ = got(is_even(GY[-1]), gi_ref, go_ref, slice(size, gi_ref.shape[0]))
    counts_t = far_count(ends.astype(F32), size)
    grad = source_grad(h_ref[...], rel_ref, ids_ref, 2)
    grad = grad + target_grad(rows_ref[...], far_ref[...], counts_t)
    xn_ref[...] = x_ref[...] - LEARN_RATE * grad


def sum_kernel(in_ref, out_ref):
    acc = in_ref[0].astype(F32)
    for i in range(1, in_ref.shape[0]):
        acc = acc + in_ref[i].astype(F32)
    total = acc.astype(BF16)
    for i in range(out_ref.shape[0]):
        out_ref[i] = total


def summed_for(parts, copies):
    count, share, width = parts.shape
    out = jax.ShapeDtypeStruct((copies, share, width), BF16)
    return call(sum_kernel, [out], [VMEM], count * share * width)(parts)[0]


def reduce_everywhere(payload):
    rows, width = payload.shape
    near = lax.axis_size(NEAR)
    far = lax.axis_size(FAR)
    part = lax.all_to_all(payload.reshape(near, rows // near, width), NEAR, 0, 0)
    part = summed_for(part, far)
    part = lax.all_to_all(part, FAR, 0, 0)
    part = lax.all_to_all(summed_for(part, near), NEAR, 0, 0)
    return part.reshape(rows, width).astype(F32)


def training(entity, relations, rel_ids, edge_src, edge_dst):
    rows, width = entity.shape
    kinds = relations.shape[0]
    turns, edges = edge_src.shape
    square = 2 * rows * rows * width
    counting = 2 * rows * rows * edges
    ends_rows = 2 * edges // width
    f_rows = jax.ShapeDtypeStruct((rows, width), F32)
    b_rows = jax.ShapeDtypeStruct((rows, width), BF16)
    b_pay = jax.ShapeDtypeStruct((rows + ends_rows, width), BF16)
    b_ends = jax.ShapeDtypeStruct((ends_rows, width), BF16)
    f_count = jax.ShapeDtypeStruct((rows, rows), F32)
    f_rel = jax.ShapeDtypeStruct(relations.shape, F32)
    b_rel = jax.ShapeDtypeStruct((kinds * width, width), BF16)
    edge_scratch = [pltpu.VMEM(edge_src.shape, jnp.int32)] * 2
    buckets = ((GY, 1), (GX, 1), (GY, -1))

    def exchanged(turn, inner, outer):
        axes = buckets[turn][0]
        outer_got = swapped_outer(outer, axes)
        inner_got = swapped_inner(inner, axes)
        return inner_got, outer_got

    sent0 = call(
        prepare_kernel, [b_pay, b_pay], [SMEM] + [HBM] * 4, square,
        scratch=[pltpu.VMEM(entity.shape, F32), pltpu.VMEM(relations.shape, F32)]
        + edge_scratch + [pltpu.SemaphoreType.DMA((4,))],
        grant=FIRST_GRANT,
    )(rel_ids, entity, relations, edge_src, edge_dst)

    got0 = exchanged(0, *sent0)
    c0, c1, c2, ends1 = call(
        first_window_kernel, [f_count] * turns + [b_ends], [HBM] * 2, turns * counting,
        scratch=edge_scratch + [pltpu.SemaphoreType.DMA((2,))],
    )(edge_src, edge_dst)
    x1, h0, *sent1 = call(
        first_round_kernel, [f_rows, b_rows, b_pay, b_pay],
        [SMEM] + [VMEM] * 8, 7 * square + counting,
    )(rel_ids, *sent0, *got0, c0, ends1, entity, relations)

    got1 = exchanged(1, *sent1)
    x2, h1, rows2, mapped2 = call(
        second_round_kernel, [f_rows, b_rows, b_rows, b_rows],
        [SMEM] + [VMEM] * 7, 7 * square + counting,
    )(rel_ids, *sent1, *got1, c1, x1, relations)

    axes, offset = buckets[2]
    xq = shifted(rows2, axes, offset)
    far = shifted(mapped2, axes, -offset)
    acc = call(
        relation_kernel, [f_rel], [SMEM] + [VMEM] * 6, 2 * square,
    )(rel_ids, *sent0, h0, *sent1, h1)[0]
    h2, payload, _ = call(
        last_kernel, [b_rows, b_rel, f_rel],
        [SMEM] + [VMEM] * 5, 3 * square, aliases={5: 2},
    )(rel_ids, rows2, xq, mapped2, c2, acc)
    x3 = call(
        finish_kernel, [f_rows], [SMEM] + [VMEM] * 7, 3 * square + counting,
    )(rel_ids, rows2, far, *got0, h2, x2, relations)[0]

    summed = reduce_everywhere(payload)
    divisor = math.sqrt(turns * lax.axis_size(AXES))
    return x3, (summed / divisor).reshape(relations.shape)


def solution(mesh):
    inner = Mesh(mesh.devices.reshape(2, 4, 2, 2, 8, 2), AXES)
    return jax.shard_map(
        training,
        mesh=inner,
        in_specs=(P(AXES, None), P(), P(None, AXES), P(None, AXES), P(None, AXES)),
        out_specs=(P(AXES, None), P()),
        check_vma=False,
    )
```

```python
import math

import jax
import jax.numpy as jnp
from jax import lax
from jax.experimental import pallas as pl
from jax.experimental.pallas import tpu as pltpu
from jax.sharding import Mesh
from jax.sharding import PartitionSpec as P


AXES = ("xh", "y", "c", "xl", "zh", "zl")
GX = ("xh", "y", "c")
GY = ("xl", "zh", "zl")
NEAR = ("xh", "y", "c", "xl")
FAR = ("zh", "zl")
LEARN_RATE = 0.5
VMEM = pl.BlockSpec(memory_space=pltpu.VMEM)
SMEM = pl.BlockSpec(memory_space=pltpu.SMEM)
HBM = pl.BlockSpec(memory_space=pltpu.HBM)
F32 = jnp.float32
BF16 = jnp.bfloat16


def shifted(value, axes, steps):
    count = lax.axis_size(axes)
    pairs = [(source, (source + steps) % count) for source in range(count)]
    return lax.ppermute(value, axes, pairs)


def swapped_inner(value, axes):
    return lax.ppermute(value, axes, [(i, i ^ 1) for i in range(lax.axis_size(axes))])


def swapped_outer(value, axes):
    count = lax.axis_size(axes)
    pairs = [(i, (i + (1 if i % 2 else -1)) % count) for i in range(count)]
    return lax.ppermute(value, axes, pairs)


def dot_nn(left, right):
    return lax.dot_general(left, right, (((1,), (0,)), ((), ())), preferred_element_type=F32)


def dot_nt(left, right):
    return lax.dot_general(left, right, (((1,), (1,)), ((), ())), preferred_element_type=F32)


def dot_tn(left, right):
    return lax.dot_general(left, right, (((0,), (0,)), ((), ())), preferred_element_type=F32)


def call(kernel, outs, in_specs, flops, aliases=None, scratch=()):
    moved = sum(math.prod(o.shape) * o.dtype.itemsize for o in outs)
    return pl.pallas_call(
        kernel,
        out_shape=tuple(outs),
        in_specs=list(in_specs),
        out_specs=tuple(VMEM for _ in outs),
        scratch_shapes=list(scratch),
        input_output_aliases=aliases or {},
        compiler_params=pltpu.CompilerParams(vmem_limit_bytes=16 * 2**20),
        cost_estimate=pl.CostEstimate(
            flops=flops, bytes_accessed=4 * moved, transcendentals=0
        ),
    )


def map_rows(rows_b, rel_ref, ids_ref, turn):
    groups = ids_ref.shape[1]
    size = rows_b.shape[0] // groups
    parts = []
    for g in range(groups):
        chosen = rel_ref[ids_ref[turn, g]].astype(BF16)
        part = slice(g * size, (g + 1) * size)
        parts.append(dot_nn(rows_b[part, :], chosen).astype(BF16))
    return jnp.concatenate(parts, axis=0)


def folded(edge_ref, turn, width):
    pieces = edge_ref.shape[1] // width
    rows = [edge_ref[turn : turn + 1, i * width : (i + 1) * width] for i in range(pieces)]
    return jnp.concatenate(rows, axis=0).astype(F32).astype(BF16)


def one_hot(row, size):
    count = row.shape[1]
    wide = jnp.broadcast_to(row.astype(F32), (16, count)).astype(BF16)
    index = lax.broadcasted_iota(jnp.int32, (16, count), 0).astype(F32).astype(BF16)
    one = jnp.ones((16, count), BF16)
    zero = jnp.zeros((16, count), BF16)
    parts = [jnp.where(wide == index + BF16(16 * i), one, zero) for i in range(size // 16)]
    return jnp.concatenate(parts, axis=0)


def counted(row_of, col_of, pieces, size):
    acc = jnp.zeros((size, size), F32)
    for i in range(pieces):
        acc = acc + dot_nt(one_hot(row_of(i), size), one_hot(col_of(i), size))
    return acc


def own_count(ends, size):
    pieces = ends.shape[0] // 2
    return counted(
        lambda i: ends[i : i + 1, :], lambda i: ends[pieces + i : pieces + i + 1, :], pieces, size
    )


def far_count(ends, size):
    pieces = ends.shape[0] // 2
    return counted(
        lambda i: ends[pieces + i : pieces + i + 1, :], lambda i: ends[i : i + 1, :], pieces, size
    )


def slopes(scores, counts):
    scaling = 1.0 / math.sqrt(scores.shape[0])
    return ((jax.nn.sigmoid(scores) - counts) * scaling).astype(BF16)


def source_grad(pulled_b, rel_ref, ids_ref, turn):
    groups = ids_ref.shape[1]
    size = pulled_b.shape[0] // groups
    parts = []
    for g in range(groups):
        chosen = rel_ref[ids_ref[turn, g]].astype(BF16)
        parts.append(dot_nt(pulled_b[g * size : (g + 1) * size, :], chosen))
    return jnp.concatenate(parts, axis=0)


def target_grad(rows_b, mapped, counts_t):
    slopes_t = slopes(dot_nt(rows_b, mapped), counts_t)
    return dot_nn(slopes_t, mapped).astype(BF16).astype(F32)


def add_relation(acc_ref, rows_b, pulled_b, ids_ref, turn):
    groups = ids_ref.shape[1]
    size = pulled_b.shape[0] // groups
    for g in range(groups):
        part = slice(g * size, (g + 1) * size)
        kind = ids_ref[turn, g]
        acc_ref[kind] = acc_ref[kind] + dot_tn(rows_b[part, :], pulled_b[part, :])


def fetched(pairs, sems):
    copies = [
        pltpu.make_async_copy(source, target, sems.at[i])
        for i, (source, target) in enumerate(pairs)
    ]
    for copy in copies:
        copy.start()
    return copies


def is_even(axis):
    return lax.axis_index(axis) == 0


def put(even, rows, mapped, inner_ref, outer_ref, part):
    inner_ref[part, :] = jnp.where(even, rows, mapped)
    outer_ref[part, :] = jnp.where(even, mapped, rows)


def sent(even, inner_ref, outer_ref, part):
    inner, outer = inner_ref[part, :], outer_ref[part, :]
    return jnp.where(even, inner, outer), jnp.where(even, outer, inner)


def got(even, inner_ref, outer_ref, part):
    inner, outer = inner_ref[part, :], outer_ref[part, :]
    return jnp.where(even, outer, inner), jnp.where(even, inner, outer)


def in_hbm(*values):
    return [pltpu.with_memory_space_constraint(value, pltpu.HBM) for value in values]


def folded_both(src_ref, dst_ref, turn, width):
    return jnp.concatenate(
        [folded(src_ref, turn, width), folded(dst_ref, turn, width)], axis=0
    )


def prepare_kernel(
    ids_hbm, x_hbm, rel_hbm, src_hbm, dst_hbm, inner_ref, outer_ref,
    ids_ref, x_ref, rel_ref, src_ref, dst_ref, sems,
):
    size, width = x_ref.shape
    even = is_even(GY[-1])
    copies = fetched(
        [
            (src_hbm, src_ref), (dst_hbm, dst_ref), (x_hbm, x_ref), (rel_hbm, rel_ref),
            (ids_hbm, ids_ref),
        ],
        sems,
    )
    copies[0].wait()
    copies[1].wait()
    ends = [folded_both(src_ref, dst_ref, turn, width) for turn in (2, 0)]
    put(even, ends[0], ends[1], inner_ref, outer_ref, slice(size, inner_ref.shape[0]))
    copies[2].wait()
    rows_b = x_ref[...].astype(BF16)
    copies[3].wait()
    copies[4].wait()
    mapped = map_rows(rows_b, rel_ref, ids_ref, 0)
    put(even, rows_b, mapped, inner_ref, outer_ref, slice(0, size))


def first_window_kernel(src_hbm, dst_hbm, *refs):
    *out_refs, src_ref, dst_ref, sems = refs
    near_ref = out_refs.pop()
    for copy in fetched([(src_hbm, src_ref), (dst_hbm, dst_ref)], sems):
        copy.wait()
    size = out_refs[0].shape[0]
    for turn, out_ref in enumerate(out_refs):
        ends = folded_both(src_ref, dst_ref, turn, size)
        if turn == 1:
            near_ref[...] = ends
        out_ref[...] = own_count(ends.astype(F32), size)


def relation_kernel(ids_ref, si0_ref, so0_ref, h0_ref, si1_ref, so1_ref, h1_ref, acc_ref):
    top = slice(0, h0_ref.shape[0])
    acc_ref[...] = jnp.zeros_like(acc_ref)
    rows_b, _ = sent(is_even(GY[-1]), si0_ref, so0_ref, top)
    add_relation(acc_ref, rows_b, h0_ref[...], ids_ref, 0)
    rows_b, _ = sent(is_even(GX[-1]), si1_ref, so1_ref, top)
    add_relation(acc_ref, rows_b, h1_ref[...], ids_ref, 1)


def stepped(turn, axis, ids_ref, sent_refs, got_refs, c_ref, x_ref, rel_ref, xn_ref, h_ref):
    size = x_ref.shape[0]
    even = is_even(axis)
    top, tail = slice(0, size), slice(size, sent_refs[0].shape[0])
    rows_b, mapped = sent(even, *sent_refs, top)
    target, far = got(even, *got_refs, top)
    slopes_b = slopes(dot_nt(mapped, target), c_ref[...])
    pulled = dot_nn(slopes_b, target).astype(BF16)
    h_ref[...] = pulled
    _, far_ends = got(even, *got_refs, tail)
    counts_t = far_count(far_ends.astype(F32), size)
    grad = source_grad(pulled, rel_ref, ids_ref, turn) + target_grad(rows_b, far, counts_t)
    moved = x_ref[...] - LEARN_RATE * grad
    xn_ref[...] = moved
    moved_b = moved.astype(BF16)
    return moved_b, map_rows(moved_b, rel_ref, ids_ref, turn + 1)


def first_round_kernel(
    ids_ref, si_ref, so_ref, gi_ref, go_ref, c_ref, near_ref, x_ref, rel_ref,
    xn_ref, h_ref, inner_ref, outer_ref,
):
    size = x_ref.shape[0]
    rows_b, mapped = stepped(
        0, GY[-1], ids_ref, (si_ref, so_ref), (gi_ref, go_ref), c_ref, x_ref, rel_ref, xn_ref, h_ref
    )
    put(is_even(GX[-1]), rows_b, mapped, inner_ref, outer_ref, slice(0, size))
    inner_ref[size:, :] = near_ref[...]
    outer_ref[size:, :] = near_ref[...]


def second_round_kernel(
    ids_ref, si_ref, so_ref, gi_ref, go_ref, c_ref, x_ref, rel_ref,
    xn_ref, h_ref, rows_ref, mapped_ref,
):
    rows_b, mapped = stepped(
        1, GX[-1], ids_ref, (si_ref, so_ref), (gi_ref, go_ref), c_ref, x_ref, rel_ref, xn_ref, h_ref
    )
    rows_ref[...] = rows_b
    mapped_ref[...] = mapped


def last_kernel(ids_ref, rows_ref, xq_ref, mapped_ref, c_ref, acc_in_ref, h_ref, out_ref, acc_ref):
    slopes_b = slopes(dot_nt(mapped_ref[...], xq_ref[...]), c_ref[...])
    pulled = dot_nn(slopes_b, xq_ref[...]).astype(BF16)
    h_ref[...] = pulled
    acc_ref[...] = acc_in_ref[...]
    add_relation(acc_ref, rows_ref, pulled, ids_ref, 2)
    kinds, width = acc_ref.shape[:2]
    for k in range(kinds):
        out_ref[k * width : (k + 1) * width, :] = acc_ref[k].astype(BF16)


def finish_kernel(ids_ref, rows_ref, far_ref, gi_ref, go_ref, h_ref, x_ref, rel_ref, xn_ref):
    size = x_ref.shape[0]
    ends, _ = got(is_even(GY[-1]), gi_ref, go_ref, slice(size, gi_ref.shape[0]))
    counts_t = far_count(ends.astype(F32), size)
    grad = source_grad(h_ref[...], rel_ref, ids_ref, 2)
    grad = grad + target_grad(rows_ref[...], far_ref[...], counts_t)
    xn_ref[...] = x_ref[...] - LEARN_RATE * grad


def sum_kernel(in_ref, out_ref):
    acc = in_ref[0].astype(F32)
    for i in range(1, in_ref.shape[0]):
        acc = acc + in_ref[i].astype(F32)
    total = acc.astype(BF16)
    for i in range(out_ref.shape[0]):
        out_ref[i] = total


def summed_for(parts, copies):
    count, share, width = parts.shape
    out = jax.ShapeDtypeStruct((copies, share, width), BF16)
    return call(sum_kernel, [out], [VMEM], count * share * width)(parts)[0]


def reduce_everywhere(payload):
    rows, width = payload.shape
    near = lax.axis_size(NEAR)
    far = lax.axis_size(FAR)
    part = lax.all_to_all(payload.reshape(near, rows // near, width), NEAR, 0, 0)
    part = summed_for(part, far)
    part = lax.all_to_all(part, FAR, 0, 0)
    part = lax.all_to_all(summed_for(part, near), NEAR, 0, 0)
    return part.reshape(rows, width).astype(F32)


def training(entity, relations, rel_ids, edge_src, edge_dst):
    rows, width = entity.shape
    kinds = relations.shape[0]
    turns, edges = edge_src.shape
    square = 2 * rows * rows * width
    counting = 2 * rows * rows * edges
    ends_rows = 2 * edges // width
    f_rows = jax.ShapeDtypeStruct((rows, width), F32)
    b_rows = jax.ShapeDtypeStruct((rows, width), BF16)
    b_pay = jax.ShapeDtypeStruct((rows + ends_rows, width), BF16)
    b_ends = jax.ShapeDtypeStruct((ends_rows, width), BF16)
    f_count = jax.ShapeDtypeStruct((rows, rows), F32)
    f_rel = jax.ShapeDtypeStruct(relations.shape, F32)
    b_rel = jax.ShapeDtypeStruct((kinds * width, width), BF16)
    edge_scratch = [pltpu.VMEM(edge_src.shape, jnp.int32)] * 2
    buckets = ((GY, 1), (GX, 1), (GY, -1))

    def exchanged(turn, inner, outer):
        axes = buckets[turn][0]
        outer_got = swapped_outer(outer, axes)
        inner_got = swapped_inner(inner, axes)
        return inner_got, outer_got

    sent0 = call(
        prepare_kernel, [b_pay, b_pay], [HBM] * 5, square,
        scratch=[pltpu.SMEM(rel_ids.shape, jnp.int32), pltpu.VMEM(entity.shape, F32)]
        + [pltpu.VMEM(relations.shape, F32)] + edge_scratch + [pltpu.SemaphoreType.DMA((5,))],
    )(*in_hbm(rel_ids, entity, relations, edge_src, edge_dst))

    got0 = exchanged(0, *sent0)
    c0, c1, c2, ends1 = call(
        first_window_kernel, [f_count] * turns + [b_ends], [HBM] * 2, turns * counting,
        scratch=edge_scratch + [pltpu.SemaphoreType.DMA((2,))],
    )(*in_hbm(edge_src, edge_dst))
    x1, h0, *sent1 = call(
        first_round_kernel, [f_rows, b_rows, b_pay, b_pay],
        [SMEM] + [VMEM] * 8, 7 * square + counting,
    )(rel_ids, *sent0, *got0, c0, ends1, entity, relations)

    got1 = exchanged(1, *sent1)
    x2, h1, rows2, mapped2 = call(
        second_round_kernel, [f_rows, b_rows, b_rows, b_rows],
        [SMEM] + [VMEM] * 7, 7 * square + counting,
    )(rel_ids, *sent1, *got1, c1, x1, relations)

    axes, offset = buckets[2]
    xq = shifted(rows2, axes, offset)
    far = shifted(mapped2, axes, -offset)
    acc = call(
        relation_kernel, [f_rel], [SMEM] + [VMEM] * 6, 2 * square,
    )(rel_ids, *sent0, h0, *sent1, h1)[0]
    h2, payload, _ = call(
        last_kernel, [b_rows, b_rel, f_rel],
        [SMEM] + [VMEM] * 5, 3 * square, aliases={5: 2},
    )(rel_ids, rows2, xq, mapped2, c2, acc)
    x3 = call(
        finish_kernel, [f_rows], [SMEM] + [VMEM] * 7, 3 * square + counting,
    )(rel_ids, rows2, far, *got0, h2, x2, relations)[0]

    summed = reduce_everywhere(payload)
    divisor = math.sqrt(turns * lax.axis_size(AXES))
    return x3, (summed / divisor).reshape(relations.shape)


def solution(mesh):
    inner = Mesh(mesh.devices.reshape(2, 4, 2, 2, 8, 2), AXES)
    return jax.shard_map(
        training,
        mesh=inner,
        in_specs=(P(AXES, None), P(), P(None, AXES), P(None, AXES), P(None, AXES)),
        out_specs=(P(AXES, None), P()),
        check_vma=False,
    )
```

```python
import functools
import math

import jax
import jax.numpy as jnp
from jax import lax
from jax.experimental import pallas as pl
from jax.experimental.pallas import tpu as pltpu
from jax.sharding import Mesh
from jax.sharding import PartitionSpec as P


AXES = ("xh", "y", "c", "xl", "zh", "zl")
GX = ("xh", "y", "c")
GY = ("xl", "zh", "zl")
PLANE = ("xh", "y", "c", "xl")
NEAR = PLANE + ("zl",)
DEPTH = ("zh", "zl")
LEARN_RATE = 0.5
VMEM = pl.BlockSpec(memory_space=pltpu.VMEM)
SMEM = pl.BlockSpec(memory_space=pltpu.SMEM)
HBM = pl.BlockSpec(memory_space=pltpu.HBM)
F32 = jnp.float32
BF16 = jnp.bfloat16


def shifted(value, axes, steps):
    count = lax.axis_size(axes)
    pairs = [(source, (source + steps) % count) for source in range(count)]
    return lax.ppermute(value, axes, pairs)


def swapped_inner(value, axes):
    return lax.ppermute(value, axes, [(i, i ^ 1) for i in range(lax.axis_size(axes))])


def swapped_outer(value, axes):
    count = lax.axis_size(axes)
    pairs = [(i, (i + (1 if i % 2 else -1)) % count) for i in range(count)]
    return lax.ppermute(value, axes, pairs)


def dot_nn(left, right):
    return lax.dot_general(left, right, (((1,), (0,)), ((), ())), preferred_element_type=F32)


def dot_nt(left, right):
    return lax.dot_general(left, right, (((1,), (1,)), ((), ())), preferred_element_type=F32)


def dot_tn(left, right):
    return lax.dot_general(left, right, (((0,), (0,)), ((), ())), preferred_element_type=F32)


def call(kernel, outs, in_specs, flops, aliases=None, scratch=()):
    moved = sum(math.prod(o.shape) * o.dtype.itemsize for o in outs)
    return pl.pallas_call(
        kernel,
        out_shape=tuple(outs),
        in_specs=list(in_specs),
        out_specs=tuple(VMEM for _ in outs),
        scratch_shapes=list(scratch),
        input_output_aliases=aliases or {},
        compiler_params=pltpu.CompilerParams(vmem_limit_bytes=16 * 2**20),
        cost_estimate=pl.CostEstimate(
            flops=flops, bytes_accessed=4 * moved, transcendentals=0
        ),
    )


def map_rows(rows_b, rel_ref, ids_ref, turn):
    groups = ids_ref.shape[1]
    size = rows_b.shape[0] // groups
    parts = []
    for g in range(groups):
        chosen = rel_ref[ids_ref[turn, g]].astype(BF16)
        part = slice(g * size, (g + 1) * size)
        parts.append(dot_nn(rows_b[part, :], chosen).astype(BF16))
    return jnp.concatenate(parts, axis=0)


def folded(edge_ref, turn, width):
    pieces = edge_ref.shape[1] // width
    rows = [edge_ref[turn : turn + 1, i * width : (i + 1) * width] for i in range(pieces)]
    return jnp.concatenate(rows, axis=0).astype(F32).astype(BF16)


def one_hot(row, size):
    count = row.shape[1]
    wide = jnp.broadcast_to(row.astype(F32), (16, count)).astype(BF16)
    index = lax.broadcasted_iota(jnp.int32, (16, count), 0).astype(F32).astype(BF16)
    one = jnp.ones((16, count), BF16)
    zero = jnp.zeros((16, count), BF16)
    parts = [jnp.where(wide == index + BF16(16 * i), one, zero) for i in range(size // 16)]
    return jnp.concatenate(parts, axis=0).astype(jnp.float8_e4m3fn)


def counted(row_of, col_of, pieces, size):
    acc = jnp.zeros((size, size), F32)
    for i in range(pieces):
        acc = acc + dot_nt(one_hot(row_of(i), size), one_hot(col_of(i), size))
    return acc


def own_count(ends, size):
    pieces = ends.shape[0] // 2
    return counted(
        lambda i: ends[i : i + 1, :], lambda i: ends[pieces + i : pieces + i + 1, :], pieces, size
    )


def far_count(ends, size):
    pieces = ends.shape[0] // 2
    return counted(
        lambda i: ends[pieces + i : pieces + i + 1, :], lambda i: ends[i : i + 1, :], pieces, size
    )


def slopes(scores, counts):
    scaling = 1.0 / math.sqrt(scores.shape[0])
    return ((jax.nn.sigmoid(scores) - counts) * scaling).astype(BF16)


def source_grad(pulled_b, rel_ref, ids_ref, turn):
    groups = ids_ref.shape[1]
    size = pulled_b.shape[0] // groups
    parts = []
    for g in range(groups):
        chosen = rel_ref[ids_ref[turn, g]].astype(BF16)
        parts.append(dot_nt(pulled_b[g * size : (g + 1) * size, :], chosen))
    return jnp.concatenate(parts, axis=0)


def target_grad(rows_b, mapped, counts_t):
    slopes_t = slopes(dot_nt(rows_b, mapped), counts_t)
    return dot_nn(slopes_t, mapped).astype(BF16).astype(F32)


def add_relation(acc_ref, rows_b, pulled_b, ids_ref, turn):
    groups = ids_ref.shape[1]
    size = pulled_b.shape[0] // groups
    for g in range(groups):
        part = slice(g * size, (g + 1) * size)
        kind = ids_ref[turn, g]
        acc_ref[kind] = acc_ref[kind] + dot_tn(rows_b[part, :], pulled_b[part, :])


def fetched(pairs, sems):
    copies = [
        pltpu.make_async_copy(source, target, sems.at[i])
        for i, (source, target) in enumerate(pairs)
    ]
    for copy in copies:
        copy.start()
    return copies


def is_even(axis):
    return lax.axis_index(axis) == 0


def put(even, rows, mapped, inner_ref, outer_ref, part):
    inner_ref[part, :] = jnp.where(even, rows, mapped)
    outer_ref[part, :] = jnp.where(even, mapped, rows)


def sent(even, inner_ref, outer_ref, part):
    inner, outer = inner_ref[part, :], outer_ref[part, :]
    return jnp.where(even, inner, outer), jnp.where(even, outer, inner)


def got(even, inner_ref, outer_ref, part):
    inner, outer = inner_ref[part, :], outer_ref[part, :]
    return jnp.where(even, outer, inner), jnp.where(even, inner, outer)


def in_hbm(*values):
    return [pltpu.with_memory_space_constraint(value, pltpu.HBM) for value in values]


def folded_both(src_ref, dst_ref, turn, width):
    return jnp.concatenate(
        [folded(src_ref, turn, width), folded(dst_ref, turn, width)], axis=0
    )


def prepare_kernel(
    ids_hbm, x_hbm, rel_hbm, src_hbm, dst_hbm, inner_ref, outer_ref,
    ids_ref, x_ref, rel_ref, src_ref, dst_ref, sems,
):
    size, width = x_ref.shape
    even = is_even(GY[-1])
    copies = fetched(
        [
            (src_hbm, src_ref), (dst_hbm, dst_ref), (x_hbm, x_ref), (rel_hbm, rel_ref),
            (ids_hbm, ids_ref),
        ],
        sems,
    )
    copies[0].wait()
    copies[1].wait()
    ends = [folded_both(src_ref, dst_ref, turn, width) for turn in (2, 0)]
    put(even, ends[0], ends[1], inner_ref, outer_ref, slice(size, inner_ref.shape[0]))
    copies[2].wait()
    rows_b = x_ref[...].astype(BF16)
    copies[3].wait()
    copies[4].wait()
    mapped = map_rows(rows_b, rel_ref, ids_ref, 0)
    put(even, rows_b, mapped, inner_ref, outer_ref, slice(0, size))


def first_window_kernel(src_hbm, dst_hbm, *refs):
    *out_refs, src_ref, dst_ref, sems = refs
    near_ref = out_refs.pop()
    for copy in fetched([(src_hbm, src_ref), (dst_hbm, dst_ref)], sems):
        copy.wait()
    size = out_refs[0].shape[0]
    for turn, out_ref in enumerate(out_refs):
        ends = folded_both(src_ref, dst_ref, turn, size)
        if turn == 1:
            near_ref[...] = ends
        out_ref[...] = own_count(ends.astype(F32), size)


def relation_kernel(ids_ref, si0_ref, so0_ref, h0_ref, si1_ref, so1_ref, h1_ref, acc_ref):
    top = slice(0, h0_ref.shape[0])
    acc_ref[...] = jnp.zeros_like(acc_ref)
    rows_b, _ = sent(is_even(GY[-1]), si0_ref, so0_ref, top)
    add_relation(acc_ref, rows_b, h0_ref[...], ids_ref, 0)
    rows_b, _ = sent(is_even(GX[-1]), si1_ref, so1_ref, top)
    add_relation(acc_ref, rows_b, h1_ref[...], ids_ref, 1)


def stepped(turn, axis, ids_ref, sent_refs, got_refs, c_ref, x_ref, rel_ref, xn_ref, h_ref):
    size = x_ref.shape[0]
    even = is_even(axis)
    top, tail = slice(0, size), slice(size, sent_refs[0].shape[0])
    rows_b, mapped = sent(even, *sent_refs, top)
    target, far = got(even, *got_refs, top)
    slopes_b = slopes(dot_nt(mapped, target), c_ref[...])
    pulled = dot_nn(slopes_b, target).astype(BF16)
    h_ref[...] = pulled
    _, far_ends = got(even, *got_refs, tail)
    counts_t = far_count(far_ends.astype(F32), size)
    grad = source_grad(pulled, rel_ref, ids_ref, turn) + target_grad(rows_b, far, counts_t)
    moved = x_ref[...] - LEARN_RATE * grad
    xn_ref[...] = moved
    moved_b = moved.astype(BF16)
    return moved_b, map_rows(moved_b, rel_ref, ids_ref, turn + 1)


def first_round_kernel(
    ids_ref, si_ref, so_ref, gi_ref, go_ref, c_ref, near_ref, x_ref, rel_ref,
    xn_ref, h_ref, inner_ref, outer_ref,
):
    size = x_ref.shape[0]
    rows_b, mapped = stepped(
        0, GY[-1], ids_ref, (si_ref, so_ref), (gi_ref, go_ref), c_ref, x_ref, rel_ref, xn_ref, h_ref
    )
    put(is_even(GX[-1]), rows_b, mapped, inner_ref, outer_ref, slice(0, size))
    inner_ref[size:, :] = near_ref[...]
    outer_ref[size:, :] = near_ref[...]


def second_round_kernel(
    ids_ref, si_ref, so_ref, gi_ref, go_ref, c_ref, x_ref, rel_ref,
    xn_ref, h_ref, rows_ref, mapped_ref,
):
    rows_b, mapped = stepped(
        1, GX[-1], ids_ref, (si_ref, so_ref), (gi_ref, go_ref), c_ref, x_ref, rel_ref, xn_ref, h_ref
    )
    rows_ref[...] = rows_b
    mapped_ref[...] = mapped


def last_kernel(ids_ref, rows_ref, xq_ref, mapped_ref, c_ref, acc_in_ref, h_ref, out_ref, acc_ref):
    slopes_b = slopes(dot_nt(mapped_ref[...], xq_ref[...]), c_ref[...])
    pulled = dot_nn(slopes_b, xq_ref[...]).astype(BF16)
    h_ref[...] = pulled
    acc_ref[...] = acc_in_ref[...]
    add_relation(acc_ref, rows_ref, pulled, ids_ref, 2)
    kinds, width = acc_ref.shape[:2]
    for k in range(kinds):
        out_ref[k * width : (k + 1) * width, :] = acc_ref[k].astype(BF16)


def finish_kernel(ids_ref, rows_ref, far_ref, gi_ref, go_ref, h_ref, x_ref, rel_ref, xn_ref):
    size = x_ref.shape[0]
    ends, _ = got(is_even(GY[-1]), gi_ref, go_ref, slice(size, gi_ref.shape[0]))
    counts_t = far_count(ends.astype(F32), size)
    grad = source_grad(h_ref[...], rel_ref, ids_ref, 2)
    grad = grad + target_grad(rows_ref[...], far_ref[...], counts_t)
    xn_ref[...] = x_ref[...] - LEARN_RATE * grad


def sum_kernel(apart, in_ref, out_ref):
    share = in_ref.shape[1]
    for i in range(apart):
        acc = in_ref[i].astype(F32)
        for j in range(i + apart, in_ref.shape[0], apart):
            acc = acc + in_ref[j].astype(F32)
        total = acc.astype(BF16)
        for k in range(out_ref.shape[0]):
            out_ref[k, i * share : (i + 1) * share, :] = total


def summed_for(parts, copies, apart):
    count, share, width = parts.shape
    out = jax.ShapeDtypeStruct((copies, apart * share, width), BF16)
    kernel = functools.partial(sum_kernel, apart)
    return call(kernel, [out], [VMEM], count * share * width)(parts)[0]


def reduce_everywhere(payload):
    rows, width = payload.shape
    near = lax.axis_size(NEAR)
    part = lax.all_to_all(payload.reshape(near, rows // near, width), NEAR, 0, 0)
    part = summed_for(part, lax.axis_size(DEPTH), 1)
    part = lax.all_to_all(part, DEPTH, 0, 0)
    part = summed_for(part, lax.axis_size(PLANE), lax.axis_size(DEPTH[-1]))
    part = lax.all_to_all(part, PLANE, 0, 0)
    return part.reshape(rows, width).astype(F32)


def training(entity, relations, rel_ids, edge_src, edge_dst):
    rows, width = entity.shape
    kinds = relations.shape[0]
    turns, edges = edge_src.shape
    square = 2 * rows * rows * width
    counting = 2 * rows * rows * edges
    ends_rows = 2 * edges // width
    f_rows = jax.ShapeDtypeStruct((rows, width), F32)
    b_rows = jax.ShapeDtypeStruct((rows, width), BF16)
    b_pay = jax.ShapeDtypeStruct((rows + ends_rows, width), BF16)
    b_ends = jax.ShapeDtypeStruct((ends_rows, width), BF16)
    f_count = jax.ShapeDtypeStruct((rows, rows), F32)
    f_rel = jax.ShapeDtypeStruct(relations.shape, F32)
    b_rel = jax.ShapeDtypeStruct((kinds * width, width), BF16)
    edge_scratch = [pltpu.VMEM(edge_src.shape, jnp.int32)] * 2
    buckets = ((GY, 1), (GX, 1), (GY, -1))

    def exchanged(turn, inner, outer):
        axes = buckets[turn][0]
        outer_got = swapped_outer(outer, axes)
        inner_got = swapped_inner(inner, axes)
        return inner_got, outer_got

    sent0 = call(
        prepare_kernel, [b_pay, b_pay], [HBM] * 5, square,
        scratch=[pltpu.SMEM(rel_ids.shape, jnp.int32), pltpu.VMEM(entity.shape, F32)]
        + [pltpu.VMEM(relations.shape, F32)] + edge_scratch + [pltpu.SemaphoreType.DMA((5,))],
    )(*in_hbm(rel_ids, entity, relations, edge_src, edge_dst))

    got0 = exchanged(0, *sent0)
    c0, c1, c2, ends1 = call(
        first_window_kernel, [f_count] * turns + [b_ends], [HBM] * 2, turns * counting,
        scratch=edge_scratch + [pltpu.SemaphoreType.DMA((2,))],
    )(*in_hbm(edge_src, edge_dst))
    x1, h0, *sent1 = call(
        first_round_kernel, [f_rows, b_rows, b_pay, b_pay],
        [SMEM] + [VMEM] * 8, 7 * square + counting,
    )(rel_ids, *sent0, *got0, c0, ends1, entity, relations)

    got1 = exchanged(1, *sent1)
    x2, h1, rows2, mapped2 = call(
        second_round_kernel, [f_rows, b_rows, b_rows, b_rows],
        [SMEM] + [VMEM] * 7, 7 * square + counting,
    )(rel_ids, *sent1, *got1, c1, x1, relations)

    axes, offset = buckets[2]
    xq = shifted(rows2, axes, offset)
    far = shifted(mapped2, axes, -offset)
    acc = call(
        relation_kernel, [f_rel], [SMEM] + [VMEM] * 6, 2 * square,
    )(rel_ids, *sent0, h0, *sent1, h1)[0]
    h2, payload, _ = call(
        last_kernel, [b_rows, b_rel, f_rel],
        [SMEM] + [VMEM] * 5, 3 * square, aliases={5: 2},
    )(rel_ids, rows2, xq, mapped2, c2, acc)
    x3 = call(
        finish_kernel, [f_rows], [SMEM] + [VMEM] * 7, 3 * square + counting,
    )(rel_ids, rows2, far, *got0, h2, x2, relations)[0]

    summed = reduce_everywhere(payload)
    divisor = math.sqrt(turns * lax.axis_size(AXES))
    return x3, (summed / divisor).reshape(relations.shape)


def solution(mesh):
    inner = Mesh(mesh.devices.reshape(2, 4, 2, 2, 8, 2), AXES)
    return jax.shard_map(
        training,
        mesh=inner,
        in_specs=(P(AXES, None), P(), P(None, AXES), P(None, AXES), P(None, AXES)),
        out_specs=(P(AXES, None), P()),
        check_vma=False,
    )
```

```python
import functools
import math

import jax
import jax.numpy as jnp
from jax import lax
from jax.experimental import pallas as pl
from jax.experimental.pallas import tpu as pltpu
from jax.sharding import Mesh
from jax.sharding import PartitionSpec as P


AXES = ("xh", "y", "c", "xl", "zh", "zl")
GX = ("xh", "y", "c")
GY = ("xl", "zh", "zl")
PLANE = ("xh", "y", "c", "xl")
NEAR = PLANE + ("zl",)
DEPTH = ("zh", "zl")
LEARN_RATE = 0.5
GROUPS = 4
VMEM = pl.BlockSpec(memory_space=pltpu.VMEM)
HBM = pl.BlockSpec(memory_space=pltpu.HBM)
F32 = jnp.float32
BF16 = jnp.bfloat16


def shifted(value, axes, steps):
    count = lax.axis_size(axes)
    pairs = [(source, (source + steps) % count) for source in range(count)]
    return lax.ppermute(value, axes, pairs)


def swapped_inner(value, axes):
    return lax.ppermute(value, axes, [(i, i ^ 1) for i in range(lax.axis_size(axes))])


def swapped_outer(value, axes):
    count = lax.axis_size(axes)
    pairs = [(i, (i + (1 if i % 2 else -1)) % count) for i in range(count)]
    return lax.ppermute(value, axes, pairs)


def dot_nn(left, right):
    return lax.dot_general(left, right, (((1,), (0,)), ((), ())), preferred_element_type=F32)


def dot_nt(left, right):
    return lax.dot_general(left, right, (((1,), (1,)), ((), ())), preferred_element_type=F32)


def dot_tn(left, right):
    return lax.dot_general(left, right, (((0,), (0,)), ((), ())), preferred_element_type=F32)


def call(kernel, outs, in_specs, flops, aliases=None, scratch=()):
    moved = sum(math.prod(o.shape) * o.dtype.itemsize for o in outs)
    return pl.pallas_call(
        kernel,
        out_shape=tuple(outs),
        in_specs=list(in_specs),
        out_specs=tuple(VMEM for _ in outs),
        scratch_shapes=list(scratch),
        input_output_aliases=aliases or {},
        compiler_params=pltpu.CompilerParams(vmem_limit_bytes=16 * 2**20),
        cost_estimate=pl.CostEstimate(
            flops=flops, bytes_accessed=4 * moved, transcendentals=0
        ),
    )


def map_rows(rows_b, chosen):
    size = rows_b.shape[0] // GROUPS
    parts = [
        dot_nn(rows_b[g * size : (g + 1) * size, :], chosen(g)).astype(BF16) for g in range(GROUPS)
    ]
    return jnp.concatenate(parts, axis=0)


def chosen_of(wsel_ref, turn):
    return lambda g: wsel_ref[turn * GROUPS + g]


def folded(edge_ref, turn, width):
    pieces = edge_ref.shape[1] // width
    rows = [edge_ref[turn : turn + 1, i * width : (i + 1) * width] for i in range(pieces)]
    return jnp.concatenate(rows, axis=0).astype(F32).astype(BF16)


def one_hot(row, size):
    count = row.shape[1]
    wide = jnp.broadcast_to(row.astype(F32), (16, count)).astype(BF16)
    index = lax.broadcasted_iota(jnp.int32, (16, count), 0).astype(F32).astype(BF16)
    one = jnp.ones((16, count), BF16)
    zero = jnp.zeros((16, count), BF16)
    parts = [jnp.where(wide == index + BF16(16 * i), one, zero) for i in range(size // 16)]
    return jnp.concatenate(parts, axis=0).astype(jnp.float8_e4m3fn)


def counted(row_of, col_of, pieces, size):
    acc = jnp.zeros((size, size), F32)
    for i in range(pieces):
        acc = acc + dot_nt(one_hot(row_of(i), size), one_hot(col_of(i), size))
    return acc


def own_count(ends, size):
    pieces = ends.shape[0] // 2
    return counted(
        lambda i: ends[i : i + 1, :], lambda i: ends[pieces + i : pieces + i + 1, :], pieces, size
    )


def far_count(ends, size):
    pieces = ends.shape[0] // 2
    return counted(
        lambda i: ends[pieces + i : pieces + i + 1, :], lambda i: ends[i : i + 1, :], pieces, size
    )


def slopes(scores, counts):
    scaling = 1.0 / math.sqrt(scores.shape[0])
    return ((jax.nn.sigmoid(scores) - counts) * scaling).astype(BF16)


def source_grad(pulled_b, chosen):
    size = pulled_b.shape[0] // GROUPS
    parts = [dot_nt(pulled_b[g * size : (g + 1) * size, :], chosen(g)) for g in range(GROUPS)]
    return jnp.concatenate(parts, axis=0)


def target_grad(rows_b, mapped, counts_t):
    slopes_t = slopes(dot_nt(rows_b, mapped), counts_t)
    return dot_nn(slopes_t, mapped).astype(BF16).astype(F32)


def add_relation(acc_ref, rows_b, pulled_b, kind_of_row):
    kinds, width = acc_ref.shape[:2]
    zero = jnp.zeros_like(pulled_b)
    apart = [jnp.where(kind_of_row == BF16(k), pulled_b, zero) for k in range(kinds)]
    added = dot_tn(rows_b, jnp.concatenate(apart, axis=1))
    for k in range(kinds):
        acc_ref[k] = acc_ref[k] + added[:, k * width : (k + 1) * width]


def fetched(pairs, sems):
    copies = [
        pltpu.make_async_copy(source, target, sems.at[i])
        for i, (source, target) in enumerate(pairs)
    ]
    for copy in copies:
        copy.start()
    return copies


def is_even(axis):
    return lax.axis_index(axis) == 0


def put(even, rows, mapped, inner_ref, outer_ref, part):
    inner_ref[part, :] = jnp.where(even, rows, mapped)
    outer_ref[part, :] = jnp.where(even, mapped, rows)


def sent(even, inner_ref, outer_ref, part):
    inner, outer = inner_ref[part, :], outer_ref[part, :]
    return jnp.where(even, inner, outer), jnp.where(even, outer, inner)


def got(even, inner_ref, outer_ref, part):
    inner, outer = inner_ref[part, :], outer_ref[part, :]
    return jnp.where(even, outer, inner), jnp.where(even, inner, outer)


def in_hbm(*values):
    return [pltpu.with_memory_space_constraint(value, pltpu.HBM) for value in values]


def folded_both(src_ref, dst_ref, turn, width):
    return jnp.concatenate(
        [folded(src_ref, turn, width), folded(dst_ref, turn, width)], axis=0
    )


def prepare_kernel(
    ids_hbm, x_hbm, rel_hbm, src_hbm, dst_hbm, inner_ref, outer_ref,
    ids_ref, x_ref, rel_ref, src_ref, dst_ref, sems,
):
    size, width = x_ref.shape
    even = is_even(GY[-1])
    copies = fetched(
        [
            (src_hbm, src_ref), (dst_hbm, dst_ref), (x_hbm, x_ref), (rel_hbm, rel_ref),
            (ids_hbm, ids_ref),
        ],
        sems,
    )
    copies[0].wait()
    copies[1].wait()
    ends = [folded_both(src_ref, dst_ref, turn, width) for turn in (2, 0)]
    put(even, ends[0], ends[1], inner_ref, outer_ref, slice(size, inner_ref.shape[0]))
    copies[2].wait()
    rows_b = x_ref[...].astype(BF16)
    copies[3].wait()
    copies[4].wait()
    mapped = map_rows(rows_b, lambda g: rel_ref[ids_ref[0, g]].astype(BF16))
    put(even, rows_b, mapped, inner_ref, outer_ref, slice(0, size))


def first_window_kernel(
    ids_hbm, rel_hbm, src_hbm, dst_hbm, c0_ref, c1_ref, c2_ref, near_ref, wsel_ref, kinds_ref,
    ids_ref, rel_ref, src_ref, dst_ref, sems,
):
    copies = fetched(
        [(src_hbm, src_ref), (dst_hbm, dst_ref), (ids_hbm, ids_ref), (rel_hbm, rel_ref)], sems
    )
    copies[0].wait()
    copies[1].wait()
    size = c0_ref.shape[0]
    for turn, out_ref in enumerate((c0_ref, c1_ref, c2_ref)):
        ends = folded_both(src_ref, dst_ref, turn, size)
        if turn == 1:
            near_ref[...] = ends
        out_ref[...] = own_count(ends.astype(F32), size)
    copies[2].wait()
    copies[3].wait()
    group_rows = size // GROUPS
    for turn in range(ids_ref.shape[0]):
        for g in range(GROUPS):
            kind = ids_ref[turn, g]
            wsel_ref[turn * GROUPS + g] = rel_ref[kind].astype(BF16)
            whole = jnp.full((group_rows, kinds_ref.shape[2]), kind, jnp.int32)
            kinds_ref[turn, g * group_rows : (g + 1) * group_rows, :] = whole.astype(F32).astype(BF16)


def relation_kernel(kinds_ref, si0_ref, so0_ref, h0_ref, si1_ref, so1_ref, h1_ref, acc_ref):
    top = slice(0, h0_ref.shape[0])
    acc_ref[...] = jnp.zeros_like(acc_ref)
    rows_b, _ = sent(is_even(GY[-1]), si0_ref, so0_ref, top)
    add_relation(acc_ref, rows_b, h0_ref[...], kinds_ref[0])
    rows_b, _ = sent(is_even(GX[-1]), si1_ref, so1_ref, top)
    add_relation(acc_ref, rows_b, h1_ref[...], kinds_ref[1])


def stepped(turn, axis, sent_refs, got_refs, c_ref, x_ref, wsel_ref, xn_ref, h_ref):
    size = x_ref.shape[0]
    even = is_even(axis)
    top, tail = slice(0, size), slice(size, sent_refs[0].shape[0])
    rows_b, mapped = sent(even, *sent_refs, top)
    target, far = got(even, *got_refs, top)
    slopes_b = slopes(dot_nt(mapped, target), c_ref[...])
    pulled = dot_nn(slopes_b, target).astype(BF16)
    h_ref[...] = pulled
    _, far_ends = got(even, *got_refs, tail)
    counts_t = far_count(far_ends.astype(F32), size)
    grad = source_grad(pulled, chosen_of(wsel_ref, turn)) + target_grad(rows_b, far, counts_t)
    moved = x_ref[...] - LEARN_RATE * grad
    xn_ref[...] = moved
    moved_b = moved.astype(BF16)
    return moved_b, map_rows(moved_b, chosen_of(wsel_ref, turn + 1))


def first_round_kernel(
    si_ref, so_ref, gi_ref, go_ref, c_ref, near_ref, x_ref, wsel_ref,
    xn_ref, h_ref, inner_ref, outer_ref,
):
    size = x_ref.shape[0]
    rows_b, mapped = stepped(
        0, GY[-1], (si_ref, so_ref), (gi_ref, go_ref), c_ref, x_ref, wsel_ref, xn_ref, h_ref
    )
    put(is_even(GX[-1]), rows_b, mapped, inner_ref, outer_ref, slice(0, size))
    inner_ref[size:, :] = near_ref[...]
    outer_ref[size:, :] = near_ref[...]


def second_round_kernel(
    si_ref, so_ref, gi_ref, go_ref, c_ref, x_ref, wsel_ref,
    xn_ref, h_ref, rows_ref, mapped_ref,
):
    rows_b, mapped = stepped(
        1, GX[-1], (si_ref, so_ref), (gi_ref, go_ref), c_ref, x_ref, wsel_ref, xn_ref, h_ref
    )
    rows_ref[...] = rows_b
    mapped_ref[...] = mapped


def last_kernel(kinds_ref, rows_ref, xq_ref, mapped_ref, c_ref, acc_in_ref, h_ref, out_ref, acc_ref):
    slopes_b = slopes(dot_nt(mapped_ref[...], xq_ref[...]), c_ref[...])
    pulled = dot_nn(slopes_b, xq_ref[...]).astype(BF16)
    h_ref[...] = pulled
    acc_ref[...] = acc_in_ref[...]
    add_relation(acc_ref, rows_ref[...], pulled, kinds_ref[2])
    kinds, width = acc_ref.shape[:2]
    for k in range(kinds):
        out_ref[k * width : (k + 1) * width, :] = acc_ref[k].astype(BF16)


def finish_kernel(rows_ref, far_ref, gi_ref, go_ref, h_ref, x_ref, wsel_ref, xn_ref):
    size = x_ref.shape[0]
    ends, _ = got(is_even(GY[-1]), gi_ref, go_ref, slice(size, gi_ref.shape[0]))
    counts_t = far_count(ends.astype(F32), size)
    grad = source_grad(h_ref[...], chosen_of(wsel_ref, 2))
    grad = grad + target_grad(rows_ref[...], far_ref[...], counts_t)
    xn_ref[...] = x_ref[...] - LEARN_RATE * grad


def sum_kernel(apart, in_ref, out_ref):
    share = in_ref.shape[1]
    for i in range(apart):
        acc = in_ref[i].astype(F32)
        for j in range(i + apart, in_ref.shape[0], apart):
            acc = acc + in_ref[j].astype(F32)
        total = acc.astype(BF16)
        for k in range(out_ref.shape[0]):
            out_ref[k, i * share : (i + 1) * share, :] = total


def summed_for(parts, copies, apart):
    count, share, width = parts.shape
    out = jax.ShapeDtypeStruct((copies, apart * share, width), BF16)
    kernel = functools.partial(sum_kernel, apart)
    return call(kernel, [out], [VMEM], count * share * width)(parts)[0]


def reduce_everywhere(payload):
    rows, width = payload.shape
    near = lax.axis_size(NEAR)
    part = lax.all_to_all(payload.reshape(near, rows // near, width), NEAR, 0, 0)
    part = summed_for(part, lax.axis_size(DEPTH), 1)
    part = lax.all_to_all(part, DEPTH, 0, 0)
    part = summed_for(part, lax.axis_size(PLANE), lax.axis_size(DEPTH[-1]))
    part = lax.all_to_all(part, PLANE, 0, 0)
    return part.reshape(rows, width).astype(F32)


def training(entity, relations, rel_ids, edge_src, edge_dst):
    rows, width = entity.shape
    kinds = relations.shape[0]
    turns, edges = edge_src.shape
    square = 2 * rows * rows * width
    counting = 2 * rows * rows * edges
    ends_rows = 2 * edges // width
    f_rows = jax.ShapeDtypeStruct((rows, width), F32)
    b_rows = jax.ShapeDtypeStruct((rows, width), BF16)
    b_pay = jax.ShapeDtypeStruct((rows + ends_rows, width), BF16)
    b_ends = jax.ShapeDtypeStruct((ends_rows, width), BF16)
    f_count = jax.ShapeDtypeStruct((rows, rows), F32)
    f_rel = jax.ShapeDtypeStruct(relations.shape, F32)
    b_rel = jax.ShapeDtypeStruct((kinds * width, width), BF16)
    first_scratch = [
        pltpu.SMEM(rel_ids.shape, jnp.int32), pltpu.VMEM(entity.shape, F32),
        pltpu.VMEM(relations.shape, F32),
    ] + [pltpu.VMEM(edge_src.shape, jnp.int32)] * 2
    buckets = ((GY, 1), (GX, 1), (GY, -1))

    def exchanged(turn, inner, outer):
        axes = buckets[turn][0]
        outer_got = swapped_outer(outer, axes)
        inner_got = swapped_inner(inner, axes)
        return inner_got, outer_got

    sent0 = call(
        prepare_kernel, [b_pay, b_pay], [HBM] * 5, square,
        scratch=first_scratch + [pltpu.SemaphoreType.DMA((5,))],
    )(*in_hbm(rel_ids, entity, relations, edge_src, edge_dst))

    got0 = exchanged(0, *sent0)
    b_wsel = jax.ShapeDtypeStruct((turns * GROUPS, width, width), BF16)
    b_kinds = jax.ShapeDtypeStruct((turns, rows, width), BF16)
    c0, c1, c2, ends1, wsel, of_row = call(
        first_window_kernel, [f_count] * turns + [b_ends, b_wsel, b_kinds], [HBM] * 4,
        turns * counting,
        scratch=first_scratch[:1] + first_scratch[2:] + [pltpu.SemaphoreType.DMA((4,))],
    )(*in_hbm(rel_ids, relations, edge_src, edge_dst))
    x1, h0, *sent1 = call(
        first_round_kernel, [f_rows, b_rows, b_pay, b_pay],
        [VMEM] * 8, 7 * square + counting,
    )(*sent0, *got0, c0, ends1, entity, wsel)

    got1 = exchanged(1, *sent1)
    x2, h1, rows2, mapped2 = call(
        second_round_kernel, [f_rows, b_rows, b_rows, b_rows],
        [VMEM] * 7, 7 * square + counting,
    )(*sent1, *got1, c1, x1, wsel)

    axes, offset = buckets[2]
    xq = shifted(rows2, axes, offset)
    far = shifted(mapped2, axes, -offset)
    acc = call(relation_kernel, [f_rel], [VMEM] * 7, 2 * square)(of_row, *sent0, h0, *sent1, h1)[0]
    h2, payload, _ = call(
        last_kernel, [b_rows, b_rel, f_rel],
        [VMEM] * 6, 3 * square, aliases={5: 2},
    )(of_row, rows2, xq, mapped2, c2, acc)
    x3 = call(
        finish_kernel, [f_rows], [VMEM] * 7, 3 * square + counting,
    )(rows2, far, *got0, h2, x2, wsel)[0]

    summed = reduce_everywhere(payload)
    divisor = math.sqrt(turns * lax.axis_size(AXES))
    return x3, (summed / divisor).reshape(relations.shape)


def solution(mesh):
    inner = Mesh(mesh.devices.reshape(2, 4, 2, 2, 8, 2), AXES)
    return jax.shard_map(
        training,
        mesh=inner,
        in_specs=(P(AXES, None), P(), P(None, AXES), P(None, AXES), P(None, AXES)),
        out_specs=(P(AXES, None), P()),
        check_vma=False,
    )
```

```python
import functools
import math

import jax
import jax.numpy as jnp
from jax import lax
from jax.experimental import pallas as pl
from jax.experimental.pallas import tpu as pltpu
from jax.sharding import Mesh
from jax.sharding import PartitionSpec as P


AXES = ("xh", "y", "c", "xl", "zh", "zl")
CORE = "c"
GX = ("xh", "y", "c")
GY = ("xl", "zh", "zl")
PLANE = ("xh", "y", "c", "xl")
NEAR = PLANE + ("zl",)
DEPTH = ("zh", "zl")
LEARN_RATE = 0.5
GROUPS = 4
VMEM = pl.BlockSpec(memory_space=pltpu.VMEM)
HBM = pl.BlockSpec(memory_space=pltpu.HBM)
F32 = jnp.float32
BF16 = jnp.bfloat16


def shifted(value, axes, steps):
    count = lax.axis_size(axes)
    pairs = [(source, (source + steps) % count) for source in range(count)]
    return lax.ppermute(value, axes, pairs)


def inner_partner(i, count):
    return i ^ 1


def outer_partner(i, count):
    return (i + (1 if i % 2 else -1)) % count


def swapped(value, axes, partner):
    count = lax.axis_size(axes)
    return lax.ppermute(value, axes, [(i, partner(i, count)) for i in range(count)])


def swapped_by_core(value, axes, partners):
    count = lax.axis_size(axes)
    pairs = [
        (core * count + i, core * count + partners[core](i, count))
        for core in range(2) for i in range(count)
    ]
    return lax.ppermute(value, (CORE,) + axes, pairs)


def dot_nn(left, right):
    return lax.dot_general(left, right, (((1,), (0,)), ((), ())), preferred_element_type=F32)


def dot_nt(left, right):
    return lax.dot_general(left, right, (((1,), (1,)), ((), ())), preferred_element_type=F32)


def dot_tn(left, right):
    return lax.dot_general(left, right, (((0,), (0,)), ((), ())), preferred_element_type=F32)


def call(kernel, outs, in_specs, flops, aliases=None, scratch=()):
    moved = sum(math.prod(o.shape) * o.dtype.itemsize for o in outs)
    return pl.pallas_call(
        kernel,
        out_shape=tuple(outs),
        in_specs=list(in_specs),
        out_specs=tuple(VMEM for _ in outs),
        scratch_shapes=list(scratch),
        input_output_aliases=aliases or {},
        compiler_params=pltpu.CompilerParams(vmem_limit_bytes=16 * 2**20),
        cost_estimate=pl.CostEstimate(
            flops=flops, bytes_accessed=4 * moved, transcendentals=0
        ),
    )


def map_rows(rows_b, chosen):
    size = rows_b.shape[0] // GROUPS
    parts = [
        dot_nn(rows_b[g * size : (g + 1) * size, :], chosen(g)).astype(BF16) for g in range(GROUPS)
    ]
    return jnp.concatenate(parts, axis=0)


def chosen_of(wsel_ref, turn):
    return lambda g: wsel_ref[turn * GROUPS + g]


def folded(edge_ref, turn, width):
    pieces = edge_ref.shape[1] // width
    rows = [edge_ref[turn : turn + 1, i * width : (i + 1) * width] for i in range(pieces)]
    return jnp.concatenate(rows, axis=0).astype(F32).astype(BF16)


def one_hot(row, size):
    count = row.shape[1]
    wide = jnp.broadcast_to(row.astype(F32), (16, count)).astype(BF16)
    index = lax.broadcasted_iota(jnp.int32, (16, count), 0).astype(F32).astype(BF16)
    one = jnp.ones((16, count), BF16)
    zero = jnp.zeros((16, count), BF16)
    parts = [jnp.where(wide == index + BF16(16 * i), one, zero) for i in range(size // 16)]
    return jnp.concatenate(parts, axis=0).astype(jnp.float8_e4m3fn)


def counted(row_of, col_of, pieces, size):
    acc = jnp.zeros((size, size), F32)
    for i in range(pieces):
        acc = acc + dot_nt(one_hot(row_of(i), size), one_hot(col_of(i), size))
    return acc


def own_count(ends, size):
    pieces = ends.shape[0] // 2
    return counted(
        lambda i: ends[i : i + 1, :], lambda i: ends[pieces + i : pieces + i + 1, :], pieces, size
    )


def far_count(ends, size):
    pieces = ends.shape[0] // 2
    return counted(
        lambda i: ends[pieces + i : pieces + i + 1, :], lambda i: ends[i : i + 1, :], pieces, size
    )


def slopes(scores, counts):
    scaling = 1.0 / math.sqrt(scores.shape[0])
    return ((jax.nn.sigmoid(scores) - counts) * scaling).astype(BF16)


def source_grad(pulled_b, chosen):
    size = pulled_b.shape[0] // GROUPS
    parts = [dot_nt(pulled_b[g * size : (g + 1) * size, :], chosen(g)) for g in range(GROUPS)]
    return jnp.concatenate(parts, axis=0)


def target_grad(rows_b, mapped, counts_t):
    slopes_t = slopes(dot_nt(rows_b, mapped), counts_t)
    return dot_nn(slopes_t, mapped).astype(BF16).astype(F32)


def add_relation(acc_ref, rows_b, pulled_b, kind_of_row):
    kinds, width = acc_ref.shape[:2]
    zero = jnp.zeros_like(pulled_b)
    apart = [jnp.where(kind_of_row == BF16(k), pulled_b, zero) for k in range(kinds)]
    added = dot_tn(rows_b, jnp.concatenate(apart, axis=1))
    for k in range(kinds):
        acc_ref[k] = acc_ref[k] + added[:, k * width : (k + 1) * width]


def fetched(pairs, sems):
    copies = [
        pltpu.make_async_copy(source, target, sems.at[i])
        for i, (source, target) in enumerate(pairs)
    ]
    for copy in copies:
        copy.start()
    return copies


def is_even(turn):
    core = lax.axis_index(CORE)
    return core == (0 if turn else lax.axis_index(GY[-1]))


def put(even, rows, mapped, inner_ref, outer_ref, part):
    inner_ref[part, :] = jnp.where(even, rows, mapped)
    outer_ref[part, :] = jnp.where(even, mapped, rows)


def sent(even, inner_ref, outer_ref, part):
    inner, outer = inner_ref[part, :], outer_ref[part, :]
    return jnp.where(even, inner, outer), jnp.where(even, outer, inner)


def got(even, inner_ref, outer_ref, part):
    inner, outer = inner_ref[part, :], outer_ref[part, :]
    return jnp.where(even, outer, inner), jnp.where(even, inner, outer)


def in_hbm(*values):
    return [pltpu.with_memory_space_constraint(value, pltpu.HBM) for value in values]


def folded_both(src_ref, dst_ref, turn, width):
    return jnp.concatenate(
        [folded(src_ref, turn, width), folded(dst_ref, turn, width)], axis=0
    )


def prepare_kernel(
    ids_hbm, x_hbm, rel_hbm, src_hbm, dst_hbm, inner_ref, outer_ref,
    ids_ref, x_ref, rel_ref, src_ref, dst_ref, sems,
):
    size, width = x_ref.shape
    even = is_even(0)
    copies = fetched(
        [
            (src_hbm, src_ref), (dst_hbm, dst_ref), (x_hbm, x_ref), (rel_hbm, rel_ref),
            (ids_hbm, ids_ref),
        ],
        sems,
    )
    copies[0].wait()
    copies[1].wait()
    ends = [folded_both(src_ref, dst_ref, turn, width) for turn in (2, 0)]
    put(even, ends[0], ends[1], inner_ref, outer_ref, slice(size, inner_ref.shape[0]))
    copies[2].wait()
    rows_b = x_ref[...].astype(BF16)
    copies[3].wait()
    copies[4].wait()
    mapped = map_rows(rows_b, lambda g: rel_ref[ids_ref[0, g]].astype(BF16))
    put(even, rows_b, mapped, inner_ref, outer_ref, slice(0, size))


def first_window_kernel(
    ids_hbm, rel_hbm, src_hbm, dst_hbm, c0_ref, c1_ref, c2_ref, near_ref, wsel_ref, kinds_ref,
    ids_ref, rel_ref, src_ref, dst_ref, sems,
):
    copies = fetched(
        [(src_hbm, src_ref), (dst_hbm, dst_ref), (ids_hbm, ids_ref), (rel_hbm, rel_ref)], sems
    )
    copies[0].wait()
    copies[1].wait()
    size = c0_ref.shape[0]
    for turn, out_ref in enumerate((c0_ref, c1_ref, c2_ref)):
        ends = folded_both(src_ref, dst_ref, turn, size)
        if turn == 1:
            near_ref[...] = ends
        out_ref[...] = own_count(ends.astype(F32), size)
    copies[2].wait()
    copies[3].wait()
    group_rows = size // GROUPS
    for turn in range(ids_ref.shape[0]):
        for g in range(GROUPS):
            kind = ids_ref[turn, g]
            wsel_ref[turn * GROUPS + g] = rel_ref[kind].astype(BF16)
            whole = jnp.full((group_rows, kinds_ref.shape[2]), kind, jnp.int32)
            kinds_ref[turn, g * group_rows : (g + 1) * group_rows, :] = whole.astype(F32).astype(BF16)


def relation_kernel(kinds_ref, si0_ref, so0_ref, h0_ref, si1_ref, so1_ref, h1_ref, acc_ref):
    top = slice(0, h0_ref.shape[0])
    acc_ref[...] = jnp.zeros_like(acc_ref)
    rows_b, _ = sent(is_even(0), si0_ref, so0_ref, top)
    add_relation(acc_ref, rows_b, h0_ref[...], kinds_ref[0])
    rows_b, _ = sent(is_even(1), si1_ref, so1_ref, top)
    add_relation(acc_ref, rows_b, h1_ref[...], kinds_ref[1])


def stepped(turn, sent_refs, got_refs, c_ref, x_ref, wsel_ref, xn_ref, h_ref):
    size = x_ref.shape[0]
    even = is_even(turn)
    top, tail = slice(0, size), slice(size, sent_refs[0].shape[0])
    rows_b, mapped = sent(even, *sent_refs, top)
    target, far = got(even, *got_refs, top)
    slopes_b = slopes(dot_nt(mapped, target), c_ref[...])
    pulled = dot_nn(slopes_b, target).astype(BF16)
    h_ref[...] = pulled
    _, far_ends = got(even, *got_refs, tail)
    counts_t = far_count(far_ends.astype(F32), size)
    grad = source_grad(pulled, chosen_of(wsel_ref, turn)) + target_grad(rows_b, far, counts_t)
    moved = x_ref[...] - LEARN_RATE * grad
    xn_ref[...] = moved
    moved_b = moved.astype(BF16)
    return moved_b, map_rows(moved_b, chosen_of(wsel_ref, turn + 1))


def first_round_kernel(
    si_ref, so_ref, gi_ref, go_ref, c_ref, near_ref, x_ref, wsel_ref,
    xn_ref, h_ref, inner_ref, outer_ref,
):
    size = x_ref.shape[0]
    rows_b, mapped = stepped(
        0, (si_ref, so_ref), (gi_ref, go_ref), c_ref, x_ref, wsel_ref, xn_ref, h_ref
    )
    put(is_even(1), rows_b, mapped, inner_ref, outer_ref, slice(0, size))
    inner_ref[size:, :] = near_ref[...]
    outer_ref[size:, :] = near_ref[...]


def second_round_kernel(
    si_ref, so_ref, gi_ref, go_ref, c_ref, x_ref, wsel_ref,
    xn_ref, h_ref, rows_ref, mapped_ref,
):
    rows_b, mapped = stepped(
        1, (si_ref, so_ref), (gi_ref, go_ref), c_ref, x_ref, wsel_ref, xn_ref, h_ref
    )
    rows_ref[...] = rows_b
    mapped_ref[...] = mapped


def last_kernel(kinds_ref, rows_ref, xq_ref, mapped_ref, c_ref, acc_in_ref, h_ref, out_ref, acc_ref):
    slopes_b = slopes(dot_nt(mapped_ref[...], xq_ref[...]), c_ref[...])
    pulled = dot_nn(slopes_b, xq_ref[...]).astype(BF16)
    h_ref[...] = pulled
    acc_ref[...] = acc_in_ref[...]
    add_relation(acc_ref, rows_ref[...], pulled, kinds_ref[2])
    kinds, width = acc_ref.shape[:2]
    for k in range(kinds):
        out_ref[k * width : (k + 1) * width, :] = acc_ref[k].astype(BF16)


def finish_kernel(rows_ref, far_ref, gi_ref, go_ref, h_ref, x_ref, wsel_ref, xn_ref):
    size = x_ref.shape[0]
    ends, _ = got(is_even(0), gi_ref, go_ref, slice(size, gi_ref.shape[0]))
    counts_t = far_count(ends.astype(F32), size)
    grad = source_grad(h_ref[...], chosen_of(wsel_ref, 2))
    grad = grad + target_grad(rows_ref[...], far_ref[...], counts_t)
    xn_ref[...] = x_ref[...] - LEARN_RATE * grad


def sum_kernel(apart, in_ref, out_ref):
    share = in_ref.shape[1]
    for i in range(apart):
        acc = in_ref[i].astype(F32)
        for j in range(i + apart, in_ref.shape[0], apart):
            acc = acc + in_ref[j].astype(F32)
        total = acc.astype(BF16)
        for k in range(out_ref.shape[0]):
            out_ref[k, i * share : (i + 1) * share, :] = total


def summed_for(parts, copies, apart):
    count, share, width = parts.shape
    out = jax.ShapeDtypeStruct((copies, apart * share, width), BF16)
    kernel = functools.partial(sum_kernel, apart)
    return call(kernel, [out], [VMEM], count * share * width)(parts)[0]


def reduce_everywhere(payload):
    rows, width = payload.shape
    near = lax.axis_size(NEAR)
    part = lax.all_to_all(payload.reshape(near, rows // near, width), NEAR, 0, 0)
    part = summed_for(part, lax.axis_size(DEPTH), 1)
    part = lax.all_to_all(part, DEPTH, 0, 0)
    part = summed_for(part, lax.axis_size(PLANE), lax.axis_size(DEPTH[-1]))
    part = lax.all_to_all(part, PLANE, 0, 0)
    return part.reshape(rows, width).astype(F32)


def training(entity, relations, rel_ids, edge_src, edge_dst):
    rows, width = entity.shape
    kinds = relations.shape[0]
    turns, edges = edge_src.shape
    square = 2 * rows * rows * width
    counting = 2 * rows * rows * edges
    ends_rows = 2 * edges // width
    f_rows = jax.ShapeDtypeStruct((rows, width), F32)
    b_rows = jax.ShapeDtypeStruct((rows, width), BF16)
    b_pay = jax.ShapeDtypeStruct((rows + ends_rows, width), BF16)
    b_ends = jax.ShapeDtypeStruct((ends_rows, width), BF16)
    f_count = jax.ShapeDtypeStruct((rows, rows), F32)
    f_rel = jax.ShapeDtypeStruct(relations.shape, F32)
    b_rel = jax.ShapeDtypeStruct((kinds * width, width), BF16)
    first_scratch = [
        pltpu.SMEM(rel_ids.shape, jnp.int32), pltpu.VMEM(entity.shape, F32),
        pltpu.VMEM(relations.shape, F32),
    ] + [pltpu.VMEM(edge_src.shape, jnp.int32)] * 2
    buckets = ((GY, 1), (GX, 1), (GY, -1))

    def exchanged(turn, inner, outer):
        axes = buckets[turn][0]
        partners = (inner_partner, outer_partner)
        if CORE in axes:
            outer_got = swapped(outer, axes, outer_partner)
        else:
            outer_got = swapped_by_core(outer, axes, partners[::-1])
        if CORE in axes:
            inner_got = swapped(inner, axes, inner_partner)
        else:
            inner_got = swapped_by_core(inner, axes, partners)
        return inner_got, outer_got

    sent0 = call(
        prepare_kernel, [b_pay, b_pay], [HBM] * 5, square,
        scratch=first_scratch + [pltpu.SemaphoreType.DMA((5,))],
    )(*in_hbm(rel_ids, entity, relations, edge_src, edge_dst))

    got0 = exchanged(0, *sent0)
    b_wsel = jax.ShapeDtypeStruct((turns * GROUPS, width, width), BF16)
    b_kinds = jax.ShapeDtypeStruct((turns, rows, width), BF16)
    c0, c1, c2, ends1, wsel, of_row = call(
        first_window_kernel, [f_count] * turns + [b_ends, b_wsel, b_kinds], [HBM] * 4,
        turns * counting,
        scratch=first_scratch[:1] + first_scratch[2:] + [pltpu.SemaphoreType.DMA((4,))],
    )(*in_hbm(rel_ids, relations, edge_src, edge_dst))
    x1, h0, *sent1 = call(
        first_round_kernel, [f_rows, b_rows, b_pay, b_pay],
        [VMEM] * 8, 7 * square + counting,
    )(*sent0, *got0, c0, ends1, entity, wsel)

    got1 = exchanged(1, *sent1)
    x2, h1, rows2, mapped2 = call(
        second_round_kernel, [f_rows, b_rows, b_rows, b_rows],
        [VMEM] * 7, 7 * square + counting,
    )(*sent1, *got1, c1, x1, wsel)

    axes, offset = buckets[2]
    xq = shifted(rows2, axes, offset)
    far = shifted(mapped2, axes, -offset)
    acc = call(relation_kernel, [f_rel], [VMEM] * 7, 2 * square)(of_row, *sent0, h0, *sent1, h1)[0]
    h2, payload, _ = call(
        last_kernel, [b_rows, b_rel, f_rel],
        [VMEM] * 6, 3 * square, aliases={5: 2},
    )(of_row, rows2, xq, mapped2, c2, acc)
    x3 = call(
        finish_kernel, [f_rows], [VMEM] * 7, 3 * square + counting,
    )(rows2, far, *got0, h2, x2, wsel)[0]

    summed = reduce_everywhere(payload)
    divisor = math.sqrt(turns * lax.axis_size(AXES))
    return x3, (summed / divisor).reshape(relations.shape)


def solution(mesh):
    inner = Mesh(mesh.devices.reshape(2, 4, 2, 2, 8, 2), AXES)
    return jax.shard_map(
        training,
        mesh=inner,
        in_specs=(P(AXES, None), P(), P(None, AXES), P(None, AXES), P(None, AXES)),
        out_specs=(P(AXES, None), P()),
        check_vma=False,
    )
```

```python
import functools
import itertools
import math

import jax
import jax.numpy as jnp
from jax import lax
from jax.experimental import pallas as pl
from jax.experimental.pallas import tpu as pltpu
from jax.sharding import Mesh
from jax.sharding import PartitionSpec as P


AXES = ("xh", "y", "c", "xl", "zh", "zl")
CORE = "c"
GX = ("xh", "y", "c")
GY = ("xl", "zh", "zl")
NEAR = ("xh", "y", "c", "xl", "zl")
DEPTH = ("zl", "zh")
PLANE = ("y", "xh", "xl", "c")
LEARN_RATE = 0.5
GROUPS = 4
VMEM = pl.BlockSpec(memory_space=pltpu.VMEM)
HBM = pl.BlockSpec(memory_space=pltpu.HBM)
F32 = jnp.float32
BF16 = jnp.bfloat16


def shifted(value, axes, steps):
    count = lax.axis_size(axes)
    pairs = [(source, (source + steps) % count) for source in range(count)]
    return lax.ppermute(value, axes, pairs)


def inner_partner(i, count):
    return i ^ 1


def outer_partner(i, count):
    return (i + (1 if i % 2 else -1)) % count


def swapped(value, axes, partner):
    count = lax.axis_size(axes)
    return lax.ppermute(value, axes, [(i, partner(i, count)) for i in range(count)])


def swapped_by_core(value, axes, partners):
    count = lax.axis_size(axes)
    pairs = [
        (core * count + i, core * count + partners[core](i, count))
        for core in range(2) for i in range(count)
    ]
    return lax.ppermute(value, (CORE,) + axes, pairs)


def dot_nn(left, right):
    return lax.dot_general(left, right, (((1,), (0,)), ((), ())), preferred_element_type=F32)


def dot_nt(left, right):
    return lax.dot_general(left, right, (((1,), (1,)), ((), ())), preferred_element_type=F32)


def dot_tn(left, right):
    return lax.dot_general(left, right, (((0,), (0,)), ((), ())), preferred_element_type=F32)


def call(kernel, outs, in_specs, flops, aliases=None, scratch=()):
    moved = sum(math.prod(o.shape) * o.dtype.itemsize for o in outs)
    return pl.pallas_call(
        kernel,
        out_shape=tuple(outs),
        in_specs=list(in_specs),
        out_specs=tuple(VMEM for _ in outs),
        scratch_shapes=list(scratch),
        input_output_aliases=aliases or {},
        compiler_params=pltpu.CompilerParams(vmem_limit_bytes=16 * 2**20),
        cost_estimate=pl.CostEstimate(
            flops=flops, bytes_accessed=4 * moved, transcendentals=0
        ),
    )


def map_rows(rows_b, chosen):
    size = rows_b.shape[0] // GROUPS
    parts = [
        dot_nn(rows_b[g * size : (g + 1) * size, :], chosen(g)).astype(BF16) for g in range(GROUPS)
    ]
    return jnp.concatenate(parts, axis=0)


def chosen_of(wsel_ref, turn):
    return lambda g: wsel_ref[turn * GROUPS + g]


def folded(edge_ref, turn, width):
    pieces = edge_ref.shape[1] // width
    rows = [edge_ref[turn : turn + 1, i * width : (i + 1) * width] for i in range(pieces)]
    return jnp.concatenate(rows, axis=0).astype(F32).astype(BF16)


def one_hot(row, size):
    count = row.shape[1]
    wide = jnp.broadcast_to(row.astype(F32), (16, count)).astype(BF16)
    index = lax.broadcasted_iota(jnp.int32, (16, count), 0).astype(F32).astype(BF16)
    one = jnp.ones((16, count), BF16)
    zero = jnp.zeros((16, count), BF16)
    parts = [jnp.where(wide == index + BF16(16 * i), one, zero) for i in range(size // 16)]
    return jnp.concatenate(parts, axis=0).astype(jnp.float8_e4m3fn)


def counted(row_of, col_of, pieces, size):
    acc = jnp.zeros((size, size), F32)
    for i in range(pieces):
        acc = acc + dot_nt(one_hot(row_of(i), size), one_hot(col_of(i), size))
    return acc


def own_count(ends, size):
    pieces = ends.shape[0] // 2
    return counted(
        lambda i: ends[i : i + 1, :], lambda i: ends[pieces + i : pieces + i + 1, :], pieces, size
    )


def far_count(ends, size):
    pieces = ends.shape[0] // 2
    return counted(
        lambda i: ends[pieces + i : pieces + i + 1, :], lambda i: ends[i : i + 1, :], pieces, size
    )


def slopes(scores, counts):
    scaling = 1.0 / math.sqrt(scores.shape[0])
    return ((jax.nn.sigmoid(scores) - counts) * scaling).astype(BF16)


def source_grad(pulled_b, chosen):
    size = pulled_b.shape[0] // GROUPS
    parts = [dot_nt(pulled_b[g * size : (g + 1) * size, :], chosen(g)) for g in range(GROUPS)]
    return jnp.concatenate(parts, axis=0)


def target_grad(rows_b, mapped, counts_t):
    slopes_t = slopes(dot_nt(rows_b, mapped), counts_t)
    return dot_nn(slopes_t, mapped).astype(BF16).astype(F32)


def add_relation(acc_ref, rows_b, pulled_b, kind_of_row):
    kinds, width = acc_ref.shape[:2]
    zero = jnp.zeros_like(pulled_b)
    apart = [jnp.where(kind_of_row == BF16(k), pulled_b, zero) for k in range(kinds)]
    added = dot_tn(rows_b, jnp.concatenate(apart, axis=1))
    for k in range(kinds):
        acc_ref[k] = acc_ref[k] + added[:, k * width : (k + 1) * width]


def fetched(pairs, sems):
    copies = [
        pltpu.make_async_copy(source, target, sems.at[i])
        for i, (source, target) in enumerate(pairs)
    ]
    for copy in copies:
        copy.start()
    return copies


def is_even(turn):
    core = lax.axis_index(CORE)
    return core == (0 if turn else lax.axis_index(GY[-1]))


def put(even, rows, mapped, inner_ref, outer_ref, part):
    inner_ref[part, :] = jnp.where(even, rows, mapped)
    outer_ref[part, :] = jnp.where(even, mapped, rows)


def sent(even, inner_ref, outer_ref, part):
    inner, outer = inner_ref[part, :], outer_ref[part, :]
    return jnp.where(even, inner, outer), jnp.where(even, outer, inner)


def got(even, inner_ref, outer_ref, part):
    inner, outer = inner_ref[part, :], outer_ref[part, :]
    return jnp.where(even, outer, inner), jnp.where(even, inner, outer)


def in_hbm(*values):
    return [pltpu.with_memory_space_constraint(value, pltpu.HBM) for value in values]


def folded_both(src_ref, dst_ref, turn, width):
    return jnp.concatenate(
        [folded(src_ref, turn, width), folded(dst_ref, turn, width)], axis=0
    )


def prepare_kernel(
    ids_hbm, x_hbm, rel_hbm, src_hbm, dst_hbm, inner_ref, outer_ref,
    ids_ref, x_ref, rel_ref, src_ref, dst_ref, sems,
):
    size, width = x_ref.shape
    even = is_even(0)
    copies = fetched(
        [
            (src_hbm, src_ref), (dst_hbm, dst_ref), (x_hbm, x_ref), (rel_hbm, rel_ref),
            (ids_hbm, ids_ref),
        ],
        sems,
    )
    copies[0].wait()
    copies[1].wait()
    ends = [folded_both(src_ref, dst_ref, turn, width) for turn in (2, 0)]
    put(even, ends[0], ends[1], inner_ref, outer_ref, slice(size, inner_ref.shape[0]))
    copies[2].wait()
    rows_b = x_ref[...].astype(BF16)
    copies[3].wait()
    copies[4].wait()
    mapped = map_rows(rows_b, lambda g: rel_ref[ids_ref[0, g]].astype(BF16))
    put(even, rows_b, mapped, inner_ref, outer_ref, slice(0, size))


def first_window_kernel(
    ids_hbm, rel_hbm, src_hbm, dst_hbm, c0_ref, c1_ref, c2_ref, near_ref, wsel_ref, kinds_ref,
    ids_ref, rel_ref, src_ref, dst_ref, sems,
):
    copies = fetched(
        [(src_hbm, src_ref), (dst_hbm, dst_ref), (ids_hbm, ids_ref), (rel_hbm, rel_ref)], sems
    )
    copies[0].wait()
    copies[1].wait()
    size = c0_ref.shape[0]
    for turn, out_ref in enumerate((c0_ref, c1_ref, c2_ref)):
        ends = folded_both(src_ref, dst_ref, turn, size)
        if turn == 1:
            near_ref[...] = ends
        out_ref[...] = own_count(ends.astype(F32), size)
    copies[2].wait()
    copies[3].wait()
    group_rows = size // GROUPS
    for turn in range(ids_ref.shape[0]):
        for g in range(GROUPS):
            kind = ids_ref[turn, g]
            wsel_ref[turn * GROUPS + g] = rel_ref[kind].astype(BF16)
            whole = jnp.full((group_rows, kinds_ref.shape[2]), kind, jnp.int32)
            kinds_ref[turn, g * group_rows : (g + 1) * group_rows, :] = whole.astype(F32).astype(BF16)


def relation_kernel(kinds_ref, si0_ref, so0_ref, h0_ref, si1_ref, so1_ref, h1_ref, acc_ref):
    top = slice(0, h0_ref.shape[0])
    acc_ref[...] = jnp.zeros_like(acc_ref)
    rows_b, _ = sent(is_even(0), si0_ref, so0_ref, top)
    add_relation(acc_ref, rows_b, h0_ref[...], kinds_ref[0])
    rows_b, _ = sent(is_even(1), si1_ref, so1_ref, top)
    add_relation(acc_ref, rows_b, h1_ref[...], kinds_ref[1])


def stepped(turn, sent_refs, got_refs, c_ref, x_ref, wsel_ref, xn_ref, h_ref):
    size = x_ref.shape[0]
    even = is_even(turn)
    top, tail = slice(0, size), slice(size, sent_refs[0].shape[0])
    rows_b, mapped = sent(even, *sent_refs, top)
    target, far = got(even, *got_refs, top)
    slopes_b = slopes(dot_nt(mapped, target), c_ref[...])
    pulled = dot_nn(slopes_b, target).astype(BF16)
    h_ref[...] = pulled
    _, far_ends = got(even, *got_refs, tail)
    counts_t = far_count(far_ends.astype(F32), size)
    grad = source_grad(pulled, chosen_of(wsel_ref, turn)) + target_grad(rows_b, far, counts_t)
    moved = x_ref[...] - LEARN_RATE * grad
    xn_ref[...] = moved
    moved_b = moved.astype(BF16)
    return moved_b, map_rows(moved_b, chosen_of(wsel_ref, turn + 1))


def first_round_kernel(
    si_ref, so_ref, gi_ref, go_ref, c_ref, near_ref, x_ref, wsel_ref,
    xn_ref, h_ref, inner_ref, outer_ref,
):
    size = x_ref.shape[0]
    rows_b, mapped = stepped(
        0, (si_ref, so_ref), (gi_ref, go_ref), c_ref, x_ref, wsel_ref, xn_ref, h_ref
    )
    put(is_even(1), rows_b, mapped, inner_ref, outer_ref, slice(0, size))
    inner_ref[size:, :] = near_ref[...]
    outer_ref[size:, :] = near_ref[...]


def second_round_kernel(
    si_ref, so_ref, gi_ref, go_ref, c_ref, x_ref, wsel_ref,
    xn_ref, h_ref, rows_ref, mapped_ref,
):
    rows_b, mapped = stepped(
        1, (si_ref, so_ref), (gi_ref, go_ref), c_ref, x_ref, wsel_ref, xn_ref, h_ref
    )
    rows_ref[...] = rows_b
    mapped_ref[...] = mapped


def block_order():
    sizes = [lax.axis_size(axis) for axis in NEAR]
    order = []
    for place in itertools.product(*map(range, sizes)):
        at = dict(zip(NEAR, place))
        block = 0
        for axis in PLANE + (DEPTH[0],):
            block = block * lax.axis_size(axis) + at[axis]
        order.append(block)
    return order


def last_kernel(order, kinds_ref, rows_ref, xq_ref, mapped_ref, c_ref, acc_in_ref, h_ref, out_ref, acc_ref):
    slopes_b = slopes(dot_nt(mapped_ref[...], xq_ref[...]), c_ref[...])
    pulled = dot_nn(slopes_b, xq_ref[...]).astype(BF16)
    h_ref[...] = pulled
    acc_ref[...] = acc_in_ref[...]
    add_relation(acc_ref, rows_ref[...], pulled, kinds_ref[2])
    width = acc_ref.shape[1]
    share = out_ref.shape[0] // len(order)
    for place, block in enumerate(order):
        kind, first = divmod(block * share, width)
        out_ref[place * share : (place + 1) * share, :] = acc_ref[
            kind, first : first + share, :
        ].astype(BF16)


def finish_kernel(rows_ref, far_ref, gi_ref, go_ref, h_ref, x_ref, wsel_ref, xn_ref):
    size = x_ref.shape[0]
    ends, _ = got(is_even(0), gi_ref, go_ref, slice(size, gi_ref.shape[0]))
    counts_t = far_count(ends.astype(F32), size)
    grad = source_grad(h_ref[...], chosen_of(wsel_ref, 2))
    grad = grad + target_grad(rows_ref[...], far_ref[...], counts_t)
    xn_ref[...] = x_ref[...] - LEARN_RATE * grad


def sum_kernel(apart, in_ref, out_ref):
    count, share = in_ref.shape[:2]
    run = count // apart
    for i in range(apart):
        acc = in_ref[i * run].astype(F32)
        for j in range(i * run + 1, (i + 1) * run):
            acc = acc + in_ref[j].astype(F32)
        total = acc.astype(BF16)
        for k in range(out_ref.shape[0]):
            out_ref[k, i * share : (i + 1) * share, :] = total


def summed_for(parts, copies, apart):
    count, share, width = parts.shape
    out = jax.ShapeDtypeStruct((copies, apart * share, width), BF16)
    kernel = functools.partial(sum_kernel, apart)
    return call(kernel, [out], [VMEM], count * share * width)(parts)[0]


def reduce_everywhere(payload):
    rows, width = payload.shape
    near = lax.axis_size(NEAR)
    part = lax.all_to_all(payload.reshape(near, rows // near, width), NEAR, 0, 0)
    part = summed_for(part, lax.axis_size(DEPTH), 1)
    part = lax.all_to_all(part, DEPTH, 0, 0)
    part = summed_for(part, lax.axis_size(PLANE), lax.axis_size(DEPTH[0]))
    part = lax.all_to_all(part, PLANE, 0, 0)
    return part.reshape(rows, width).astype(F32)


def training(entity, relations, rel_ids, edge_src, edge_dst):
    rows, width = entity.shape
    kinds = relations.shape[0]
    turns, edges = edge_src.shape
    square = 2 * rows * rows * width
    counting = 2 * rows * rows * edges
    ends_rows = 2 * edges // width
    f_rows = jax.ShapeDtypeStruct((rows, width), F32)
    b_rows = jax.ShapeDtypeStruct((rows, width), BF16)
    b_pay = jax.ShapeDtypeStruct((rows + ends_rows, width), BF16)
    b_ends = jax.ShapeDtypeStruct((ends_rows, width), BF16)
    f_count = jax.ShapeDtypeStruct((rows, rows), F32)
    f_rel = jax.ShapeDtypeStruct(relations.shape, F32)
    b_rel = jax.ShapeDtypeStruct((kinds * width, width), BF16)
    first_scratch = [
        pltpu.SMEM(rel_ids.shape, jnp.int32), pltpu.VMEM(entity.shape, F32),
        pltpu.VMEM(relations.shape, F32),
    ] + [pltpu.VMEM(edge_src.shape, jnp.int32)] * 2
    buckets = ((GY, 1), (GX, 1), (GY, -1))

    def exchanged(turn, inner, outer):
        axes = buckets[turn][0]
        partners = (inner_partner, outer_partner)
        if CORE in axes:
            outer_got = swapped(outer, axes, outer_partner)
        else:
            outer_got = swapped_by_core(outer, axes, partners[::-1])
        if CORE in axes:
            inner_got = swapped(inner, axes, inner_partner)
        else:
            inner_got = swapped_by_core(inner, axes, partners)
        return inner_got, outer_got

    sent0 = call(
        prepare_kernel, [b_pay, b_pay], [HBM] * 5, square,
        scratch=first_scratch + [pltpu.SemaphoreType.DMA((5,))],
    )(*in_hbm(rel_ids, entity, relations, edge_src, edge_dst))

    got0 = exchanged(0, *sent0)
    b_wsel = jax.ShapeDtypeStruct((turns * GROUPS, width, width), BF16)
    b_kinds = jax.ShapeDtypeStruct((turns, rows, width), BF16)
    c0, c1, c2, ends1, wsel, of_row = call(
        first_window_kernel, [f_count] * turns + [b_ends, b_wsel, b_kinds], [HBM] * 4,
        turns * counting,
        scratch=first_scratch[:1] + first_scratch[2:] + [pltpu.SemaphoreType.DMA((4,))],
    )(*in_hbm(rel_ids, relations, edge_src, edge_dst))
    x1, h0, *sent1 = call(
        first_round_kernel, [f_rows, b_rows, b_pay, b_pay],
        [VMEM] * 8, 7 * square + counting,
    )(*sent0, *got0, c0, ends1, entity, wsel)

    got1 = exchanged(1, *sent1)
    x2, h1, rows2, mapped2 = call(
        second_round_kernel, [f_rows, b_rows, b_rows, b_rows],
        [VMEM] * 7, 7 * square + counting,
    )(*sent1, *got1, c1, x1, wsel)

    axes, offset = buckets[2]
    xq = shifted(rows2, axes, offset)
    far = shifted(mapped2, axes, -offset)
    acc = call(relation_kernel, [f_rel], [VMEM] * 7, 2 * square)(of_row, *sent0, h0, *sent1, h1)[0]
    h2, payload, _ = call(
        functools.partial(last_kernel, block_order()), [b_rows, b_rel, f_rel],
        [VMEM] * 6, 3 * square, aliases={5: 2},
    )(of_row, rows2, xq, mapped2, c2, acc)
    x3 = call(
        finish_kernel, [f_rows], [VMEM] * 7, 3 * square + counting,
    )(rows2, far, *got0, h2, x2, wsel)[0]

    summed = reduce_everywhere(payload)
    divisor = math.sqrt(turns * lax.axis_size(AXES))
    return x3, (summed / divisor).reshape(relations.shape)


def solution(mesh):
    inner = Mesh(mesh.devices.reshape(2, 4, 2, 2, 8, 2), AXES)
    return jax.shard_map(
        training,
        mesh=inner,
        in_specs=(P(AXES, None), P(), P(None, AXES), P(None, AXES), P(None, AXES)),
        out_specs=(P(AXES, None), P()),
        check_vma=False,
    )
```

```python
import functools
import math

import jax
import jax.numpy as jnp
from jax import lax
from jax.experimental import pallas as pl
from jax.experimental.pallas import tpu as pltpu
from jax.sharding import Mesh
from jax.sharding import PartitionSpec as P


AXES = ("xh", "y", "c", "xl", "zh", "zl")
CORE = "c"
GX = ("xh", "y", "c")
GY = ("xl", "zh", "zl")
PLANE = ("xh", "y", "c", "xl")
NEAR = PLANE + ("zl",)
DEPTH = ("zh", "zl")
LEARN_RATE = 0.5
GROUPS = 4
VMEM = pl.BlockSpec(memory_space=pltpu.VMEM)
HBM = pl.BlockSpec(memory_space=pltpu.HBM)
F32 = jnp.float32
BF16 = jnp.bfloat16


def shifted(value, axes, steps):
    count = lax.axis_size(axes)
    pairs = [(source, (source + steps) % count) for source in range(count)]
    return lax.ppermute(value, axes, pairs)


def inner_partner(i, count):
    return i ^ 1


def outer_partner(i, count):
    return (i + (1 if i % 2 else -1)) % count


def swapped(value, axes, partner):
    count = lax.axis_size(axes)
    return lax.ppermute(value, axes, [(i, partner(i, count)) for i in range(count)])


def swapped_by_core(value, axes, partners):
    count = lax.axis_size(axes)
    pairs = [
        (core * count + i, core * count + partners[core](i, count))
        for core in range(2) for i in range(count)
    ]
    return lax.ppermute(value, (CORE,) + axes, pairs)


def dot_nn(left, right):
    return lax.dot_general(left, right, (((1,), (0,)), ((), ())), preferred_element_type=F32)


def dot_nt(left, right):
    return lax.dot_general(left, right, (((1,), (1,)), ((), ())), preferred_element_type=F32)


def dot_tn(left, right):
    return lax.dot_general(left, right, (((0,), (0,)), ((), ())), preferred_element_type=F32)


def call(kernel, outs, in_specs, flops, aliases=None, scratch=()):
    moved = sum(math.prod(o.shape) * o.dtype.itemsize for o in outs)
    return pl.pallas_call(
        kernel,
        out_shape=tuple(outs),
        in_specs=list(in_specs),
        out_specs=tuple(VMEM for _ in outs),
        scratch_shapes=list(scratch),
        input_output_aliases=aliases or {},
        compiler_params=pltpu.CompilerParams(vmem_limit_bytes=16 * 2**20),
        cost_estimate=pl.CostEstimate(
            flops=flops, bytes_accessed=4 * moved, transcendentals=0
        ),
    )


def map_rows(rows_b, chosen):
    size = rows_b.shape[0] // GROUPS
    parts = [
        dot_nn(rows_b[g * size : (g + 1) * size, :], chosen(g)).astype(BF16) for g in range(GROUPS)
    ]
    return jnp.concatenate(parts, axis=0)


def chosen_of(wsel_ref, turn):
    return lambda g: wsel_ref[turn * GROUPS + g]


def folded(edge_ref, turn, width):
    pieces = edge_ref.shape[1] // width
    rows = [edge_ref[turn : turn + 1, i * width : (i + 1) * width] for i in range(pieces)]
    return jnp.concatenate(rows, axis=0).astype(F32).astype(BF16)


def one_hot(row, size):
    count = row.shape[1]
    wide = jnp.broadcast_to(row.astype(F32), (16, count)).astype(BF16)
    index = lax.broadcasted_iota(jnp.int32, (16, count), 0).astype(F32).astype(BF16)
    one = jnp.ones((16, count), BF16)
    zero = jnp.zeros((16, count), BF16)
    parts = [jnp.where(wide == index + BF16(16 * i), one, zero) for i in range(size // 16)]
    return jnp.concatenate(parts, axis=0).astype(jnp.float8_e4m3fn)


def counted(row_of, col_of, pieces, size):
    acc = jnp.zeros((size, size), F32)
    for i in range(pieces):
        acc = acc + dot_nt(one_hot(row_of(i), size), one_hot(col_of(i), size))
    return acc


def own_count(ends, size):
    pieces = ends.shape[0] // 2
    return counted(
        lambda i: ends[i : i + 1, :], lambda i: ends[pieces + i : pieces + i + 1, :], pieces, size
    )


def far_count(ends, size):
    pieces = ends.shape[0] // 2
    return counted(
        lambda i: ends[pieces + i : pieces + i + 1, :], lambda i: ends[i : i + 1, :], pieces, size
    )


def slopes(scores, counts):
    scaling = 1.0 / math.sqrt(scores.shape[0])
    return ((jax.nn.sigmoid(scores) - counts) * scaling).astype(BF16)


def source_grad(pulled_b, chosen):
    size = pulled_b.shape[0] // GROUPS
    parts = [dot_nt(pulled_b[g * size : (g + 1) * size, :], chosen(g)) for g in range(GROUPS)]
    return jnp.concatenate(parts, axis=0)


def target_grad(rows_b, mapped, counts_t):
    slopes_t = slopes(dot_nt(rows_b, mapped), counts_t)
    return dot_nn(slopes_t, mapped).astype(BF16).astype(F32)


def add_relation(acc_ref, rows_b, pulled_b, kind_of_row):
    kinds, width = acc_ref.shape[:2]
    zero = jnp.zeros_like(pulled_b)
    apart = [jnp.where(kind_of_row == BF16(k), pulled_b, zero) for k in range(kinds)]
    added = dot_tn(rows_b, jnp.concatenate(apart, axis=1))
    for k in range(kinds):
        acc_ref[k] = acc_ref[k] + added[:, k * width : (k + 1) * width]


def fetched(pairs, sems):
    copies = [
        pltpu.make_async_copy(source, target, sems.at[i])
        for i, (source, target) in enumerate(pairs)
    ]
    for copy in copies:
        copy.start()
    return copies


def is_even(turn):
    core = lax.axis_index(CORE)
    return core == (0 if turn else lax.axis_index(GY[-1]))


def put(even, rows, mapped, inner_ref, outer_ref, part):
    inner_ref[part, :] = jnp.where(even, rows, mapped)
    outer_ref[part, :] = jnp.where(even, mapped, rows)


def sent(even, inner_ref, outer_ref, part):
    inner, outer = inner_ref[part, :], outer_ref[part, :]
    return jnp.where(even, inner, outer), jnp.where(even, outer, inner)


def got(even, inner_ref, outer_ref, part):
    inner, outer = inner_ref[part, :], outer_ref[part, :]
    return jnp.where(even, outer, inner), jnp.where(even, inner, outer)


def in_hbm(*values):
    return [pltpu.with_memory_space_constraint(value, pltpu.HBM) for value in values]


def folded_both(src_ref, dst_ref, turn, width):
    return jnp.concatenate(
        [folded(src_ref, turn, width), folded(dst_ref, turn, width)], axis=0
    )


def prepare_kernel(
    ids_hbm, x_hbm, rel_hbm, src_hbm, dst_hbm, inner_ref, outer_ref,
    ids_ref, x_ref, rel_ref, src_ref, dst_ref, sems,
):
    size, width = x_ref.shape
    even = is_even(0)
    copies = fetched(
        [
            (src_hbm, src_ref), (dst_hbm, dst_ref), (x_hbm, x_ref), (rel_hbm, rel_ref),
            (ids_hbm, ids_ref),
        ],
        sems,
    )
    copies[0].wait()
    copies[1].wait()
    ends = [folded_both(src_ref, dst_ref, turn, width) for turn in (2, 0)]
    put(even, ends[0], ends[1], inner_ref, outer_ref, slice(size, inner_ref.shape[0]))
    copies[2].wait()
    rows_b = x_ref[...].astype(BF16)
    copies[3].wait()
    copies[4].wait()
    mapped = map_rows(rows_b, lambda g: rel_ref[ids_ref[0, g]].astype(BF16))
    put(even, rows_b, mapped, inner_ref, outer_ref, slice(0, size))


def first_window_kernel(
    ids_hbm, rel_hbm, src_hbm, dst_hbm, c0_ref, c1_ref, c2_ref, near_ref, wsel_ref, kinds_ref,
    ids_ref, rel_ref, src_ref, dst_ref, sems,
):
    copies = fetched(
        [(src_hbm, src_ref), (dst_hbm, dst_ref), (ids_hbm, ids_ref), (rel_hbm, rel_ref)], sems
    )
    copies[0].wait()
    copies[1].wait()
    size = c0_ref.shape[0]
    for turn, out_ref in enumerate((c0_ref, c1_ref, c2_ref)):
        ends = folded_both(src_ref, dst_ref, turn, size)
        if turn == 1:
            near_ref[...] = ends
        out_ref[...] = own_count(ends.astype(F32), size)
    copies[2].wait()
    copies[3].wait()
    group_rows = size // GROUPS
    for turn in range(ids_ref.shape[0]):
        for g in range(GROUPS):
            kind = ids_ref[turn, g]
            wsel_ref[turn * GROUPS + g] = rel_ref[kind].astype(BF16)
            whole = jnp.full((group_rows, kinds_ref.shape[2]), kind, jnp.int32)
            kinds_ref[turn, g * group_rows : (g + 1) * group_rows, :] = whole.astype(F32).astype(BF16)


def relation_kernel(kinds_ref, si0_ref, so0_ref, h0_ref, si1_ref, so1_ref, h1_ref, acc_ref):
    top = slice(0, h0_ref.shape[0])
    acc_ref[...] = jnp.zeros_like(acc_ref)
    rows_b, _ = sent(is_even(0), si0_ref, so0_ref, top)
    add_relation(acc_ref, rows_b, h0_ref[...], kinds_ref[0])
    rows_b, _ = sent(is_even(1), si1_ref, so1_ref, top)
    add_relation(acc_ref, rows_b, h1_ref[...], kinds_ref[1])


def stepped(turn, sent_refs, got_refs, c_ref, x_ref, wsel_ref, xn_ref, h_ref):
    size = x_ref.shape[0]
    even = is_even(turn)
    top, tail = slice(0, size), slice(size, sent_refs[0].shape[0])
    rows_b, mapped = sent(even, *sent_refs, top)
    target, far = got(even, *got_refs, top)
    slopes_b = slopes(dot_nt(mapped, target), c_ref[...])
    pulled = dot_nn(slopes_b, target).astype(BF16)
    h_ref[...] = pulled
    _, far_ends = got(even, *got_refs, tail)
    counts_t = far_count(far_ends.astype(F32), size)
    grad = source_grad(pulled, chosen_of(wsel_ref, turn)) + target_grad(rows_b, far, counts_t)
    moved = x_ref[...] - LEARN_RATE * grad
    xn_ref[...] = moved
    moved_b = moved.astype(BF16)
    return moved_b, map_rows(moved_b, chosen_of(wsel_ref, turn + 1))


def first_round_kernel(
    si_ref, so_ref, gi_ref, go_ref, c_ref, near_ref, x_ref, wsel_ref,
    xn_ref, h_ref, inner_ref, outer_ref,
):
    size = x_ref.shape[0]
    rows_b, mapped = stepped(
        0, (si_ref, so_ref), (gi_ref, go_ref), c_ref, x_ref, wsel_ref, xn_ref, h_ref
    )
    put(is_even(1), rows_b, mapped, inner_ref, outer_ref, slice(0, size))
    inner_ref[size:, :] = near_ref[...]
    outer_ref[size:, :] = near_ref[...]


def second_round_kernel(
    si_ref, so_ref, gi_ref, go_ref, c_ref, x_ref, wsel_ref,
    xn_ref, h_ref, rows_ref, mapped_ref,
):
    rows_b, mapped = stepped(
        1, (si_ref, so_ref), (gi_ref, go_ref), c_ref, x_ref, wsel_ref, xn_ref, h_ref
    )
    rows_ref[...] = rows_b
    mapped_ref[...] = mapped


def last_kernel(kinds_ref, rows_ref, xq_ref, mapped_ref, c_ref, acc_in_ref, h_ref, out_ref, acc_ref):
    slopes_b = slopes(dot_nt(mapped_ref[...], xq_ref[...]), c_ref[...])
    pulled = dot_nn(slopes_b, xq_ref[...]).astype(BF16)
    h_ref[...] = pulled
    acc_ref[...] = acc_in_ref[...]
    add_relation(acc_ref, rows_ref[...], pulled, kinds_ref[2])
    kinds, width = acc_ref.shape[:2]
    for k in range(kinds):
        out_ref[k * width : (k + 1) * width, :] = acc_ref[k].astype(BF16)


def finish_kernel(rows_ref, far_ref, gi_ref, go_ref, h_ref, x_ref, wsel_ref, xn_ref):
    size = x_ref.shape[0]
    ends, _ = got(is_even(0), gi_ref, go_ref, slice(size, gi_ref.shape[0]))
    counts_t = far_count(ends.astype(F32), size)
    grad = source_grad(h_ref[...], chosen_of(wsel_ref, 2))
    grad = grad + target_grad(rows_ref[...], far_ref[...], counts_t)
    xn_ref[...] = x_ref[...] - LEARN_RATE * grad


def sum_kernel(apart, in_ref, out_ref):
    share = in_ref.shape[1]
    for i in range(apart):
        acc = in_ref[i].astype(F32)
        for j in range(i + apart, in_ref.shape[0], apart):
            acc = acc + in_ref[j].astype(F32)
        total = acc.astype(BF16)
        for k in range(out_ref.shape[0]):
            out_ref[k, i * share : (i + 1) * share, :] = total


def widen_kernel(scale, in_ref, out_hbm, wide_ref, sems):
    kinds, width = wide_ref.shape[:2]
    copies = []
    for k in range(kinds):
        wide_ref[k] = in_ref[k * width : (k + 1) * width, :].astype(F32) * scale
        copies.append(pltpu.make_async_copy(wide_ref.at[k], out_hbm.at[k], sems.at[k]))
        copies[-1].start()
    for copy in copies:
        copy.wait()


def summed_for(parts, copies, apart):
    count, share, width = parts.shape
    out = jax.ShapeDtypeStruct((copies, apart * share, width), BF16)
    kernel = functools.partial(sum_kernel, apart)
    return call(kernel, [out], [VMEM], count * share * width)(parts)[0]


def reduce_everywhere(payload):
    rows, width = payload.shape
    near = lax.axis_size(NEAR)
    part = lax.all_to_all(payload.reshape(near, rows // near, width), NEAR, 0, 0)
    part = summed_for(part, lax.axis_size(DEPTH), 1)
    part = lax.all_to_all(part, DEPTH, 0, 0)
    part = summed_for(part, lax.axis_size(PLANE), lax.axis_size(DEPTH[-1]))
    return lax.all_to_all(part, PLANE, 0, 0).reshape(rows, width)


def training(entity, relations, rel_ids, edge_src, edge_dst):
    rows, width = entity.shape
    kinds = relations.shape[0]
    turns, edges = edge_src.shape
    square = 2 * rows * rows * width
    counting = 2 * rows * rows * edges
    ends_rows = 2 * edges // width
    f_rows = jax.ShapeDtypeStruct((rows, width), F32)
    b_rows = jax.ShapeDtypeStruct((rows, width), BF16)
    b_pay = jax.ShapeDtypeStruct((rows + ends_rows, width), BF16)
    b_ends = jax.ShapeDtypeStruct((ends_rows, width), BF16)
    f_count = jax.ShapeDtypeStruct((rows, rows), F32)
    f_rel = jax.ShapeDtypeStruct(relations.shape, F32)
    b_rel = jax.ShapeDtypeStruct((kinds * width, width), BF16)
    first_scratch = [
        pltpu.SMEM(rel_ids.shape, jnp.int32), pltpu.VMEM(entity.shape, F32),
        pltpu.VMEM(relations.shape, F32),
    ] + [pltpu.VMEM(edge_src.shape, jnp.int32)] * 2
    buckets = ((GY, 1), (GX, 1), (GY, -1))

    def exchanged(turn, inner, outer):
        axes = buckets[turn][0]
        partners = (inner_partner, outer_partner)
        if CORE in axes:
            outer_got = swapped(outer, axes, outer_partner)
        else:
            outer_got = swapped_by_core(outer, axes, partners[::-1])
        if CORE in axes:
            inner_got = swapped(inner, axes, inner_partner)
        else:
            inner_got = swapped_by_core(inner, axes, partners)
        return inner_got, outer_got

    sent0 = call(
        prepare_kernel, [b_pay, b_pay], [HBM] * 5, square,
        scratch=first_scratch + [pltpu.SemaphoreType.DMA((5,))],
    )(*in_hbm(rel_ids, entity, relations, edge_src, edge_dst))

    got0 = exchanged(0, *sent0)
    b_wsel = jax.ShapeDtypeStruct((turns * GROUPS, width, width), BF16)
    b_kinds = jax.ShapeDtypeStruct((turns, rows, width), BF16)
    c0, c1, c2, ends1, wsel, of_row = call(
        first_window_kernel, [f_count] * turns + [b_ends, b_wsel, b_kinds], [HBM] * 4,
        turns * counting,
        scratch=first_scratch[:1] + first_scratch[2:] + [pltpu.SemaphoreType.DMA((4,))],
    )(*in_hbm(rel_ids, relations, edge_src, edge_dst))
    x1, h0, *sent1 = call(
        first_round_kernel, [f_rows, b_rows, b_pay, b_pay],
        [VMEM] * 8, 7 * square + counting,
    )(*sent0, *got0, c0, ends1, entity, wsel)

    got1 = exchanged(1, *sent1)
    x2, h1, rows2, mapped2 = call(
        second_round_kernel, [f_rows, b_rows, b_rows, b_rows],
        [VMEM] * 7, 7 * square + counting,
    )(*sent1, *got1, c1, x1, wsel)

    axes, offset = buckets[2]
    xq = shifted(rows2, axes, offset)
    far = shifted(mapped2, axes, -offset)
    acc = call(relation_kernel, [f_rel], [VMEM] * 7, 2 * square)(of_row, *sent0, h0, *sent1, h1)[0]
    h2, payload, _ = call(
        last_kernel, [b_rows, b_rel, f_rel],
        [VMEM] * 6, 3 * square, aliases={5: 2},
    )(of_row, rows2, xq, mapped2, c2, acc)
    x3 = call(
        finish_kernel, [f_rows], [VMEM] * 7, 3 * square + counting,
    )(rows2, far, *got0, h2, x2, wsel)[0]

    scale = 1.0 / math.sqrt(turns * lax.axis_size(AXES))
    rel_grad = pl.pallas_call(
        functools.partial(widen_kernel, scale),
        out_shape=f_rel,
        in_specs=[VMEM],
        out_specs=HBM,
        scratch_shapes=[pltpu.VMEM(relations.shape, F32), pltpu.SemaphoreType.DMA((kinds,))],
        compiler_params=pltpu.CompilerParams(vmem_limit_bytes=16 * 2**20),
        name="widen",
    )(reduce_everywhere(payload))
    return x3, rel_grad


def solution(mesh):
    inner = Mesh(mesh.devices.reshape(2, 4, 2, 2, 8, 2), AXES)
    return jax.shard_map(
        training,
        mesh=inner,
        in_specs=(P(AXES, None), P(), P(None, AXES), P(None, AXES), P(None, AXES)),
        out_specs=(P(AXES, None), P()),
        check_vma=False,
    )
```

```python
import functools
import itertools
import math

import jax
import jax.numpy as jnp
from jax import lax
from jax.experimental import pallas as pl
from jax.experimental.pallas import tpu as pltpu
from jax.sharding import Mesh
from jax.sharding import PartitionSpec as P


AXES = ("xh", "y", "c", "xl", "zh", "zl")
CORE = "c"
GX = ("xh", "y", "c")
GY = ("xl", "zh", "zl")
NEAR = ("xh", "y", "c", "xl", "zl")
DEPTH = ("zh", "zl")
PLANE = ("y", "xh", "xl", "c")
LEARN_RATE = 0.5
GROUPS = 4
VMEM = pl.BlockSpec(memory_space=pltpu.VMEM)
HBM = pl.BlockSpec(memory_space=pltpu.HBM)
F32 = jnp.float32
BF16 = jnp.bfloat16


def shifted(value, axes, steps):
    count = lax.axis_size(axes)
    pairs = [(source, (source + steps) % count) for source in range(count)]
    return lax.ppermute(value, axes, pairs)


def inner_partner(i, count):
    return i ^ 1


def outer_partner(i, count):
    return (i + (1 if i % 2 else -1)) % count


def swapped(value, axes, partner):
    count = lax.axis_size(axes)
    return lax.ppermute(value, axes, [(i, partner(i, count)) for i in range(count)])


def swapped_by_core(value, axes, partners):
    count = lax.axis_size(axes)
    pairs = [
        (core * count + i, core * count + partners[core](i, count))
        for core in range(2) for i in range(count)
    ]
    return lax.ppermute(value, (CORE,) + axes, pairs)


def dot_nn(left, right):
    return lax.dot_general(left, right, (((1,), (0,)), ((), ())), preferred_element_type=F32)


def dot_nt(left, right):
    return lax.dot_general(left, right, (((1,), (1,)), ((), ())), preferred_element_type=F32)


def dot_tn(left, right):
    return lax.dot_general(left, right, (((0,), (0,)), ((), ())), preferred_element_type=F32)


def call(kernel, outs, in_specs, flops, aliases=None, scratch=()):
    moved = sum(math.prod(o.shape) * o.dtype.itemsize for o in outs)
    return pl.pallas_call(
        kernel,
        out_shape=tuple(outs),
        in_specs=list(in_specs),
        out_specs=tuple(VMEM for _ in outs),
        scratch_shapes=list(scratch),
        input_output_aliases=aliases or {},
        compiler_params=pltpu.CompilerParams(vmem_limit_bytes=16 * 2**20),
        cost_estimate=pl.CostEstimate(
            flops=flops, bytes_accessed=4 * moved, transcendentals=0
        ),
    )


def map_rows(rows_b, chosen):
    size = rows_b.shape[0] // GROUPS
    parts = [
        dot_nn(rows_b[g * size : (g + 1) * size, :], chosen(g)).astype(BF16) for g in range(GROUPS)
    ]
    return jnp.concatenate(parts, axis=0)


def chosen_of(wsel_ref, turn):
    return lambda g: wsel_ref[turn * GROUPS + g]


def folded(edge_ref, turn, width):
    pieces = edge_ref.shape[1] // width
    rows = [edge_ref[turn : turn + 1, i * width : (i + 1) * width] for i in range(pieces)]
    return jnp.concatenate(rows, axis=0).astype(F32).astype(BF16)


def one_hot(row, size):
    count = row.shape[1]
    wide = jnp.broadcast_to(row.astype(F32), (16, count)).astype(BF16)
    index = lax.broadcasted_iota(jnp.int32, (16, count), 0).astype(F32).astype(BF16)
    one = jnp.ones((16, count), BF16)
    zero = jnp.zeros((16, count), BF16)
    parts = [jnp.where(wide == index + BF16(16 * i), one, zero) for i in range(size // 16)]
    return jnp.concatenate(parts, axis=0).astype(jnp.float8_e4m3fn)


def counted(row_of, col_of, pieces, size):
    acc = jnp.zeros((size, size), F32)
    for i in range(pieces):
        acc = acc + dot_nt(one_hot(row_of(i), size), one_hot(col_of(i), size))
    return acc


def own_count(ends, size):
    pieces = ends.shape[0] // 2
    return counted(
        lambda i: ends[i : i + 1, :], lambda i: ends[pieces + i : pieces + i + 1, :], pieces, size
    )


def far_count(ends, size):
    pieces = ends.shape[0] // 2
    return counted(
        lambda i: ends[pieces + i : pieces + i + 1, :], lambda i: ends[i : i + 1, :], pieces, size
    )


def slopes(scores, counts):
    scaling = 1.0 / math.sqrt(scores.shape[0])
    return ((jax.nn.sigmoid(scores) - counts) * scaling).astype(BF16)


def source_grad(pulled_b, chosen):
    size = pulled_b.shape[0] // GROUPS
    parts = [dot_nt(pulled_b[g * size : (g + 1) * size, :], chosen(g)) for g in range(GROUPS)]
    return jnp.concatenate(parts, axis=0)


def target_grad(rows_b, mapped, counts_t):
    slopes_t = slopes(dot_nt(rows_b, mapped), counts_t)
    return dot_nn(slopes_t, mapped).astype(BF16).astype(F32)


def add_relation(acc_ref, rows_b, pulled_b, kind_of_row):
    kinds, width = acc_ref.shape[:2]
    zero = jnp.zeros_like(pulled_b)
    apart = [jnp.where(kind_of_row == BF16(k), pulled_b, zero) for k in range(kinds)]
    added = dot_tn(rows_b, jnp.concatenate(apart, axis=1))
    for k in range(kinds):
        acc_ref[k] = acc_ref[k] + added[:, k * width : (k + 1) * width]


def fetched(pairs, sems):
    copies = [
        pltpu.make_async_copy(source, target, sems.at[i])
        for i, (source, target) in enumerate(pairs)
    ]
    for copy in copies:
        copy.start()
    return copies


def is_even(turn):
    core = lax.axis_index(CORE)
    return core == (0 if turn else lax.axis_index(GY[-1]))


def put(even, rows, mapped, inner_ref, outer_ref, part):
    inner_ref[part, :] = jnp.where(even, rows, mapped)
    outer_ref[part, :] = jnp.where(even, mapped, rows)


def sent(even, inner_ref, outer_ref, part):
    inner, outer = inner_ref[part, :], outer_ref[part, :]
    return jnp.where(even, inner, outer), jnp.where(even, outer, inner)


def got(even, inner_ref, outer_ref, part):
    inner, outer = inner_ref[part, :], outer_ref[part, :]
    return jnp.where(even, outer, inner), jnp.where(even, inner, outer)


def in_hbm(*values):
    return [pltpu.with_memory_space_constraint(value, pltpu.HBM) for value in values]


def folded_both(src_ref, dst_ref, turn, width):
    return jnp.concatenate(
        [folded(src_ref, turn, width), folded(dst_ref, turn, width)], axis=0
    )


def prepare_kernel(
    ids_hbm, x_hbm, rel_hbm, src_hbm, dst_hbm, inner_ref, outer_ref,
    ids_ref, x_ref, rel_ref, src_ref, dst_ref, sems,
):
    size, width = x_ref.shape
    even = is_even(0)
    copies = fetched(
        [
            (src_hbm, src_ref), (dst_hbm, dst_ref), (x_hbm, x_ref), (rel_hbm, rel_ref),
            (ids_hbm, ids_ref),
        ],
        sems,
    )
    copies[0].wait()
    copies[1].wait()
    ends = [folded_both(src_ref, dst_ref, turn, width) for turn in (2, 0)]
    put(even, ends[0], ends[1], inner_ref, outer_ref, slice(size, inner_ref.shape[0]))
    copies[2].wait()
    rows_b = x_ref[...].astype(BF16)
    copies[3].wait()
    copies[4].wait()
    mapped = map_rows(rows_b, lambda g: rel_ref[ids_ref[0, g]].astype(BF16))
    put(even, rows_b, mapped, inner_ref, outer_ref, slice(0, size))


def first_window_kernel(
    ids_hbm, rel_hbm, src_hbm, dst_hbm, c0_ref, c1_ref, c2_ref, near_ref, wsel_ref, kinds_ref,
    ids_ref, rel_ref, src_ref, dst_ref, sems,
):
    copies = fetched(
        [(src_hbm, src_ref), (dst_hbm, dst_ref), (ids_hbm, ids_ref), (rel_hbm, rel_ref)], sems
    )
    copies[0].wait()
    copies[1].wait()
    size = c0_ref.shape[0]
    for turn, out_ref in enumerate((c0_ref, c1_ref, c2_ref)):
        ends = folded_both(src_ref, dst_ref, turn, size)
        if turn == 1:
            near_ref[...] = ends
        out_ref[...] = own_count(ends.astype(F32), size)
    copies[2].wait()
    copies[3].wait()
    group_rows = size // GROUPS
    for turn in range(ids_ref.shape[0]):
        for g in range(GROUPS):
            kind = ids_ref[turn, g]
            wsel_ref[turn * GROUPS + g] = rel_ref[kind].astype(BF16)
            whole = jnp.full((group_rows, kinds_ref.shape[2]), kind, jnp.int32)
            kinds_ref[turn, g * group_rows : (g + 1) * group_rows, :] = whole.astype(F32).astype(BF16)


def relation_kernel(kinds_ref, si0_ref, so0_ref, h0_ref, si1_ref, so1_ref, h1_ref, acc_ref):
    top = slice(0, h0_ref.shape[0])
    acc_ref[...] = jnp.zeros_like(acc_ref)
    rows_b, _ = sent(is_even(0), si0_ref, so0_ref, top)
    add_relation(acc_ref, rows_b, h0_ref[...], kinds_ref[0])
    rows_b, _ = sent(is_even(1), si1_ref, so1_ref, top)
    add_relation(acc_ref, rows_b, h1_ref[...], kinds_ref[1])


def stepped(turn, sent_refs, got_refs, c_ref, x_ref, wsel_ref, xn_ref, h_ref):
    size = x_ref.shape[0]
    even = is_even(turn)
    top, tail = slice(0, size), slice(size, sent_refs[0].shape[0])
    rows_b, mapped = sent(even, *sent_refs, top)
    target, far = got(even, *got_refs, top)
    slopes_b = slopes(dot_nt(mapped, target), c_ref[...])
    pulled = dot_nn(slopes_b, target).astype(BF16)
    h_ref[...] = pulled
    _, far_ends = got(even, *got_refs, tail)
    counts_t = far_count(far_ends.astype(F32), size)
    grad = source_grad(pulled, chosen_of(wsel_ref, turn)) + target_grad(rows_b, far, counts_t)
    moved = x_ref[...] - LEARN_RATE * grad
    xn_ref[...] = moved
    moved_b = moved.astype(BF16)
    return moved_b, map_rows(moved_b, chosen_of(wsel_ref, turn + 1))


def first_round_kernel(
    si_ref, so_ref, gi_ref, go_ref, c_ref, near_ref, x_ref, wsel_ref,
    xn_ref, h_ref, inner_ref, outer_ref,
):
    size = x_ref.shape[0]
    rows_b, mapped = stepped(
        0, (si_ref, so_ref), (gi_ref, go_ref), c_ref, x_ref, wsel_ref, xn_ref, h_ref
    )
    put(is_even(1), rows_b, mapped, inner_ref, outer_ref, slice(0, size))
    inner_ref[size:, :] = near_ref[...]
    outer_ref[size:, :] = near_ref[...]


def second_round_kernel(
    si_ref, so_ref, gi_ref, go_ref, c_ref, x_ref, wsel_ref,
    xn_ref, h_ref, rows_ref, mapped_ref,
):
    rows_b, mapped = stepped(
        1, (si_ref, so_ref), (gi_ref, go_ref), c_ref, x_ref, wsel_ref, xn_ref, h_ref
    )
    rows_ref[...] = rows_b
    mapped_ref[...] = mapped


def block_order():
    sizes = [lax.axis_size(axis) for axis in NEAR]
    order = []
    for place in itertools.product(*map(range, sizes)):
        at = dict(zip(NEAR, place))
        block = 0
        for axis in PLANE + (DEPTH[-1],):
            block = block * lax.axis_size(axis) + at[axis]
        order.append(block)
    return order


def last_kernel(order, kinds_ref, rows_ref, xq_ref, mapped_ref, c_ref, acc_in_ref, h_ref, out_ref, acc_ref):
    slopes_b = slopes(dot_nt(mapped_ref[...], xq_ref[...]), c_ref[...])
    pulled = dot_nn(slopes_b, xq_ref[...]).astype(BF16)
    h_ref[...] = pulled
    acc_ref[...] = acc_in_ref[...]
    add_relation(acc_ref, rows_ref[...], pulled, kinds_ref[2])
    width = acc_ref.shape[1]
    share = out_ref.shape[0] // len(order)
    for place, block in enumerate(order):
        kind, first = divmod(block * share, width)
        out_ref[place * share : (place + 1) * share, :] = acc_ref[
            kind, first : first + share, :
        ].astype(BF16)


def finish_kernel(rows_ref, far_ref, gi_ref, go_ref, h_ref, x_ref, wsel_ref, xn_ref):
    size = x_ref.shape[0]
    ends, _ = got(is_even(0), gi_ref, go_ref, slice(size, gi_ref.shape[0]))
    counts_t = far_count(ends.astype(F32), size)
    grad = source_grad(h_ref[...], chosen_of(wsel_ref, 2))
    grad = grad + target_grad(rows_ref[...], far_ref[...], counts_t)
    xn_ref[...] = x_ref[...] - LEARN_RATE * grad


def sum_kernel(apart, in_ref, out_ref):
    share = in_ref.shape[1]
    for i in range(apart):
        acc = in_ref[i].astype(F32)
        for j in range(i + apart, in_ref.shape[0], apart):
            acc = acc + in_ref[j].astype(F32)
        total = acc.astype(BF16)
        for k in range(out_ref.shape[0]):
            out_ref[k, i * share : (i + 1) * share, :] = total


def summed_for(parts, copies, apart):
    count, share, width = parts.shape
    out = jax.ShapeDtypeStruct((copies, apart * share, width), BF16)
    kernel = functools.partial(sum_kernel, apart)
    return call(kernel, [out], [VMEM], count * share * width)(parts)[0]


def reduce_everywhere(payload):
    rows, width = payload.shape
    near = lax.axis_size(NEAR)
    part = lax.all_to_all(payload.reshape(near, rows // near, width), NEAR, 0, 0)
    part = summed_for(part, lax.axis_size(DEPTH), 1)
    part = lax.all_to_all(part, DEPTH, 0, 0)
    part = summed_for(part, lax.axis_size(PLANE), lax.axis_size(DEPTH[-1]))
    part = lax.all_to_all(part, PLANE, 0, 0)
    return part.reshape(rows, width).astype(F32)


def training(entity, relations, rel_ids, edge_src, edge_dst):
    rows, width = entity.shape
    kinds = relations.shape[0]
    turns, edges = edge_src.shape
    square = 2 * rows * rows * width
    counting = 2 * rows * rows * edges
    ends_rows = 2 * edges // width
    f_rows = jax.ShapeDtypeStruct((rows, width), F32)
    b_rows = jax.ShapeDtypeStruct((rows, width), BF16)
    b_pay = jax.ShapeDtypeStruct((rows + ends_rows, width), BF16)
    b_ends = jax.ShapeDtypeStruct((ends_rows, width), BF16)
    f_count = jax.ShapeDtypeStruct((rows, rows), F32)
    f_rel = jax.ShapeDtypeStruct(relations.shape, F32)
    b_rel = jax.ShapeDtypeStruct((kinds * width, width), BF16)
    first_scratch = [
        pltpu.SMEM(rel_ids.shape, jnp.int32), pltpu.VMEM(entity.shape, F32),
        pltpu.VMEM(relations.shape, F32),
    ] + [pltpu.VMEM(edge_src.shape, jnp.int32)] * 2
    buckets = ((GY, 1), (GX, 1), (GY, -1))

    def exchanged(turn, inner, outer):
        axes = buckets[turn][0]
        partners = (inner_partner, outer_partner)
        if CORE in axes:
            outer_got = swapped(outer, axes, outer_partner)
        else:
            outer_got = swapped_by_core(outer, axes, partners[::-1])
        if CORE in axes:
            inner_got = swapped(inner, axes, inner_partner)
        else:
            inner_got = swapped_by_core(inner, axes, partners)
        return inner_got, outer_got

    sent0 = call(
        prepare_kernel, [b_pay, b_pay], [HBM] * 5, square,
        scratch=first_scratch + [pltpu.SemaphoreType.DMA((5,))],
    )(*in_hbm(rel_ids, entity, relations, edge_src, edge_dst))

    got0 = exchanged(0, *sent0)
    b_wsel = jax.ShapeDtypeStruct((turns * GROUPS, width, width), BF16)
    b_kinds = jax.ShapeDtypeStruct((turns, rows, width), BF16)
    c0, c1, c2, ends1, wsel, of_row = call(
        first_window_kernel, [f_count] * turns + [b_ends, b_wsel, b_kinds], [HBM] * 4,
        turns * counting,
        scratch=first_scratch[:1] + first_scratch[2:] + [pltpu.SemaphoreType.DMA((4,))],
    )(*in_hbm(rel_ids, relations, edge_src, edge_dst))
    x1, h0, *sent1 = call(
        first_round_kernel, [f_rows, b_rows, b_pay, b_pay],
        [VMEM] * 8, 7 * square + counting,
    )(*sent0, *got0, c0, ends1, entity, wsel)

    got1 = exchanged(1, *sent1)
    x2, h1, rows2, mapped2 = call(
        second_round_kernel, [f_rows, b_rows, b_rows, b_rows],
        [VMEM] * 7, 7 * square + counting,
    )(*sent1, *got1, c1, x1, wsel)

    axes, offset = buckets[2]
    xq = shifted(rows2, axes, offset)
    far = shifted(mapped2, axes, -offset)
    acc = call(relation_kernel, [f_rel], [VMEM] * 7, 2 * square)(of_row, *sent0, h0, *sent1, h1)[0]
    h2, payload, _ = call(
        functools.partial(last_kernel, block_order()), [b_rows, b_rel, f_rel],
        [VMEM] * 6, 3 * square, aliases={5: 2},
    )(of_row, rows2, xq, mapped2, c2, acc)
    x3 = call(
        finish_kernel, [f_rows], [VMEM] * 7, 3 * square + counting,
    )(rows2, far, *got0, h2, x2, wsel)[0]

    summed = reduce_everywhere(payload)
    divisor = math.sqrt(turns * lax.axis_size(AXES))
    return x3, (summed / divisor).reshape(relations.shape)


def solution(mesh):
    inner = Mesh(mesh.devices.reshape(2, 4, 2, 2, 8, 2), AXES)
    return jax.shard_map(
        training,
        mesh=inner,
        in_specs=(P(AXES, None), P(), P(None, AXES), P(None, AXES), P(None, AXES)),
        out_specs=(P(AXES, None), P()),
        check_vma=False,
    )
```
